32 devices in a mesh: dp: 8 (over y, x, core), shard: 4 (over z).
Axes of the slice: x: 2, y: 2, z: 4, core: 2. Of those that a mesh axis runs over, the one named last changes fastest.
Arguments:
- token_ids: int32 [64, 128], P(('dp', 'shard')), may hold values from 0 to 49151
- lengths: int32 [64], P(('dp', 'shard')), may hold values from 1 to 128, 6144 in all
- deal_order: int32 [64], replicated, may hold values from 0 to 63, each once
- embed_table: float32 [576, 49152], P('dp', 'shard'), may hold values from -0.4 to 0.4
- table_mom: float32 [576, 49152], P('dp', 'shard'), may hold values from -1 to 1
- table_avg: float32 [576, 49152], P('dp', 'shard'), may hold values from -0.4 to 0.4
- model_flat: float32 [7413120], P(('dp', 'shard')), may hold values from -1 to 2
- model_mom: float32 [7413120], P(('dp', 'shard')), may hold values from -1 to 1
- model_avg: float32 [7413120], P(('dp', 'shard')), may hold values from -1 to 2
Outputs:
- loss_total: float32 [], replicated
- seq_loss: float32 [64], P(('dp', 'shard'))
- slot_loss: float32 [64], P(('dp', 'shard'))
- grad_norm: float32 [], replicated
- table_grad: float32 [576, 49152], P('dp', 'shard')
- table_new: float32 [576, 49152], P('dp', 'shard')
- table_mom_new: float32 [576, 49152], P('dp', 'shard')
- table_avg_new: float32 [576, 49152], P('dp', 'shard')
- table_bf16: bfloat16 [576, 49152], P('dp', 'shard')
- model_grad: float32 [7413120], P(('dp', 'shard'))
- model_new: float32 [7413120], P(('dp', 'shard'))
- model_mom_new: float32 [7413120], P(('dp', 'shard'))
- model_avg_new: float32 [7413120], P(('dp', 'shard'))
- model_bf16: bfloat16 [7413120], P(('dp', 'shard'))
The draws below stay inside these ranges and needn't reach their ends.
Inputs may be any that keep to these rules, and one draw needn't show every extreme that they name: The lengths add up to 6144 and one of them is 128. `deal_order`: every sequence number appears once.
All inputs are finite; a program needn't handle non-finite values. No bound on the sum of `lengths` on one device may be relied on, other than what follows from the above.
Results may differ from the reference program's by a relative error of at most 0.009.
Values may be sent and summed in bfloat16 or wider, within the bound.
No kernel may reach another device: no remote copies, remote signals or barrier semaphores. Data moves between devices by JAX's collectives and lax.ppermute only.
A program may use at most 448 MiB of HBM per device.

```python
import math
import jax
import jax.numpy as jnp
import numpy as np
from jax import lax

MODEL_WIDTH = 576
QUERY_HEADS = 9
KEY_VALUE_HEADS = 3
HEAD_SIZE = 64
FEED_UNITS = 1536
V = 49152
LAYERS = 2
LEN = 128
SEQS = 64
PL = 3540096
NP = 7413120


CLIP_NORM = 0.01


def model_values(key):
    positions = jnp.arange(NP, dtype=jnp.int32)
    offset_in = jnp.where(positions < LAYERS * PL, positions % PL, positions - LAYERS * PL + PL)
    bound_query_key = MODEL_WIDTH * (QUERY_HEADS + 2 * KEY_VALUE_HEADS) * HEAD_SIZE
    bound_out = bound_query_key + QUERY_HEADS * HEAD_SIZE * MODEL_WIDTH
    bound_gate = bound_out + 2 * MODEL_WIDTH * FEED_UNITS
    bound_down = bound_gate + FEED_UNITS * MODEL_WIDTH
    bound_head = PL + MODEL_WIDTH * MODEL_WIDTH
    scales = jnp.where(offset_in < bound_query_key, MODEL_WIDTH ** (-0.5), jnp.where(offset_in < bound_out, 2.5 * (QUERY_HEADS * HEAD_SIZE) ** (-0.5), jnp.where(offset_in < bound_gate, MODEL_WIDTH ** (-0.5), jnp.where(offset_in < bound_down, FEED_UNITS ** (-0.5), jnp.where(offset_in < PL, 0.1, jnp.where(offset_in < bound_head, MODEL_WIDTH ** (-0.5), 0.1))))))
    is_gain = (offset_in >= bound_down) & (offset_in < PL) | (offset_in >= bound_head)
    noise_draw = jax.random.truncated_normal(key, -3.0, 3.0, (NP,), jnp.float32)
    return jnp.where(is_gain, 1.0, 0.0) + noise_draw * scales


def grad_scale():
    return CLIP_NORM / math.sqrt(V * MODEL_WIDTH + NP)


def draw_model_flat(key, part):
    return model_values(jax.random.fold_in(key, 11))


def draw_model_avg(key, part):
    return model_values(jax.random.fold_in(key, 23))


def draw_model_mom(key, part):
    return jax.random.truncated_normal(jax.random.fold_in(key, 37), -4.0, 4.0, (NP,), jnp.float32) * grad_scale()


def draw_table_mom(key, part):
    return jax.random.truncated_normal(jax.random.fold_in(key, 41), -4.0, 4.0, (MODEL_WIDTH, V), jnp.float32) * grad_scale()


def plant(entries, rng, low, high):
    longest = entries.shape.index(max(entries.shape))
    spots = []
    for shift in (0, 1):
        where = [jax.random.randint(jax.random.fold_in(rng, axis), (), 0, length) for axis, length in enumerate(entries.shape)]
        where[longest] = (where[longest] + shift) % entries.shape[longest]
        spots.append(tuple(where))
    return entries.at[spots[0]].set(low).at[spots[1]].set(high)


def level_of(own_key, shape, split, low, top_value):
    loudness, own = 1.0, jax.random.fold_in(own_key, 6)
    for axis_at, blocks in split:
        draws = jnp.exp(jax.random.uniform(jax.random.fold_in(own, axis_at), (blocks,), jnp.float32, low / len(split), top_value / len(split)))
        loudness = loudness * jnp.repeat(draws, shape[axis_at] // blocks).reshape([-1 if axis == axis_at else 1 for axis in range(len(shape))])
    return loudness


def rank_bounds(count, skew):
    weights = [(1 << 20) // math.isqrt(grade ** skew) + 1 for grade in range(1, count + 1)]
    scale = 1 + sum(weights) // (1 << 30)
    return np.cumsum(np.array([max(1, weight // scale) for weight in weights]))


def ranked(key, shape, amount, slope):
    grid = rank_bounds(amount, slope)
    ticket = jax.random.randint(jax.random.fold_in(key, 1), shape, 0, int(grid[amount - 1]))
    standing = jnp.searchsorted(jnp.asarray(grid, jnp.int32), ticket, side="right")
    return jax.random.permutation(jax.random.fold_in(key, 2), amount)[standing].astype(jnp.int32)


def length_profile(number_of, total, bound, skew):
    weights = [(1 << 20) // math.isqrt(standing ** skew) + 1 for standing in range(2, number_of + 1)]
    surplus, holding = total - bound - (number_of - 1), [1] * (number_of - 1)
    while surplus > 0:
        movable = [i for i in range(number_of - 1) if holding[i] < bound]
        mass, remaining = sum([weights[i] for i in movable]), surplus
        for i in movable:
            addition = min(bound - holding[i], max(1, remaining * weights[i] // mass), surplus)
            holding[i] = holding[i] + addition
            surplus = surplus - addition
    return np.array([bound] + holding)


def ragged(key, count, total, bound, slope):
    if count == 2:
        one = jax.random.randint(key, (), max(1, total - bound), min(bound, total - 1) + 1)
        return jnp.stack([one, total - one])
    tallies = jnp.asarray(length_profile(count, total, bound, slope), jnp.int32)
    couples = (count - 1) // 2
    source_of, receiver = tallies[1:1 + 2 * couples:2], tallies[2:2 + 2 * couples:2]
    margin = jnp.minimum(source_of - 1, bound - receiver)
    passed = jax.random.randint(jax.random.fold_in(key, 1), (couples,), 0, 1 << 20) % (margin + 1)
    tallies = tallies.at[1:1 + 2 * couples:2].set(source_of - passed).at[2:2 + 2 * couples:2].set(receiver + passed)
    return tallies[jax.random.permutation(jax.random.fold_in(key, 2), count)]


def centred(own_key, shape, deviation, reach, shards=(), kind=jnp.bfloat16):
    values = deviation * jax.random.normal(own_key, shape, jnp.float32)
    if shards:
        values = values * level_of(own_key, shape, shards, -0.22, 0.18)
    return jnp.clip(values, -reach, reach).astype(kind)


def setup_inputs(seed: int = 0) -> dict:
    seeds = jax.random.split(jax.random.key(seed), 10)
    return {
        "token_ids": plant(ranked(seeds[0], (SEQS, LEN), V, 2), jax.random.fold_in(seeds[0], 3), 0, V - 1).astype(jnp.int32),
        "lengths": ragged(seeds[1], SEQS, 3 * SEQS * LEN // 4, LEN, 2).astype(jnp.int32),
        "deal_order": jax.random.permutation(seeds[2], SEQS).astype(jnp.int32),
        "embed_table": centred(seeds[3], (MODEL_WIDTH, V), 0.08, 0.4, ((0, 8), (1, 4)), jnp.float32),
        "table_mom": draw_table_mom(jax.random.fold_in(seeds[9], 71), 0),
        "table_avg": centred(seeds[5], (MODEL_WIDTH, V), 0.08, 0.4, ((0, 8), (1, 4)), jnp.float32),
        "model_flat": draw_model_flat(jax.random.fold_in(seeds[9], 71), 0),
        "model_mom": draw_model_mom(jax.random.fold_in(seeds[9], 71), 0),
        "model_avg": draw_model_avg(jax.random.fold_in(seeds[9], 71), 0),
    }


EPSILON = 1e-05
ROPE_BASE = 100000.0
CLIP_NORM = 0.01
LEARN_RATE = 6000.0
MOMENTUM = 0.9
AVERAGE_KEEP = 0.9
SECOND_WEIGHT = 0.3
MASKED_SCORE = -1e+30
EXACT_MODE = lax.Precision.HIGHEST

@jax.custom_vjp
def low(v):
    return lax.optimization_barrier(v.astype(jnp.bfloat16)).astype(jnp.float32)

@jax.custom_vjp
def low_back(v):
    return v

def low_keep(v):
    return (low(v), None)

def low_pass(kept, grad):
    return (grad,)

def back_keep(v):
    return (v, None)

def back_low(kept, grad):
    return (low(grad),)
low.defvjp(low_keep, low_pass)
low_back.defvjp(back_keep, back_low)

def forward_and_back(values):
    return low_back(low(values))

def hi_dot(left, right):
    return jnp.dot(left, right, precision=EXACT_MODE, preferred_element_type=jnp.float32)

def rms_norm(values, gain_vec):
    return values * lax.rsqrt(lax.optimization_barrier(jnp.mean(values * values, axis=-1, keepdims=True)) + EPSILON) * gain_vec

def rope_tables(length):
    halves = HEAD_SIZE // 2
    inverse = ROPE_BASE ** (-jnp.arange(halves, dtype=jnp.float32) * 2.0 / HEAD_SIZE)
    angles = jnp.arange(length, dtype=jnp.float32)[:, None] * inverse[None, :]
    return (jnp.cos(angles), jnp.sin(angles))

def rotate(values, cosine, sine_table):
    halves = values.shape[-1] // 2
    first_half = values[..., :halves]
    second_half = values[..., halves:]
    cos_part = cosine[:, None, :]
    sin_part = sine_table[:, None, :]
    return jnp.concatenate([first_half * cos_part - second_half * sin_part, second_half * cos_part + first_half * sin_part], axis=-1)

def unpack_layer(vector):
    head_arrangement = [(MODEL_WIDTH, (QUERY_HEADS + 2 * KEY_VALUE_HEADS) * HEAD_SIZE), (QUERY_HEADS * HEAD_SIZE, MODEL_WIDTH), (MODEL_WIDTH, 2 * FEED_UNITS), (FEED_UNITS, MODEL_WIDTH), (1, MODEL_WIDTH), (1, MODEL_WIDTH)]
    pieces = []
    offset = 0
    for height, breadth in head_arrangement:
        pieces.append(vector[offset:offset + height * breadth].reshape(height, breadth))
        offset += height * breadth
    return (pieces[0], pieces[1], pieces[2], pieces[3], pieces[4][0], pieces[5][0])

def attend(query_rows, key_matrix, value_matrix, length):
    sequence_length = query_rows.shape[0]
    grouped_queries = query_rows.reshape(sequence_length, KEY_VALUE_HEADS, QUERY_HEADS // KEY_VALUE_HEADS, HEAD_SIZE)
    unscaled_scores = jnp.einsum('mnya,lna->nyml', grouped_queries, key_matrix, precision=EXACT_MODE) * HEAD_SIZE ** (-0.5)
    scores = low_back(unscaled_scores)
    places = jnp.arange(sequence_length)
    allowed = (places[None, :] <= places[:, None]) & (places[None, :] < length)
    scores = jnp.where(allowed, scores, MASKED_SCORE)
    attention_weights = low(jax.nn.softmax(scores, axis=-1))
    attended_rows = jnp.einsum('ycvo,oyh->vych', attention_weights, value_matrix, precision=EXACT_MODE)
    return attended_rows.reshape(sequence_length, QUERY_HEADS * HEAD_SIZE)

def layer_apply(hidden, vector, length, cosine, sine_table):
    w_qkv, w_out, w_gateup, w_down, gain_one, gain_two = unpack_layer(vector)
    sequence_length = hidden.shape[0]
    normed = low(rms_norm(hidden, gain_one))
    query_key_value = low_back(hi_dot(normed, w_qkv))
    query_rows = query_key_value[:, :QUERY_HEADS * HEAD_SIZE].reshape(sequence_length, QUERY_HEADS, HEAD_SIZE)
    key_matrix = query_key_value[:, QUERY_HEADS * HEAD_SIZE:(QUERY_HEADS + KEY_VALUE_HEADS) * HEAD_SIZE].reshape(sequence_length, KEY_VALUE_HEADS, HEAD_SIZE)
    value_matrix = forward_and_back(query_key_value[:, (QUERY_HEADS + KEY_VALUE_HEADS) * HEAD_SIZE:].reshape(sequence_length, KEY_VALUE_HEADS, HEAD_SIZE))
    query_rows = forward_and_back(rotate(query_rows, cosine, sine_table))
    key_matrix = forward_and_back(rotate(key_matrix, cosine, sine_table))
    attended_rows = forward_and_back(attend(query_rows, key_matrix, value_matrix, length))
    hidden = hidden + low_back(hi_dot(attended_rows, w_out))
    normed_two = low(rms_norm(hidden, gain_two))
    gate_up = low_back(hi_dot(normed_two, w_gateup))
    activated = forward_and_back(jax.nn.silu(gate_up[:, :FEED_UNITS]) * gate_up[:, FEED_UNITS:])
    return hidden + low_back(hi_dot(activated, w_down))

def group_loss(table_in, model_in, token_rows, length_rows):
    table_low = low(table_in)
    model_low = low(model_in)
    cosine, sine_table = rope_tables(LEN)
    hidden = low_back(table_low.T[token_rows])
    for layer_idx in range(LAYERS):
        vector = model_low[layer_idx * PL:(layer_idx + 1) * PL]
        hidden = jax.vmap(layer_apply, in_axes=(0, None, 0, None, None))(hidden, vector, length_rows, cosine, sine_table)
    head_params = model_low[LAYERS * PL:]
    w_second = head_params[:MODEL_WIDTH * MODEL_WIDTH].reshape(MODEL_WIDTH, MODEL_WIDTH)
    gain_final = head_params[MODEL_WIDTH * MODEL_WIDTH:MODEL_WIDTH * MODEL_WIDTH + MODEL_WIDTH]
    gain_second = head_params[MODEL_WIDTH * MODEL_WIDTH + MODEL_WIDTH:]
    count_seq = token_rows.shape[0]
    flat_rows = hidden.reshape(count_seq * LEN, MODEL_WIDTH)
    head_one = low(rms_norm(flat_rows, gain_final))
    projected = low_back(hi_dot(head_one, w_second))
    head_two = low(rms_norm(projected, gain_second))
    places = jnp.arange(LEN)
    target_one = jnp.roll(token_rows, -1, axis=1).reshape(-1)
    target_two = jnp.roll(token_rows, -2, axis=1).reshape(-1)
    weight_one = (places[None, :] + 1 < length_rows[:, None]).astype(jnp.float32).reshape(-1)
    weight_two = SECOND_WEIGHT * (places[None, :] + 2 < length_rows[:, None]).astype(jnp.float32).reshape(-1)
    total_rows = count_seq * LEN
    block_rows = min(512, total_rows)
    blocks = total_rows // block_rows

    def block_terms(block_items):
        rows_one, rows_two, tgt_one, tgt_two, wgt_one, wgt_two = block_items
        result = jnp.zeros((rows_one.shape[0],), jnp.float32)
        for rows_in, targets, weights in ((rows_one, tgt_one, wgt_one), (rows_two, tgt_two, wgt_two)):
            logits = low_back(jnp.einsum('bd,dv->bv', rows_in, table_low, precision=EXACT_MODE))
            picked = jnp.take_along_axis(logits, targets[:, None], axis=1)[:, 0]
            result = result + weights * (jax.nn.logsumexp(logits, axis=1) - picked)
        return result
    shaped = tuple((member.reshape((blocks, block_rows) + member.shape[1:]) for member in (head_one, head_two, target_one, target_two, weight_one, weight_two)))
    row_terms = lax.map(jax.checkpoint(block_terms), shaped).reshape(count_seq, LEN)
    seq_terms = lax.optimization_barrier(jnp.sum(row_terms, axis=1))
    return (jnp.sum(seq_terms), seq_terms)

def reference(token_ids, lengths, deal_order, embed_table, table_mom, table_avg, model_flat, model_mom, model_avg):
    target_count = jnp.sum(lengths - 1).astype(jnp.float32)
    group_size = min(SEQS, max(1, 4096 // LEN))
    ids_grouped = token_ids.reshape(SEQS // group_size, group_size, LEN)
    len_grouped = lengths.reshape(SEQS // group_size, group_size)

    def accumulate(carried, item_pair):
        grad_table, grad_model = carried
        token_rows, length_rows = item_pair
        total_value, pull_back, seq_terms = jax.vjp(lambda table_in, model_in: group_loss(table_in, model_in, token_rows, length_rows), embed_table, model_flat, has_aux=True)
        part_table, part_model = pull_back(jnp.ones_like(total_value) / target_count)
        return ((grad_table + part_table, grad_model + part_model), seq_terms)
    (grad_table, grad_model), seq_terms = lax.scan(accumulate, (jnp.zeros_like(embed_table), jnp.zeros_like(model_flat)), (ids_grouped, len_grouped))
    seq_loss = seq_terms.reshape(SEQS) / target_count
    loss_total = jnp.sum(seq_loss)
    slot_loss = seq_loss[deal_order]
    grad_norm = jnp.sqrt(jnp.sum(grad_table * grad_table) + jnp.sum(grad_model * grad_model))
    factor = jnp.minimum(1.0, CLIP_NORM / (grad_norm + 1e-06))
    results = []
    for weights, gradient, moment, average in ((embed_table, grad_table, table_mom, table_avg), (model_flat, grad_model, model_mom, model_avg)):
        clipped = gradient * factor
        new_moment = MOMENTUM * moment + clipped
        new_weight = weights - LEARN_RATE * (clipped + MOMENTUM * new_moment)
        new_average = AVERAGE_KEEP * average + (1.0 - AVERAGE_KEEP) * new_weight
        results.append((clipped, new_weight, new_moment, new_average, new_weight.astype(jnp.bfloat16)))
    return (loss_total, seq_loss, slot_loss, grad_norm, results[0][0], results[0][1], results[0][2], results[0][3], results[0][4], results[1][0], results[1][1], results[1][2], results[1][3], results[1][4])
```

```python
import jax
import jax.numpy as jnp
from jax import lax
from jax.experimental import pallas as pl
from jax.experimental.pallas import tpu as pltpu
from jax.sharding import PartitionSpec as P

MODEL_WIDTH = 576
QUERY_HEADS = 9
KEY_VALUE_HEADS = 3
HEAD_SIZE = 64
FEED_UNITS = 1536
LAYERS = 2
LEN = 128
PL = 3540096
NP = 7413120
QKV = (QUERY_HEADS + 2 * KEY_VALUE_HEADS) * HEAD_SIZE
ROPED = (QUERY_HEADS + KEY_VALUE_HEADS) * HEAD_SIZE
MEAN_LENGTH = 96

EPSILON = 1e-05
ROPE_BASE = 100000.0
CLIP_NORM = 0.01
LEARN_RATE = 6000.0
MOMENTUM = 0.9
AVERAGE_KEEP = 0.9
SECOND_WEIGHT = 0.3
MASKED_SCORE = -1e30

GRAIN = 2048
GRANULE = 16
BLOCK = 512
CHUNK = 1024
LANES = 128
COLUMNS = 256
VMEM_LIMIT = 62 * 1024 * 1024
F32 = jnp.float32
BF16 = jnp.bfloat16


def flip_dp(values, bit):
    return lax.ppermute(values, "dp", [(i, i ^ bit) for i in range(lax.axis_size("dp"))])


def flip_shard(values, bit):
    return lax.ppermute(values, "shard", [(i, i ^ bit) for i in range(lax.axis_size("shard"))])


def next_shard(values):
    size = lax.axis_size("shard")
    return lax.ppermute(values, "shard", [(i, (i + 1) % size) for i in range(size)])


def bits_below(size):
    return [1 << k for k in range(size.bit_length() - 1)]


def dp_bit(bit):
    return (lax.axis_index("dp") // bit) % 2


def join(own, other, bit, axis):
    return jnp.where(
        dp_bit(bit) == 0,
        jnp.concatenate([own, other], axis),
        jnp.concatenate([other, own], axis),
    )


def pick(values, idx, axis):
    return lax.dynamic_index_in_dim(values, idx, axis, keepdims=False)


def high_bits():
    return bits_below(lax.axis_size("dp"))[1:]


def gather_cube(values, order):
    bits = sorted(order, reverse=True)
    out = values.reshape((1,) * len(bits) + values.shape)
    for bit in order:
        out = join(out, flip_dp(out, bit), bit, bits.index(bit))
    return out.reshape((-1,) + values.shape)


def reduce_cube(values, order):
    bits = sorted(order, reverse=True)
    left = list(bits)
    out = values.reshape((2,) * len(bits) + values.shape[1:])
    for bit in order:
        axis = left.index(bit)
        mine = dp_bit(bit)
        got = flip_dp(pick(out, 1 - mine, axis).astype(BF16), bit)
        out = pick(out, mine, axis).astype(F32) + got.astype(F32)
        left.remove(bit)
    return out


def ring_gather(values):
    size = lax.axis_size("shard")
    me = lax.axis_index("shard")
    parts = [values]
    for _ in range(size - 1):
        parts.append(next_shard(parts[-1]))
    stacked = jnp.stack(parts[::-1])
    return jnp.roll(stacked, me + 1, axis=0)


def ring_reduce(values):
    size = lax.axis_size("shard")
    me = lax.axis_index("shard")
    total = None
    for step in range(size - 1):
        term = pick(values, (me - 1 - step) % size, 0).astype(F32)
        if total is not None:
            term = term + total
        total = next_shard(term.astype(BF16)).astype(F32)
    return total + pick(values, me, 0).astype(F32)


def group_gather(rows):
    parts = ring_gather(rows)
    other = flip_dp(parts, 1)
    return join(parts[None], other[None], 1, 0)


def group_reduce(parts):
    mine = dp_bit(1)
    got = flip_dp(pick(parts, 1 - mine, 0).astype(BF16), 1)
    return ring_reduce(pick(parts, mine, 0).astype(F32) + got.astype(F32))


def sum_all(value):
    total = value
    for bit in bits_below(lax.axis_size("dp")):
        total = total + flip_dp(total, bit)
    for bit in bits_below(lax.axis_size("shard")):
        total = total + flip_shard(total, bit)
    return total


def top_bit():
    return high_bits()[-1]


def block_starts(length, total):
    return [length * i // GRAIN for i in range(total)] + [-(-length * total // GRAIN)]


def own_blocks(model_flat):
    length = model_flat.shape[0]
    total = lax.axis_size("dp") * lax.axis_size("shard")
    device = lax.axis_index(("dp", "shard"))
    low = model_flat.astype(BF16)
    before = lax.ppermute(
        low[length - GRAIN :], ("dp", "shard"), [(i, i + 1) for i in range(total - 1)]
    )
    starts = block_starts(length, total)
    blocks = max(starts[i + 1] - starts[i] for i in range(total))
    extended = jnp.concatenate([before, low, jnp.zeros((3 * GRAIN,), BF16)])
    shift = (length * device) % GRAIN
    whole = lax.dynamic_slice_in_dim(extended, GRAIN - shift, blocks * GRAIN, 0)
    return whole.reshape(-1, 128)


LAYER_SHAPES = (
    (MODEL_WIDTH, QKV),
    (MODEL_WIDTH, MODEL_WIDTH),
    (MODEL_WIDTH, 2 * FEED_UNITS),
    (FEED_UNITS, MODEL_WIDTH),
)
SQUARE = ((MODEL_WIDTH, MODEL_WIDTH),)
TALL = 64


def line_up(flat_at, out, height, breadth):
    tiles, odd = breadth // 128, breadth % 128
    if not odd:
        for j in range(tiles):
            out(0, j, flat_at(j, height, tiles))
        return
    period = 2 * tiles + 1
    loads = [flat_at(j, height // 2, period) for j in range(period)]
    for j in range(tiles + 1):
        out(0, j, loads[j])
        after = loads[min(tiles + j + 1, period - 1)]
        out(1, j, jnp.concatenate([loads[tiles + j][:, 64:], after[:, :64]], 1))


def unpack_matrix(flat_ref, at, out_ref, wide_ref, tall_ref):
    height, breadth = out_ref.shape
    rows = TALL * breadth // 128
    shift = at % 16
    load = rows + (16 if shift else 0)

    @pl.loop(0, height // TALL)
    def _(k):
        first = pl.multiple_of(k * rows + (at - shift), 16)
        wide_ref[:load, :] = flat_ref[pl.ds(first, load), :].astype(F32)
        out_at = pl.multiple_of(k * TALL, TALL)

        def flat_at(j, count, stride):
            return wide_ref[pl.ds(shift + j, count, stride=stride), :]

        if breadth % 128:
            def put(parity, j, values):
                tall_ref[j, pl.ds(parity, TALL // 2, stride=2), :] = values

            line_up(flat_at, put, TALL, breadth)
            for j in range(breadth // 128 + 1):
                stop = min((j + 1) * 128, breadth)
                out_ref[pl.ds(out_at, TALL), j * 128 : stop] = tall_ref[
                    j, :, : stop - j * 128
                ].astype(BF16)
        else:
            def put(_, j, values):
                out_ref[pl.ds(out_at, TALL), j * 128 : (j + 1) * 128] = values.astype(BF16)

            line_up(flat_at, put, TALL, breadth)


def unpack_rows(everything, length, first_row, last_row, shapes, gaps, lead, tails):
    total = lax.axis_size("dp") * lax.axis_size("shard")
    starts = block_starts(length, total)
    per = GRAIN // 128
    moves = []
    for owner in range(total):
        low = max(starts[owner] * per, first_row)
        high = min(starts[owner + 1] * per, last_row)
        if low < high:
            moves.append((owner, low - starts[owner] * per, low - first_row, high - low))
    outs = [jax.ShapeDtypeStruct(shape, BF16) for shape in shapes]
    outs += [jax.ShapeDtypeStruct((rows, 128), BF16) for _, rows in tails]
    wide_rows = TALL * max(shape[1] for shape in shapes) // 128 + 16
    height = last_row - first_row

    def kernel(all_ref, *refs):
        outs, (flat_ref, wide_ref, tall_ref, sems) = refs[:-4], refs[-4:]
        copies = [
            pltpu.make_async_copy(
                all_ref.at[owner, pl.ds(source, rows)], flat_ref.at[pl.ds(at, rows)], sems.at[k]
            )
            for k, (owner, source, at, rows) in enumerate(moves)
        ]
        for copy in copies:
            copy.start()
        arrived = 0
        at = lead
        for k, (tall, wide) in enumerate(shapes):
            end = at + tall * wide // 128
            while arrived < len(moves) and moves[arrived][2] < end:
                copies[arrived].wait()
                arrived += 1
            unpack_matrix(flat_ref, at, outs[k], wide_ref, tall_ref)
            at = end + gaps.get(k, 0)
        for copy in copies[arrived:]:
            copy.wait()
        for k, (start, rows) in enumerate(tails):
            outs[len(shapes) + k][...] = flat_ref[pl.ds(start, rows), :]

    return pl.pallas_call(
        kernel,
        in_specs=[pl.BlockSpec(memory_space=pl.ANY)],
        out_specs=[pl.BlockSpec(memory_space=pltpu.VMEM)] * len(outs),
        out_shape=outs,
        scratch_shapes=[
            pltpu.VMEM((height, 128), BF16),
            pltpu.VMEM((wide_rows, 128), F32),
            pltpu.VMEM((8, TALL, 128), F32),
            pltpu.SemaphoreType.DMA((len(moves),)),
        ],
        compiler_params=pltpu.CompilerParams(vmem_limit_bytes=VMEM_LIMIT),
        cost_estimate=pl.CostEstimate(flops=0, bytes_accessed=512 * height, transcendentals=0),
        name="unpack_rows",
    )(everything)


def pack_matrix(left_ref, right_ref, flat_ref, at, tall_ref):
    height, breadth = left_ref.shape[1], right_ref.shape[1]
    part = 512 if height % 512 == 0 else height
    tiles, odd = breadth // 128, breadth % 128
    for k in range(height // part):
        first = at + k * part * breadth // 128
        product = against(left_ref[:, k * part : (k + 1) * part], right_ref[...])
        for j in range(tiles + (1 if odd else 0)):
            stop = min((j + 1) * 128, breadth)
            tall_ref[j, :part, : stop - j * 128] = product[:, j * 128 : stop]
        if not odd:
            for j in range(tiles):
                flat_ref[pl.ds(first + j, part, stride=tiles), :] = tall_ref[j, :part, :]
            continue
        period = 2 * tiles + 1
        count = part // 2

        def half(parity, j):
            return tall_ref[j, pl.ds(parity, count, stride=2), :]

        for j in range(tiles):
            flat_ref[pl.ds(first + j, count, stride=period), :] = half(0, j)
        flat_ref[pl.ds(first + tiles, count, stride=period), :] = jnp.concatenate(
            [half(0, tiles)[:, :64], half(1, 0)[:, :64]], 1
        )
        for j in range(tiles):
            flat_ref[pl.ds(first + tiles + 1 + j, count, stride=period), :] = jnp.concatenate(
                [half(1, j)[:, 64:], half(1, j + 1)[:, :64]], 1
            )


def pack_kernel(info_ref, *refs, pairs, loose, early, lead, gaps, count, sub_rows, keep, first_loose):
    lefts, rights, refs = refs[:pairs], refs[pairs : 2 * pairs], refs[2 * pairs :]
    loose_refs, refs = refs[:loose], refs[loose:]
    if early:
        early_ref, refs = refs[0], refs[1:]
    own_ref, send_ref, refs = refs[0], refs[1], refs[2:]
    if keep:
        keep_ref, refs = refs[0], refs[1:]
    flat_ref, low_ref, tall_ref, sems = refs
    height = flat_ref.shape[0]
    at = lead
    for k in range(pairs):
        pack_matrix(lefts[k], rights[k], flat_ref, at, tall_ref)
        at += lefts[k].shape[1] * rights[k].shape[1] // 128
        if k in gaps:
            flat_ref[at : at + gaps[k], :] = loose_refs[list(gaps).index(k)][...]
            at += gaps[k]
    if early:
        flat_ref[at : at + early, :] = early_ref[...].astype(F32)[first_loose : first_loose + early]
        at += early
    if at < height:
        flat_ref[at:height, :] = jnp.zeros((height - at, 128), F32)
    step = 16 * 32
    for row in range(0, height, step):
        rows = min(step, height - row)
        low_ref[row : row + rows, :] = flat_ref[row : row + rows, :].astype(BF16)
    copies = []
    for idx in range(count):
        for k, ref in enumerate((own_ref, send_ref)):
            row = pl.multiple_of(info_ref[k * count + idx], 16)
            copies.append(
                pltpu.make_async_copy(
                    low_ref.at[pl.ds(row, sub_rows)], ref.at[idx], sems.at[k * count + idx]
                )
            )
    for copy in copies:
        copy.start()
    if keep:
        keep_ref[...] = low_ref[:keep, :]
    for copy in copies:
        copy.wait()


def pack_half(info, pairs, loose, early, lead, gaps, height, sub_rows, keep, skip):
    count = info.shape[0] // 2
    lefts = [left for left, _ in pairs]
    rights = [right for _, right in pairs]
    in_place = pl.BlockSpec(memory_space=pltpu.VMEM)
    anywhere = pl.BlockSpec(memory_space=pl.ANY)
    operands = lefts + rights + loose + ([early[0]] if early is not None else [])
    outs = [jax.ShapeDtypeStruct((count, sub_rows, 128), BF16)] * 2
    specs = [anywhere] * 2
    if keep:
        outs.append(jax.ShapeDtypeStruct((keep, 128), BF16))
        specs.append(in_place)

    def kernel(info_ref, *refs):
        pack_kernel(
            info_ref, *refs, pairs=len(pairs), loose=len(loose),
            early=0 if early is None else early[1], lead=lead, gaps=gaps,
            count=count, sub_rows=sub_rows, keep=keep, first_loose=skip,
        )

    flops = sum(2 * left.size * right.shape[1] for left, right in pairs)
    return pl.pallas_call(
        kernel,
        in_specs=[pl.BlockSpec(memory_space=pltpu.SMEM)] + [in_place] * len(operands),
        out_specs=specs,
        out_shape=outs,
        scratch_shapes=[
            pltpu.VMEM((height, 128), F32),
            pltpu.VMEM((height, 128), BF16),
            pltpu.VMEM((max(right.shape[1] for right in rights) // 128, MODEL_WIDTH, 128), F32),
            pltpu.SemaphoreType.DMA((2 * count,)),
        ],
        compiler_params=pltpu.CompilerParams(vmem_limit_bytes=VMEM_LIMIT),
        cost_estimate=pl.CostEstimate(
            flops=flops, bytes_accessed=512 * height, transcendentals=0
        ),
        name="pack_half",
    )(info, *operands)


def owner_rows(length, which, first_row):
    dp_size, shard_size = lax.axis_size("dp"), lax.axis_size("shard")
    sub_rows = owner_sub_rows(length)
    per = GRAIN // 128
    j = jnp.arange(2)[:, None, None]
    x = jnp.arange(dp_size // 4)[None, :, None]
    z = jnp.arange(shard_size)[None, None, :]
    rows = []
    for core in (dp_bit(1), 1 - dp_bit(1)):
        owner = ((which * (dp_size // 4) + x) * 2 + core) * shard_size + z
        rows.append((length * owner // GRAIN * per + sub_rows * j - first_row).reshape(-1))
    return jnp.concatenate(rows).astype(jnp.int32)


def owner_sub_rows(length):
    blocks = -(-(GRAIN - 1 + length) // GRAIN)
    return (blocks + blocks % 2) * (GRAIN // 128) // 2


def reduce_half(own, send, which):
    dp_size, shard_size = lax.axis_size("dp"), lax.axis_size("shard")
    paired = (own.astype(F32) + flip_dp(send, 1).astype(F32)).astype(BF16)
    paired = paired.reshape((-1, shard_size) + own.shape[1:])
    half = shard_size // 2
    order = high_bits()
    first = reduce_cube(paired[:, :half], order)
    second = reduce_cube(paired[:, half:], order[::-1])
    done = ring_reduce(jnp.concatenate([first, second], 0).astype(BF16))
    top = top_bit()
    away = [(i, i ^ top) for i in range(dp_size) if (i // top) % 2 != which]
    got = lax.ppermute(done.astype(BF16), "dp", away).astype(F32)
    return done, got


def own_part(halves, length):
    (done_zero, got_zero), (done_one, got_one) = halves
    top = dp_bit(top_bit())
    lower = jnp.where(top == 0, done_zero, got_one)
    upper = jnp.where(top == 0, got_zero, done_one)
    shift = (length * lax.axis_index(("dp", "shard"))) % GRAIN
    flat = jnp.concatenate([lower, upper], 0).reshape(-1)
    return lax.dynamic_slice_in_dim(flat, shift, length, 0)


def gather_table(embed_table):
    low = embed_table.astype(BF16)
    half = low.shape[1] // 2
    core = dp_bit(1)
    own = lax.dynamic_slice_in_dim(low, core * half, half, 1)
    send = lax.dynamic_slice_in_dim(low, (1 - core) * half, half, 1)
    pair = join(own, flip_dp(send, 1), 1, 0)
    bits = sorted(high_bits(), reverse=True)
    shape = (1,) * len(bits) + (pair.shape[0], half // 2)
    sides = [pair[:, : half // 2].reshape(shape), pair[:, half // 2 :].reshape(shape)]
    orders = [high_bits(), high_bits()[::-1]]
    for k in range(len(bits)):
        got = [flip_dp(side, order[k]) for side, order in zip(sides, orders)]
        sides = [
            join(side, other, order[k], bits.index(order[k]))
            for side, other, order in zip(sides, got, orders)
        ]
    return jnp.concatenate([side.reshape(MODEL_WIDTH, -1) for side in sides], 1)


def reduce_table(table_grad, features):
    half = table_grad.shape[1]
    parts = table_grad.reshape(-1, 2 * features, half)
    order = high_bits()
    first = reduce_cube(parts[:, :, : half // 2], order)
    second = reduce_cube(parts[:, :, half // 2 :], order[::-1])
    return jnp.concatenate([first, second], 1)


def to_owner(joined, features):
    core = dp_bit(1)
    own = lax.dynamic_slice_in_dim(joined, core * features, features, 0)
    send = lax.dynamic_slice_in_dim(joined, (1 - core) * features, features, 0)
    return join(own, flip_dp(send, 1), 1, 1)


def rms_scale(values):
    return lax.rsqrt(jnp.mean(values * values, axis=-1, keepdims=True) + EPSILON)


def rms_back(values, scale, gain, grad):
    weighted = grad * gain
    inner = jnp.sum(weighted * values, axis=-1, keepdims=True)
    grad_values = scale * weighted - values * (scale * scale * scale * inner / MODEL_WIDTH)
    grad_gain = jnp.sum(grad * values * scale, axis=0)
    return grad_values, grad_gain


def rope_rows(rows):
    halves = HEAD_SIZE // 2
    inverse = ROPE_BASE ** (-jnp.arange(halves, dtype=F32) * 2.0 / HEAD_SIZE)
    angles = jnp.arange(LEN, dtype=F32)[:, None] * inverse[None, :]
    cosine, sine = jnp.cos(angles), jnp.sin(angles)
    heads = ROPED // HEAD_SIZE
    cos_full = jnp.tile(jnp.concatenate([cosine, cosine], 1), (rows // LEN, heads))
    sin_full = jnp.tile(jnp.concatenate([-sine, sine], 1), (rows // LEN, heads))
    return cos_full, sin_full


def swap_halves(values):
    halves = HEAD_SIZE // 2
    lanes = lax.broadcasted_iota(jnp.int32, values.shape, 1) % HEAD_SIZE
    return jnp.where(lanes < halves, jnp.roll(values, -halves, 1), jnp.roll(values, halves, 1))


def split_heads(rows, heads):
    return rows.reshape(-1, LEN, heads, HEAD_SIZE)


def layer_forward(hidden, pieces, allowed, rope):
    w_qkv, w_out, w_gateup, w_down, gains = pieces
    cos_full, sin_full = rope
    gains = gains.astype(F32)
    group = QUERY_HEADS // KEY_VALUE_HEADS
    scale_one = rms_scale(hidden)
    normed = (hidden * scale_one * gains[0]).astype(BF16)
    qkv = jnp.dot(normed, w_qkv, preferred_element_type=F32)
    straight = qkv[:, :ROPED]
    turned = (straight * cos_full + swap_halves(straight) * sin_full).astype(BF16)
    query = turned[:, : QUERY_HEADS * HEAD_SIZE].reshape(
        -1, LEN, KEY_VALUE_HEADS, group, HEAD_SIZE
    )
    key = split_heads(turned[:, QUERY_HEADS * HEAD_SIZE :], KEY_VALUE_HEADS)
    value = split_heads(qkv[:, ROPED:].astype(BF16), KEY_VALUE_HEADS)
    scores = jnp.einsum("stgja,suga->sgjtu", query, key, preferred_element_type=F32)
    scores = jnp.where(allowed, scores * HEAD_SIZE ** (-0.5), MASKED_SCORE)
    probs = jax.nn.softmax(scores, axis=-1)
    attended = jnp.einsum(
        "sgjtu,suga->stgja", probs.astype(BF16), value, preferred_element_type=F32
    )
    attended = attended.reshape(-1, QUERY_HEADS * HEAD_SIZE).astype(BF16)
    middle = hidden + jnp.dot(attended, w_out, preferred_element_type=F32)
    scale_two = rms_scale(middle)
    normed_two = (middle * scale_two * gains[1]).astype(BF16)
    gate_up = jnp.dot(normed_two, w_gateup, preferred_element_type=F32)
    acted = (jax.nn.silu(gate_up[:, :FEED_UNITS]) * gate_up[:, FEED_UNITS:]).astype(BF16)
    output = middle + jnp.dot(acted, w_down, preferred_element_type=F32)
    kept = (
        hidden, scale_one, normed, query, key, value, probs, attended,
        middle, scale_two, normed_two, gate_up, acted,
    )
    return output, kept


def against(left, right):
    return lax.dot_general(left, right, (((0,), (0,)), ((), ())), preferred_element_type=F32)


def times_t(left, right):
    return lax.dot_general(left, right, (((1,), (1,)), ((), ())), preferred_element_type=F32)


def layer_backward(kept, pieces, rope, grad_output):
    w_qkv, w_out, w_gateup, w_down, gains = pieces
    cos_full, sin_full = rope
    gains = gains.astype(F32)
    (
        hidden, scale_one, normed, query, key, value, probs, attended,
        middle, scale_two, normed_two, gate_up, acted,
    ) = kept
    scaling = HEAD_SIZE ** (-0.5)
    rows = hidden.shape[0]
    grad_low = grad_output.astype(BF16)
    grad_act = times_t(grad_low, w_down).astype(BF16).astype(F32)
    gate, up = gate_up[:, :FEED_UNITS], gate_up[:, FEED_UNITS:]
    sigma = jax.nn.sigmoid(gate)
    grad_up = grad_act * (gate * sigma)
    grad_gate = grad_act * up * (sigma * (1.0 + gate * (1.0 - sigma)))
    grad_gu = jnp.concatenate([grad_gate, grad_up], 1).astype(BF16)
    grad_normed_two = times_t(grad_gu, w_gateup)
    grad_mid, grad_gain_two = rms_back(middle, scale_two, gains[1], grad_normed_two)
    grad_mid = grad_mid + grad_output
    grad_mid_low = grad_mid.astype(BF16)
    grad_att = times_t(grad_mid_low, w_out).astype(BF16).reshape(query.shape)
    grad_probs = jnp.einsum("stgja,suga->sgjtu", grad_att, value, preferred_element_type=F32)
    grad_value = jnp.einsum(
        "sgjtu,stgja->suga", probs.astype(BF16), grad_att, preferred_element_type=F32
    )
    grad_scores = (
        probs * (grad_probs - jnp.sum(grad_probs * probs, axis=-1, keepdims=True))
    ).astype(BF16)
    grad_query = (
        jnp.einsum("sgjtu,suga->stgja", grad_scores, key, preferred_element_type=F32) * scaling
    )
    grad_key = (
        jnp.einsum("sgjtu,stgja->suga", grad_scores, query, preferred_element_type=F32) * scaling
    )
    turned = jnp.concatenate(
        [grad_query.reshape(rows, -1).astype(BF16), grad_key.reshape(rows, -1).astype(BF16)], 1
    ).astype(F32)
    straight = (turned * cos_full - swap_halves(turned) * sin_full).astype(BF16)
    grad_qkv = jnp.concatenate([straight, grad_value.reshape(rows, -1).astype(BF16)], 1)
    grad_normed = times_t(grad_qkv, w_qkv)
    grad_input, grad_gain_one = rms_back(hidden, scale_one, gains[0], grad_normed)
    grad_input = grad_input + grad_mid
    pairs = [
        (normed, grad_qkv), (attended, grad_mid_low), (normed_two, grad_gu), (acted, grad_low),
    ]
    return grad_input, pairs, flat_rows(grad_gain_one, grad_gain_two)


def flat_rows(first, second):
    return jnp.concatenate([first, second]).reshape(-1, 128)


def token_bits(tokens):
    return tokens.bit_length() - 1


def for_chunks(keys_ref, lines_ref, span_ref, columns, run):
    bits = token_bits(keys_ref.shape[0])
    base = span_ref[2]
    places = lax.broadcasted_iota(jnp.int32, (LANES, LANES), 1)

    def chunk_step(chunk, _):
        line = lines_ref[pl.ds(chunk, 1), :]
        ids = jnp.transpose(jnp.broadcast_to(lax.shift_right_logical(line, bits), (LANES, LANES)))
        low = lax.shift_right_logical(keys_ref[chunk * LANES], bits) - base
        high = lax.shift_right_logical(keys_ref[chunk * LANES + LANES - 1], bits) - base
        first = jnp.maximum(low, 0) // COLUMNS
        last = jnp.minimum(high, columns - 1) // COLUMNS

        def hot(block):
            parts = []
            for k in range(COLUMNS // LANES):
                match = ids - (base + block * COLUMNS + k * LANES) == places
                parts.append(jnp.where(match, 1.0, 0.0).astype(BF16))
            return jnp.concatenate(parts, 1)

        run(chunk, first, last + 1, hot)
        return 0

    lax.fori_loop(span_ref[0] // LANES, (span_ref[1] + LANES - 1) // LANES, chunk_step, 0)


def row_of(keys_ref, at):
    return keys_ref[at] & (keys_ref.shape[0] - 1)


def embed_kernel(keys_ref, span_ref, lines_ref, table_ref, out_ref, low_ref, rows_ref, found_ref):
    features, columns = table_ref.shape
    blocks, _, width = out_ref.shape
    low_ref[:features, :] = table_ref[...].astype(BF16)
    low_ref[features:, :] = jnp.zeros((LANES - features, columns), BF16)
    for k in range(blocks):
        rows_ref[k * width : (k + 1) * width, :] = jnp.zeros((width, LANES), F32)

    def run(chunk, first, last, hot):
        def block_step(block, total):
            at = pl.multiple_of(block * COLUMNS, COLUMNS)
            return total + times_t(hot(block), low_ref[:, pl.ds(at, COLUMNS)])

        found_ref[...] = lax.fori_loop(first, last, block_step, jnp.zeros((LANES, LANES), F32))

        def move(k, _):
            for j in range(8):
                row = row_of(keys_ref, chunk * LANES + k * 8 + j)
                rows_ref[pl.ds(row, 1), :] = found_ref[pl.ds(k * 8 + j, 1), :]
            return 0

        lax.fori_loop(0, LANES // 8, move, 0)

    for_chunks(keys_ref, lines_ref, span_ref, columns, run)

    def finish(k, _):
        at = pl.multiple_of(k * width, width)
        out_ref[k] = jnp.transpose(rows_ref[pl.ds(at, width), :])[:features].astype(BF16)
        return 0

    lax.fori_loop(0, blocks, finish, 0)


def embed_rows(keys, span, table, blocks):
    tokens = keys.shape[0]
    features, columns = table.shape
    scalars = pl.BlockSpec(memory_space=pltpu.SMEM)
    in_place = pl.BlockSpec(memory_space=pltpu.VMEM)
    return pl.pallas_call(
        embed_kernel,
        in_specs=[scalars, scalars, in_place, in_place],
        out_specs=in_place,
        out_shape=jax.ShapeDtypeStruct((blocks, features, tokens // blocks), BF16),
        scratch_shapes=[
            pltpu.VMEM((LANES, columns), BF16),
            pltpu.VMEM((tokens, LANES), F32),
            pltpu.VMEM((LANES, LANES), F32),
        ],
        compiler_params=pltpu.CompilerParams(vmem_limit_bytes=VMEM_LIMIT),
        cost_estimate=pl.CostEstimate(
            flops=2 * tokens * LANES * COLUMNS, bytes_accessed=4 * table.size, transcendentals=0
        ),
        name="embed_rows",
    )(keys, span, keys.reshape(-1, LANES), table)


def spread_kernel(keys_ref, span_ref, place_ref, lines_ref, *refs):
    parts, (base_ref, out_ref, rows_ref, packed_ref) = refs[:-4], refs[-4:]
    features, columns = base_ref.shape
    count, _, width = parts[0].shape
    for k, part in enumerate(parts):
        def unfold(j, _):
            at = pl.multiple_of(place_ref[k * count + j] * width, width)
            flat = part[j].astype(F32)
            flat = jnp.concatenate([flat, jnp.zeros((LANES - features, width), F32)], 0)
            rows_ref[pl.ds(at, width), :] = jnp.transpose(flat)
            return 0

        lax.fori_loop(0, count, unfold, 0)
    out_ref[...] = base_ref[...]

    def run(chunk, first, last, hot):
        def move(k, _):
            for j in range(8):
                row = row_of(keys_ref, chunk * LANES + k * 8 + j)
                packed_ref[pl.ds(k * 8 + j, 1), :] = rows_ref[pl.ds(row, 1), :]
            return 0

        lax.fori_loop(0, LANES // 8, move, 0)
        packed = packed_ref[...].astype(BF16)

        def block_step(block, _):
            at = pl.multiple_of(block * COLUMNS, COLUMNS)
            out_ref[:, pl.ds(at, COLUMNS)] += against(packed, hot(block))[:features]
            return 0

        lax.fori_loop(first, last, block_step, 0)

    for_chunks(keys_ref, lines_ref, span_ref, columns, run)


def spread_rows(keys, span, places, parts, base):
    tokens = keys.shape[0]
    scalars = pl.BlockSpec(memory_space=pltpu.SMEM)
    in_place = pl.BlockSpec(memory_space=pltpu.VMEM)
    return pl.pallas_call(
        spread_kernel,
        in_specs=[scalars] * 3 + [in_place] * (2 + len(parts)),
        out_specs=in_place,
        out_shape=jax.ShapeDtypeStruct(base.shape, F32),
        scratch_shapes=[
            pltpu.VMEM((tokens, LANES), F32),
            pltpu.VMEM((LANES, LANES), F32),
        ],
        compiler_params=pltpu.CompilerParams(vmem_limit_bytes=VMEM_LIMIT),
        cost_estimate=pl.CostEstimate(
            flops=2 * tokens * LANES * COLUMNS, bytes_accessed=8 * base.size, transcendentals=0
        ),
        name="spread_rows",
    )(keys, span, places, keys.reshape(-1, LANES), *parts, base)


def block_count(count_ref):
    per = BLOCK // GRANULE
    return (count_ref[0] + per - 1) // per


def block_at(i, count_ref, list_ref):
    return (jnp.minimum(i, jnp.maximum(block_count(count_ref) - 1, 0)), 0)


def head_kernel(
    count_ref, list_ref, rows_ref, table_ref,
    exp_ref, back_ref, sum_ref, peak_ref,
    packed, even, odd,
):
    columns = table_ref.shape[1]
    chunk = even.shape[1]
    chunks = columns // chunk
    logits = (even, odd)
    per = BLOCK // GRANULE
    block = pl.program_id(0)

    @pl.when(block == 0)
    def _():
        back_ref[...] = jnp.zeros(back_ref.shape, F32)
        sum_ref[...] = jnp.ones(sum_ref.shape, F32)
        peak_ref[...] = jnp.zeros(peak_ref.shape, F32)

    def spot(g):
        return pl.multiple_of(list_ref[block * per + g] * GRANULE, GRANULE)

    def dot_chunk(k):
        return jnp.dot(
            packed[...], table_ref[:, k * chunk : (k + 1) * chunk], preferred_element_type=F32
        )

    def put(stat_ref, line):
        for g in range(per):
            lane = g * GRANULE // 128 * 128
            part = line[:, lane : lane + 128]
            if g * GRANULE % 128:
                part = pltpu.roll(part, 128 - g * GRANULE % 128, 1)
            stat_ref[pl.ds(list_ref[block * per + g], 1), :] = part

    def run(peak):
        total = jnp.zeros((BLOCK, 128), F32)
        logits[0][...] = dot_chunk(0)
        for k in range(chunks):
            if k + 1 < chunks:
                logits[(k + 1) % 2][...] = dot_chunk(k + 1)
            here = logits[k % 2][...]
            powers = jnp.exp(here if peak is None else here - peak)
            for j in range(chunk // 128):
                total = total + powers[:, j * 128 : (j + 1) * 128]
            exp_ref[:, k * chunk : (k + 1) * chunk] = powers.astype(BF16)
        line = jnp.sum(jnp.transpose(total), axis=0, keepdims=True)
        put(sum_ref, line)
        back = times_t(exp_ref[...], table_ref[...])
        for g in range(per):
            back_ref[pl.ds(spot(g), GRANULE), :] = back[g * GRANULE : (g + 1) * GRANULE]
        return line

    @pl.when(block < block_count(count_ref))
    def _():
        for g in range(per):
            packed[g * GRANULE : (g + 1) * GRANULE, :] = rows_ref[pl.ds(spot(g), GRANULE), :]
        sums = run(None)
        fits = jnp.min(jnp.where((sums > 1e-20) & (sums < 1e30), 1.0, 0.0))

        @pl.when(fits < 0.5)
        def _():
            wide = jnp.full((BLOCK, 128), -jnp.inf, F32)
            for k in range(chunks):
                here = dot_chunk(k)
                for j in range(chunk // 128):
                    wide = jnp.maximum(wide, here[:, j * 128 : (j + 1) * 128])
            put(peak_ref, jnp.max(jnp.transpose(wide), axis=0, keepdims=True))
            run(jnp.max(wide, axis=1, keepdims=True))


def head_forward(count, order, rows, table):
    height, columns = rows.shape[0], table.shape[1]
    granules = height // GRANULE
    chunk = min(CHUNK // 2, columns // 2)
    whole = pl.Buffered(1)

    def once(i, count_ref, list_ref):
        return (0, 0)

    return pl.pallas_call(
        head_kernel,
        grid_spec=pltpu.PrefetchScalarGridSpec(
            num_scalar_prefetch=2,
            grid=(height // BLOCK,),
            in_specs=[
                pl.BlockSpec(rows.shape, once, pipeline_mode=whole),
                pl.BlockSpec(table.shape, once, pipeline_mode=whole),
            ],
            out_specs=[
                pl.BlockSpec((BLOCK, columns), block_at),
                pl.BlockSpec((height, MODEL_WIDTH), once, pipeline_mode=whole),
                pl.BlockSpec((granules, 128), once),
                pl.BlockSpec((granules, 128), once),
            ],
            scratch_shapes=[
                pltpu.VMEM((BLOCK, MODEL_WIDTH), BF16),
                pltpu.VMEM((BLOCK, chunk), F32),
                pltpu.VMEM((BLOCK, chunk), F32),
            ],
        ),
        out_shape=[
            jax.ShapeDtypeStruct((height, columns), BF16),
            jax.ShapeDtypeStruct((height, MODEL_WIDTH), F32),
            jax.ShapeDtypeStruct((granules, 128), F32),
            jax.ShapeDtypeStruct((granules, 128), F32),
        ],
        compiler_params=pltpu.CompilerParams(vmem_limit_bytes=VMEM_LIMIT),
        cost_estimate=pl.CostEstimate(
            flops=4 * height * table.size,
            bytes_accessed=2 * height * columns,
            transcendentals=height * columns,
        ),
        name="head_forward",
    )(count, order, rows, table)


def table_kernel(count_ref, list_ref, rows_ref, exp_ref, out_ref, packed, total):
    per = BLOCK // GRANULE
    block = pl.program_id(0)
    columns = exp_ref.shape[1]
    chunk = min(CHUNK, columns)

    @pl.when(block == 0)
    def _():
        total[...] = jnp.zeros(total.shape, F32)

    @pl.when(block < block_count(count_ref))
    def _():
        for g in range(per):
            at = block * per + g
            spot = pl.multiple_of(list_ref[at] * GRANULE, GRANULE)
            part = rows_ref[pl.ds(spot, GRANULE), :]
            packed[g * GRANULE : (g + 1) * GRANULE, :] = jnp.where(
                at < count_ref[0], part, jnp.zeros_like(part)
            )
        for k in range(columns // chunk):
            at = slice(k * chunk, (k + 1) * chunk)
            total[:, at] += against(packed[...], exp_ref[:, at])

    @pl.when(block == pl.num_programs(0) - 1)
    def _():
        out_ref[...] = total[...].astype(BF16)


def table_backward(count, order, rows, powers):
    height, columns = powers.shape
    whole = pl.Buffered(1)

    def once(i, count_ref, list_ref):
        return (0, 0)

    return pl.pallas_call(
        table_kernel,
        grid_spec=pltpu.PrefetchScalarGridSpec(
            num_scalar_prefetch=2,
            grid=(height // BLOCK,),
            in_specs=[
                pl.BlockSpec(rows.shape, once, pipeline_mode=whole),
                pl.BlockSpec((BLOCK, columns), block_at),
            ],
            out_specs=pl.BlockSpec((MODEL_WIDTH, columns), once, pipeline_mode=whole),
            scratch_shapes=[
                pltpu.VMEM((BLOCK, MODEL_WIDTH), BF16),
                pltpu.VMEM((MODEL_WIDTH, columns), F32),
            ],
        ),
        out_shape=jax.ShapeDtypeStruct((MODEL_WIDTH, columns), BF16),
        compiler_params=pltpu.CompilerParams(vmem_limit_bytes=VMEM_LIMIT),
        cost_estimate=pl.CostEstimate(
            flops=2 * MODEL_WIDTH * powers.size, bytes_accessed=2 * powers.size, transcendentals=0
        ),
        name="table_backward",
    )(count, order, rows, powers)


def shards(
    token_ids,
    lengths,
    deal_order,
    embed_table,
    table_mom,
    table_avg,
    model_flat,
    model_mom,
    model_avg,
):
    dp_size, shard_size = lax.axis_size("dp"), lax.axis_size("shard")
    shard_idx, dp_idx = lax.axis_index("shard"), lax.axis_index("dp")
    device_idx = lax.axis_index(("dp", "shard"))
    core = dp_bit(1)
    seqs = token_ids.shape[0]
    own_rows = seqs * LEN
    group = 2 * shard_size
    groups = dp_size // 2
    slots = group * seqs
    seq_total = groups * slots
    target_count = jnp.float32((MEAN_LENGTH - 1) * seq_total)
    features, columns = embed_table.shape
    half = columns // 2
    vocab_start = shard_idx * columns + core * half
    length = model_flat.shape[0]

    tiny = jnp.concatenate([token_ids, jnp.broadcast_to(lengths[:, None], (seqs, LEN))], 0)
    tiny = tiny.reshape((1,) * (len(bits_below(dp_size)) + len(bits_below(shard_size))) + tiny.shape)
    for k, bit in enumerate(bits_below(dp_size)[::-1]):
        tiny = join(tiny, flip_dp(tiny, bit), bit, k)
    for k, bit in enumerate(bits_below(shard_size)[::-1]):
        other = flip_shard(tiny, bit)
        axis = len(bits_below(dp_size)) + k
        tiny = jnp.where(
            (shard_idx // bit) % 2 == 0,
            jnp.concatenate([tiny, other], axis),
            jnp.concatenate([other, tiny], axis),
        )
    tiny = tiny.reshape(dp_size * shard_size, 2 * seqs, LEN)
    all_ids = tiny[:, :seqs].reshape(seq_total, LEN)
    all_lens = tiny[:, seqs:, 0].reshape(seq_total)
    here = jnp.arange(seq_total)
    longer = all_lens[None, :] > all_lens[:, None]
    tie = (all_lens[None, :] == all_lens[:, None]) & (here[None, :] < here[:, None])
    rank = jnp.sum((longer | tie).astype(jnp.int32), axis=1)
    turn, seat = rank // groups, rank % groups
    group_of = jnp.where(turn % 2 == 0, seat, groups - 1 - seat)
    place_of = group_of * slots + turn
    hits = (place_of[None, :] == here[:, None]).astype(jnp.int32)
    seq_at = jnp.sum(hits * here[None, :], axis=1)
    dealt_ids = all_ids[seq_at]
    dealt_lens = jnp.sum(hits * all_lens[None, :], axis=1)
    my_group = dp_idx // 2
    group_ids = lax.dynamic_slice_in_dim(dealt_ids, my_group * slots, slots, 0)
    group_lens = lax.dynamic_slice_in_dim(dealt_lens, my_group * slots, slots, 0)
    own_at = core * shard_size + shard_idx
    own_lens = lax.dynamic_slice_in_dim(group_lens, own_at * seqs, seqs, 0)
    own_seqs = lax.dynamic_slice_in_dim(seq_at, (my_group * group + own_at) * seqs, seqs, 0)

    places = jnp.arange(LEN)
    weight_one = (places[None, :] + 1 < group_lens[:, None]).astype(F32)
    weight_two = SECOND_WEIGHT * (places[None, :] + 2 < group_lens[:, None]).astype(F32)
    weights = jnp.stack([weight_one, weight_two]) / target_count

    per_seq = LEN // GRANULE
    starts = jnp.arange(per_seq) * GRANULE
    useful = jnp.stack([starts[None, :] + k + 1 < group_lens[:, None] for k in range(2)])
    useful = useful.reshape(-1)
    index = jnp.arange(useful.shape[0])
    before = jnp.sum((useful[None, :] & (index[None, :] < index[:, None])).astype(jnp.int32), axis=1)
    count = jnp.sum(useful.astype(jnp.int32))
    last = jnp.max(jnp.where(useful, index, 0))
    found = useful[None, :] & (before[None, :] == index[:, None])
    order = jnp.sum(jnp.where(found, index[None, :], 0), axis=1)
    order = jnp.where(index < count, order, last).astype(jnp.int32)
    count = count.reshape(1)

    everything = lax.all_gather(own_blocks(model_flat), ("dp", "shard"))

    tokens = seq_total * LEN
    bits = token_bits(tokens)
    keys = jnp.sort(dealt_ids.reshape(-1) * tokens + jnp.arange(tokens, dtype=jnp.int32))
    first_id = shard_idx * columns
    span = jnp.stack(
        [
            jnp.sum((keys < first_id * tokens).astype(jnp.int32)),
            jnp.sum(((keys >> bits) < first_id + columns).astype(jnp.int32)),
            first_id,
        ]
    ).astype(jnp.int32)
    devices = dp_size * shard_size
    picked = embed_rows(keys, span, embed_table, devices)
    picked = picked.reshape(dp_size, shard_size, features, own_rows)
    mine = ring_reduce(picked.transpose(1, 0, 2, 3)).astype(BF16)
    parts = [pick(mine, dp_idx, 0)]
    parts += [flip_dp(pick(mine, dp_idx ^ k, 0), k) for k in range(1, dp_size)]
    embedded = jnp.stack(parts)[jnp.arange(dp_size) ^ dp_idx]
    embedded = embedded.reshape(MODEL_WIDTH, own_rows).T.astype(F32)

    held_table, everything = lax.optimization_barrier((embed_table, everything))
    table_low = gather_table(held_table)
    middle_rows = PL // 128
    low_rows = middle_rows // 16 * 16
    total_devices = dp_size * shard_size
    per = GRAIN // 128
    end_row = block_starts(length, total_devices)[-1] * per
    tail = 2 * MODEL_WIDTH // 128
    square = MODEL_WIDTH * MODEL_WIDTH // 128
    *layer_zero, gains_zero = unpack_rows(
        everything, length, 0, low_rows + 16, LAYER_SHAPES, {}, 0, ((middle_rows - tail, 16),)
    )
    gain_row = middle_rows - low_rows + middle_rows - tail
    second_row = gain_row + tail + square
    base_one = gain_row // 16 * 16
    base_two = second_row // 16 * 16 - 16
    *layer_one, w_second, gains_one, gains_head = unpack_rows(
        everything, length, low_rows, end_row, LAYER_SHAPES + SQUARE, {3: tail},
        middle_rows - low_rows, ((base_one, 32), (base_two, 32)),
    )

    def gain_pair(rows, at):
        return rows[at : at + tail].reshape(2, MODEL_WIDTH)

    layer_zero.append(gain_pair(gains_zero, 0))
    layer_one.append(gain_pair(gains_one, gain_row - base_one))
    head_gains = gain_pair(gains_head, second_row - base_two).astype(F32)

    allowed = (places[None, :] <= places[:, None])[None] & (
        places[None, None, :] < own_lens[:, None, None]
    )
    allowed = allowed[:, None, None]
    rope = rope_rows(own_rows)
    hidden, kept_zero = layer_forward(embedded, layer_zero, allowed, rope)
    hidden, kept_one = layer_forward(hidden, layer_one, allowed, rope)
    scale_final = rms_scale(hidden)
    head_one = (hidden * scale_final * head_gains[0]).astype(BF16)
    all_one = group_gather(head_one).reshape(-1, MODEL_WIDTH)
    projected = jnp.dot(all_one, w_second, preferred_element_type=F32)
    scale_second = rms_scale(projected)
    all_two = (projected * scale_second * head_gains[1]).astype(BF16)
    both = jnp.concatenate([all_one, all_two], 0)
    group_rows = all_one.shape[0]

    powers, back, sums, peaks = head_forward(count, order, both, table_low)
    sums = sums[:, :GRANULE].reshape(-1, 128)
    peaks = peaks[:, :GRANULE].reshape(-1, 128)
    sum_all_rows, peak_all = sums, peaks
    for flip, bits in ((flip_shard, bits_below(shard_size)), (flip_dp, [1])):
        for bit in bits:
            stats = flip(jnp.stack([sum_all_rows, peak_all]), bit)
            top = jnp.maximum(peak_all, stats[1])
            sum_all_rows = sum_all_rows * jnp.exp(peak_all - top) + stats[0] * jnp.exp(
                stats[1] - top
            )
            peak_all = top
    log_total = (peak_all + jnp.log(sum_all_rows)).reshape(2, group, seqs, LEN)
    row_scale = (
        weights.reshape(-1, 128) * jnp.exp(peaks - peak_all) / sum_all_rows
    ).reshape(-1, 1)

    own_log = pick(log_total, own_at, 1)
    own_weights = pick(weights.reshape(2, group, seqs, LEN), own_at, 1)
    words = embedded.reshape(seqs, LEN, MODEL_WIDTH)
    next_one = jnp.roll(words, -1, 1).reshape(own_rows, MODEL_WIDTH)
    next_two = jnp.roll(words, -2, 1).reshape(own_rows, MODEL_WIDTH)
    head_two = lax.dynamic_slice_in_dim(all_two, own_at * own_rows, own_rows, 0)
    chosen_one = jnp.sum(head_one.astype(F32) * next_one, axis=-1)
    chosen_two = jnp.sum(head_two.astype(F32) * next_two, axis=-1)
    chosen = jnp.stack([chosen_one, chosen_two]).reshape(2, seqs, LEN)
    own_loss = jnp.sum(own_weights * (own_log - chosen), axis=(0, 2))

    weight_col = own_weights.reshape(2, own_rows, 1)
    grad_rows = back * row_scale
    part_two = grad_rows[group_rows:]
    own_two = lax.dynamic_slice_in_dim(part_two, own_at * own_rows, own_rows, 0)
    part_two = lax.dynamic_update_slice_in_dim(
        part_two, own_two - weight_col[1] * next_two, own_at * own_rows, 0
    )
    grad_proj, grad_gain_second = rms_back(projected, scale_second, head_gains[1], part_two)
    grad_proj_low = grad_proj.astype(BF16)
    part_one = grad_rows[:group_rows] + times_t(grad_proj_low, w_second)
    grad_final = group_reduce(part_one.reshape(2, shard_size, own_rows, MODEL_WIDTH))
    scaled_rows = (both.astype(F32) * row_scale).astype(BF16)
    head_grad = table_backward(count, order, scaled_rows, powers)
    table_part = to_owner(reduce_table(head_grad, features), features)
    grad_final = grad_final - weight_col[0] * next_one
    grad_hidden, grad_gain_final = rms_back(hidden, scale_final, head_gains[0], grad_final)

    sub_rows = owner_sub_rows(length)
    height_zero = length * (total_devices // 2 - 1) // GRAIN * per + 2 * sub_rows
    height_one = length * (total_devices - 1) // GRAIN * per + 2 * sub_rows - low_rows
    keep = height_zero - low_rows
    grad_hidden, pairs, gain_grads = layer_backward(kept_one, layer_one, rope, grad_hidden)
    own_one, send_one, kept_rows = pack_half(
        owner_rows(length, 1, low_rows),
        pairs + [(all_one, grad_proj_low)],
        [gain_grads, flat_rows(grad_gain_final, grad_gain_second)],
        None, middle_rows - low_rows, {3: tail, 4: tail}, height_one, sub_rows, keep, 0,
    )
    grad_hidden, own_one, send_one = lax.optimization_barrier((grad_hidden, own_one, send_one))
    reduced_one = reduce_half(own_one, send_one, 1)
    grad_hidden, pairs, gain_grads = layer_backward(kept_zero, layer_zero, rope, grad_hidden)
    own_zero, send_zero = pack_half(
        owner_rows(length, 0, 0), pairs, [gain_grads],
        (kept_rows, height_zero - middle_rows), 0, {3: tail}, height_zero, sub_rows, 0,
        middle_rows - low_rows,
    )
    reduced_zero = reduce_half(own_zero, send_zero, 0)
    model_sum = own_part((reduced_zero, reduced_one), length)

    one_terms = (weight_col[0] * head_one.astype(F32)).reshape(seqs, LEN, MODEL_WIDTH)
    two_terms = (weight_col[1] * head_two.astype(F32)).reshape(seqs, LEN, MODEL_WIDTH)
    token_grad = (
        grad_hidden.astype(BF16).astype(F32)
        - jnp.roll(one_terms, 1, 1).reshape(own_rows, MODEL_WIDTH)
        - jnp.roll(two_terms, 2, 1).reshape(own_rows, MODEL_WIDTH)
    ).astype(BF16)
    token_parts = token_grad.T.reshape(dp_size, features, own_rows)
    parts = [pick(token_parts, dp_idx, 0)]
    parts += [flip_dp(pick(token_parts, dp_idx ^ k, 0), k) for k in range(1, dp_size)]
    chain = [jnp.stack(parts)]
    for _ in range(shard_size - 1):
        chain.append(next_shard(chain[-1]))
    from_dp = (jnp.arange(dp_size) ^ dp_idx)[None, :]
    from_shard = (shard_idx - jnp.arange(shard_size))[:, None] % shard_size
    spots = (from_dp * shard_size + from_shard).reshape(-1).astype(jnp.int32)
    table_sum = spread_rows(keys, span, spots, chain, table_part)

    square_sum = sum_all(
        (jnp.sum(table_sum * table_sum) + jnp.sum(model_sum * model_sum)).reshape(1, 1)
    )[0, 0]
    grad_norm = jnp.sqrt(square_sum)
    factor = jnp.minimum(1.0, CLIP_NORM / (grad_norm + 1e-06))

    spots = jnp.sum(
        jnp.where(own_seqs[:, None] == here[None, :], own_loss[:, None], 0.0), axis=0
    )[None]
    all_loss = sum_all(spots)[0]
    loss_total = jnp.sum(all_loss)
    seq_loss = lax.dynamic_slice_in_dim(all_loss, device_idx * seqs, seqs, 0)
    own_slots = lax.dynamic_slice_in_dim(deal_order, device_idx * seqs, seqs, 0)
    slot_loss = all_loss[own_slots]

    results = []
    for weights_in, gradient, moment, average in (
        (embed_table, table_sum, table_mom, table_avg),
        (model_flat, model_sum, model_mom, model_avg),
    ):
        clipped = gradient * factor
        new_moment = MOMENTUM * moment + clipped
        new_weight = weights_in - LEARN_RATE * (clipped + MOMENTUM * new_moment)
        new_average = AVERAGE_KEEP * average + (1.0 - AVERAGE_KEEP) * new_weight
        results.append(
            (clipped, new_weight, new_moment, new_average, new_weight.astype(BF16))
        )
    return (loss_total, seq_loss, slot_loss, grad_norm) + results[0] + results[1]


def solution(mesh):
    both = P(("dp", "shard"))
    block = P("dp", "shard")
    return jax.shard_map(
        shards,
        mesh=mesh,
        in_specs=(P(("dp", "shard"), None), both, P(), block, block, block, both, both, both),
        out_specs=(P(), both, both, P()) + (block,) * 5 + (both,) * 5,
        check_vma=False,
    )
```

```python
import jax
import jax.numpy as jnp
from jax import lax
from jax.experimental import pallas as pl
from jax.experimental.pallas import tpu as pltpu
from jax.sharding import PartitionSpec as P

MODEL_WIDTH = 576
QUERY_HEADS = 9
KEY_VALUE_HEADS = 3
HEAD_SIZE = 64
FEED_UNITS = 1536
LAYERS = 2
LEN = 128
PL = 3540096
NP = 7413120
QKV = (QUERY_HEADS + 2 * KEY_VALUE_HEADS) * HEAD_SIZE
ROPED = (QUERY_HEADS + KEY_VALUE_HEADS) * HEAD_SIZE
MEAN_LENGTH = 96

EPSILON = 1e-05
ROPE_BASE = 100000.0
CLIP_NORM = 0.01
LEARN_RATE = 6000.0
MOMENTUM = 0.9
AVERAGE_KEEP = 0.9
SECOND_WEIGHT = 0.3
MASKED_SCORE = -1e30

GRAIN = 2048
GRANULE = 16
BLOCK = 512
CHUNK = 1024
LANES = 128
COLUMNS = 256
VMEM_LIMIT = 62 * 1024 * 1024
F32 = jnp.float32
BF16 = jnp.bfloat16


def flip_dp(values, bit):
    return lax.ppermute(values, "dp", [(i, i ^ bit) for i in range(lax.axis_size("dp"))])


def flip_shard(values, bit):
    return lax.ppermute(values, "shard", [(i, i ^ bit) for i in range(lax.axis_size("shard"))])


def next_shard(values):
    size = lax.axis_size("shard")
    return lax.ppermute(values, "shard", [(i, (i + 1) % size) for i in range(size)])


def bits_below(size):
    return [1 << k for k in range(size.bit_length() - 1)]


def dp_bit(bit):
    return (lax.axis_index("dp") // bit) % 2


def join(own, other, bit, axis):
    return jnp.where(
        dp_bit(bit) == 0,
        jnp.concatenate([own, other], axis),
        jnp.concatenate([other, own], axis),
    )


def pick(values, idx, axis):
    return lax.dynamic_index_in_dim(values, idx, axis, keepdims=False)


def high_bits():
    return bits_below(lax.axis_size("dp"))[1:]


def gather_cube(values, order):
    bits = sorted(order, reverse=True)
    out = values.reshape((1,) * len(bits) + values.shape)
    for bit in order:
        out = join(out, flip_dp(out, bit), bit, bits.index(bit))
    return out.reshape((-1,) + values.shape)


class Cube:
    def __init__(self, values, order):
        self.left = sorted(order, reverse=True)
        self.order = list(order)
        self.out = values.reshape((2,) * len(order) + values.shape[1:])
        self.start()

    def start(self):
        bit = self.order[0]
        axis = self.left.index(bit)
        mine = dp_bit(bit)
        self.got = flip_dp(pick(self.out, 1 - mine, axis).astype(BF16), bit)
        self.keep = pick(self.out, mine, axis)

    def step(self):
        self.out = self.keep.astype(F32) + self.got.astype(F32)
        self.left.remove(self.order.pop(0))
        if self.order:
            self.start()
        return bool(self.order)

    def finish(self):
        while self.order:
            self.step()
        return self.out


def tie(main, cubes):
    main, gots = lax.optimization_barrier((main, [cube.got for cube in cubes]))
    for cube, got in zip(cubes, gots):
        cube.got = got
    return main


def ring_gather(values, hook=None):
    size = lax.axis_size("shard")
    me = lax.axis_index("shard")
    parts = [values]
    for k in range(size - 1):
        parts.append(next_shard(parts[-1]))
        if hook is not None and k == 1:
            parts[-1] = hook(parts[-1])
    stacked = jnp.stack(parts[::-1])
    return jnp.roll(stacked, me + 1, axis=0)


def ring_reduce(values, hooks=()):
    size = lax.axis_size("shard")
    me = lax.axis_index("shard")
    total = None
    for step in range(size - 1):
        term = pick(values, (me - 1 - step) % size, 0).astype(F32)
        if total is not None:
            term = term + total
        got = next_shard(term.astype(BF16))
        if step < len(hooks):
            got = hooks[step](got)
        total = got.astype(F32)
    return total + pick(values, me, 0).astype(F32)


def group_gather(rows, hook=None):
    parts = ring_gather(rows, hook)
    other = flip_dp(parts, 1)
    return join(parts[None], other[None], 1, 0)


def group_reduce(parts, hooks):
    mine = dp_bit(1)
    got = hooks[0](flip_dp(pick(parts, 1 - mine, 0).astype(BF16), 1))
    return ring_reduce(pick(parts, mine, 0).astype(F32) + got.astype(F32), hooks[1:])


def sum_all(value):
    total = value
    for bit in bits_below(lax.axis_size("dp")):
        total = total + flip_dp(total, bit)
    for bit in bits_below(lax.axis_size("shard")):
        total = total + flip_shard(total, bit)
    return total


def top_bit():
    return high_bits()[-1]


def block_starts(length, total):
    return [length * i // GRAIN for i in range(total)] + [-(-length * total // GRAIN)]


def own_blocks(model_flat):
    length = model_flat.shape[0]
    total = lax.axis_size("dp") * lax.axis_size("shard")
    device = lax.axis_index(("dp", "shard"))
    low = model_flat.astype(BF16)
    before = lax.ppermute(
        low[length - GRAIN :], ("dp", "shard"), [(i, i + 1) for i in range(total - 1)]
    )
    starts = block_starts(length, total)
    blocks = max(starts[i + 1] - starts[i] for i in range(total))
    extended = jnp.concatenate([before, low, jnp.zeros((3 * GRAIN,), BF16)])
    shift = (length * device) % GRAIN
    whole = lax.dynamic_slice_in_dim(extended, GRAIN - shift, blocks * GRAIN, 0)
    return whole.reshape(-1, 128)


LAYER_SHAPES = (
    (MODEL_WIDTH, QKV),
    (MODEL_WIDTH, MODEL_WIDTH),
    (MODEL_WIDTH, 2 * FEED_UNITS),
    (FEED_UNITS, MODEL_WIDTH),
)
SQUARE = ((MODEL_WIDTH, MODEL_WIDTH),)
TALL = 64


def line_up(flat_at, out, height, breadth):
    tiles, odd = breadth // 128, breadth % 128
    if not odd:
        for j in range(tiles):
            out(0, j, flat_at(j, height, tiles))
        return
    period = 2 * tiles + 1
    loads = [flat_at(j, height // 2, period) for j in range(period)]
    for j in range(tiles + 1):
        out(0, j, loads[j])
        after = loads[min(tiles + j + 1, period - 1)]
        out(1, j, jnp.concatenate([loads[tiles + j][:, 64:], after[:, :64]], 1))


def unpack_matrix(flat_ref, at, out_ref, wide_ref, tall_ref):
    height, breadth = out_ref.shape
    rows = TALL * breadth // 128
    shift = at % 16
    load = rows + (16 if shift else 0)

    @pl.loop(0, height // TALL)
    def _(k):
        first = pl.multiple_of(k * rows + (at - shift), 16)
        wide_ref[:load, :] = flat_ref[pl.ds(first, load), :].astype(F32)
        out_at = pl.multiple_of(k * TALL, TALL)

        def flat_at(j, count, stride):
            return wide_ref[pl.ds(shift + j, count, stride=stride), :]

        if breadth % 128:
            def put(parity, j, values):
                tall_ref[j, pl.ds(parity, TALL // 2, stride=2), :] = values

            line_up(flat_at, put, TALL, breadth)
            for j in range(breadth // 128 + 1):
                stop = min((j + 1) * 128, breadth)
                out_ref[pl.ds(out_at, TALL), j * 128 : stop] = tall_ref[
                    j, :, : stop - j * 128
                ].astype(BF16)
        else:
            def put(_, j, values):
                out_ref[pl.ds(out_at, TALL), j * 128 : (j + 1) * 128] = values.astype(BF16)

            line_up(flat_at, put, TALL, breadth)


def unpack_rows(everything, length, first_row, last_row, shapes, gaps, lead, tails):
    total = lax.axis_size("dp") * lax.axis_size("shard")
    starts = block_starts(length, total)
    per = GRAIN // 128
    moves = []
    for owner in range(total):
        low = max(starts[owner] * per, first_row)
        high = min(starts[owner + 1] * per, last_row)
        if low < high:
            moves.append((owner, low - starts[owner] * per, low - first_row, high - low))
    outs = [jax.ShapeDtypeStruct(shape, BF16) for shape in shapes]
    outs += [jax.ShapeDtypeStruct((rows, 128), BF16) for _, rows in tails]
    wide_rows = TALL * max(shape[1] for shape in shapes) // 128 + 16
    height = last_row - first_row

    def kernel(all_ref, *refs):
        outs, (flat_ref, wide_ref, tall_ref, sems) = refs[:-4], refs[-4:]
        copies = [
            pltpu.make_async_copy(
                all_ref.at[owner, pl.ds(source, rows)], flat_ref.at[pl.ds(at, rows)], sems.at[k]
            )
            for k, (owner, source, at, rows) in enumerate(moves)
        ]
        for copy in copies:
            copy.start()
        arrived = 0
        at = lead
        for k, (tall, wide) in enumerate(shapes):
            end = at + tall * wide // 128
            while arrived < len(moves) and moves[arrived][2] < end:
                copies[arrived].wait()
                arrived += 1
            unpack_matrix(flat_ref, at, outs[k], wide_ref, tall_ref)
            at = end + gaps.get(k, 0)
        for copy in copies[arrived:]:
            copy.wait()
        for k, (start, rows) in enumerate(tails):
            outs[len(shapes) + k][...] = flat_ref[pl.ds(start, rows), :]

    return pl.pallas_call(
        kernel,
        in_specs=[pl.BlockSpec(memory_space=pl.ANY)],
        out_specs=[pl.BlockSpec(memory_space=pltpu.VMEM)] * len(outs),
        out_shape=outs,
        scratch_shapes=[
            pltpu.VMEM((height, 128), BF16),
            pltpu.VMEM((wide_rows, 128), F32),
            pltpu.VMEM((8, TALL, 128), F32),
            pltpu.SemaphoreType.DMA((len(moves),)),
        ],
        compiler_params=pltpu.CompilerParams(vmem_limit_bytes=VMEM_LIMIT),
        cost_estimate=pl.CostEstimate(flops=0, bytes_accessed=512 * height, transcendentals=0),
        name="unpack_rows",
    )(everything)


def pack_matrix(left_ref, right_ref, flat_ref, at, tall_ref):
    height, breadth = left_ref.shape[1], right_ref.shape[1]
    part = 512 if height % 512 == 0 else height
    tiles, odd = breadth // 128, breadth % 128
    for k in range(height // part):
        first = at + k * part * breadth // 128
        product = against(left_ref[:, k * part : (k + 1) * part], right_ref[...])
        for j in range(tiles + (1 if odd else 0)):
            stop = min((j + 1) * 128, breadth)
            tall_ref[j, :part, : stop - j * 128] = product[:, j * 128 : stop]
        if not odd:
            for j in range(tiles):
                flat_ref[pl.ds(first + j, part, stride=tiles), :] = tall_ref[j, :part, :]
            continue
        period = 2 * tiles + 1
        count = part // 2

        def half(parity, j):
            return tall_ref[j, pl.ds(parity, count, stride=2), :]

        for j in range(tiles):
            flat_ref[pl.ds(first + j, count, stride=period), :] = half(0, j)
        flat_ref[pl.ds(first + tiles, count, stride=period), :] = jnp.concatenate(
            [half(0, tiles)[:, :64], half(1, 0)[:, :64]], 1
        )
        for j in range(tiles):
            flat_ref[pl.ds(first + tiles + 1 + j, count, stride=period), :] = jnp.concatenate(
                [half(1, j)[:, 64:], half(1, j + 1)[:, :64]], 1
            )


def pack_kernel(info_ref, *refs, pairs, loose, early, lead, gaps, count, sub_rows, keep, first_loose):
    lefts, rights, refs = refs[:pairs], refs[pairs : 2 * pairs], refs[2 * pairs :]
    loose_refs, refs = refs[:loose], refs[loose:]
    if early:
        early_ref, refs = refs[0], refs[1:]
    own_ref, send_ref, refs = refs[0], refs[1], refs[2:]
    if keep:
        keep_ref, refs = refs[0], refs[1:]
    flat_ref, low_ref, tall_ref, sems = refs
    height = flat_ref.shape[0]
    at = lead
    for k in range(pairs):
        pack_matrix(lefts[k], rights[k], flat_ref, at, tall_ref)
        at += lefts[k].shape[1] * rights[k].shape[1] // 128
        if k in gaps:
            flat_ref[at : at + gaps[k], :] = loose_refs[list(gaps).index(k)][...]
            at += gaps[k]
    if early:
        flat_ref[at : at + early, :] = early_ref[...].astype(F32)[first_loose : first_loose + early]
        at += early
    if at < height:
        flat_ref[at:height, :] = jnp.zeros((height - at, 128), F32)
    step = 16 * 32
    for row in range(0, height, step):
        rows = min(step, height - row)
        low_ref[row : row + rows, :] = flat_ref[row : row + rows, :].astype(BF16)
    copies = []
    for idx in range(count):
        for k, ref in enumerate((own_ref, send_ref)):
            row = pl.multiple_of(info_ref[k * count + idx], 16)
            copies.append(
                pltpu.make_async_copy(
                    low_ref.at[pl.ds(row, sub_rows)], ref.at[idx], sems.at[k * count + idx]
                )
            )
    for copy in copies:
        copy.start()
    if keep:
        keep_ref[...] = low_ref[:keep, :]
    for copy in copies:
        copy.wait()


def pack_half(info, pairs, loose, early, lead, gaps, height, sub_rows, keep, skip):
    count = info.shape[0] // 2
    lefts = [left for left, _ in pairs]
    rights = [right for _, right in pairs]
    in_place = pl.BlockSpec(memory_space=pltpu.VMEM)
    anywhere = pl.BlockSpec(memory_space=pl.ANY)
    operands = lefts + rights + loose + ([early[0]] if early is not None else [])
    outs = [jax.ShapeDtypeStruct((count, sub_rows, 128), BF16)] * 2
    specs = [anywhere] * 2
    if keep:
        outs.append(jax.ShapeDtypeStruct((keep, 128), BF16))
        specs.append(in_place)

    def kernel(info_ref, *refs):
        pack_kernel(
            info_ref, *refs, pairs=len(pairs), loose=len(loose),
            early=0 if early is None else early[1], lead=lead, gaps=gaps,
            count=count, sub_rows=sub_rows, keep=keep, first_loose=skip,
        )

    flops = sum(2 * left.size * right.shape[1] for left, right in pairs)
    return pl.pallas_call(
        kernel,
        in_specs=[pl.BlockSpec(memory_space=pltpu.SMEM)] + [in_place] * len(operands),
        out_specs=specs,
        out_shape=outs,
        scratch_shapes=[
            pltpu.VMEM((height, 128), F32),
            pltpu.VMEM((height, 128), BF16),
            pltpu.VMEM((max(right.shape[1] for right in rights) // 128, MODEL_WIDTH, 128), F32),
            pltpu.SemaphoreType.DMA((2 * count,)),
        ],
        compiler_params=pltpu.CompilerParams(vmem_limit_bytes=VMEM_LIMIT),
        cost_estimate=pl.CostEstimate(
            flops=flops, bytes_accessed=512 * height, transcendentals=0
        ),
        name="pack_half",
    )(info, *operands)


def owner_rows(length, which, first_row):
    dp_size, shard_size = lax.axis_size("dp"), lax.axis_size("shard")
    sub_rows = owner_sub_rows(length)
    per = GRAIN // 128
    j = jnp.arange(2)[:, None, None]
    x = jnp.arange(dp_size // 4)[None, :, None]
    z = jnp.arange(shard_size)[None, None, :]
    rows = []
    for core in (dp_bit(1), 1 - dp_bit(1)):
        owner = ((which * (dp_size // 4) + x) * 2 + core) * shard_size + z
        rows.append((length * owner // GRAIN * per + sub_rows * j - first_row).reshape(-1))
    return jnp.concatenate(rows).astype(jnp.int32)


def owner_sub_rows(length):
    blocks = -(-(GRAIN - 1 + length) // GRAIN)
    return (blocks + blocks % 2) * (GRAIN // 128) // 2


def half_cubes(own, got):
    shard_size = lax.axis_size("shard")
    paired = (own.astype(F32) + got.astype(F32)).astype(BF16)
    paired = paired.reshape((-1, shard_size) + own.shape[1:])
    half = shard_size // 2
    order = high_bits()
    return [Cube(paired[:, :half], order), Cube(paired[:, half:], order[::-1])]


def finish_cubes(cubes):
    return ring_reduce(jnp.concatenate([cube.finish() for cube in cubes], 0).astype(BF16))


def to_top(done, which):
    top = top_bit()
    away = [(i, i ^ top) for i in range(lax.axis_size("dp")) if (i // top) % 2 != which]
    return done, lax.ppermute(done.astype(BF16), "dp", away).astype(F32)


def own_part(halves, length):
    (done_zero, got_zero), (done_one, got_one) = halves
    top = dp_bit(top_bit())
    lower = jnp.where(top == 0, done_zero, got_one)
    upper = jnp.where(top == 0, got_zero, done_one)
    shift = (length * lax.axis_index(("dp", "shard"))) % GRAIN
    flat = jnp.concatenate([lower, upper], 0).reshape(-1)
    return lax.dynamic_slice_in_dim(flat, shift, length, 0)


class TableGather:
    def __init__(self, embed_table):
        low = embed_table.astype(BF16)
        half = low.shape[1] // 2
        core = dp_bit(1)
        own = lax.dynamic_slice_in_dim(low, core * half, half, 1)
        send = lax.dynamic_slice_in_dim(low, (1 - core) * half, half, 1)
        pair = join(own, flip_dp(send, 1), 1, 0)
        self.bits = sorted(high_bits(), reverse=True)
        shape = (1,) * len(self.bits) + (pair.shape[0], half // 2)
        self.sides = [pair[:, : half // 2].reshape(shape), pair[:, half // 2 :].reshape(shape)]
        self.orders = [high_bits(), high_bits()[::-1]]
        self.start()

    def start(self):
        self.got = [flip_dp(side, order[0]) for side, order in zip(self.sides, self.orders)]

    def step(self):
        self.sides = [
            join(side, other, order[0], self.bits.index(order[0]))
            for side, other, order in zip(self.sides, self.got, self.orders)
        ]
        self.orders = [order[1:] for order in self.orders]
        if self.orders[0]:
            self.start()

    def tied(self, main):
        main, self.got = lax.optimization_barrier((main, self.got))
        return main

    def finish(self):
        while self.orders[0]:
            self.step()
        return jnp.concatenate([side.reshape(MODEL_WIDTH, -1) for side in self.sides], 1)


def owner_flip(joined, features):
    core = dp_bit(1)
    send = lax.dynamic_slice_in_dim(joined, (1 - core) * features, features, 0)
    return flip_dp(send, 1)


def owner_join(joined, got, features):
    own = lax.dynamic_slice_in_dim(joined, dp_bit(1) * features, features, 0)
    return join(own, got, 1, 1)


def rms_scale(values):
    return lax.rsqrt(jnp.mean(values * values, axis=-1, keepdims=True) + EPSILON)


def rms_back(values, scale, gain, grad):
    weighted = grad * gain
    inner = jnp.sum(weighted * values, axis=-1, keepdims=True)
    grad_values = scale * weighted - values * (scale * scale * scale * inner / MODEL_WIDTH)
    grad_gain = jnp.sum(grad * values * scale, axis=0)
    return grad_values, grad_gain


def rope_rows(rows):
    halves = HEAD_SIZE // 2
    inverse = ROPE_BASE ** (-jnp.arange(halves, dtype=F32) * 2.0 / HEAD_SIZE)
    angles = jnp.arange(LEN, dtype=F32)[:, None] * inverse[None, :]
    cosine, sine = jnp.cos(angles), jnp.sin(angles)
    heads = ROPED // HEAD_SIZE
    cos_full = jnp.tile(jnp.concatenate([cosine, cosine], 1), (rows // LEN, heads))
    sin_full = jnp.tile(jnp.concatenate([-sine, sine], 1), (rows // LEN, heads))
    return cos_full, sin_full


def against(left, right):
    return lax.dot_general(left, right, (((0,), (0,)), ((), ())), preferred_element_type=F32)


def times_t(left, right):
    return lax.dot_general(left, right, (((1,), (1,)), ((), ())), preferred_element_type=F32)


QUERY_WIDTH = QUERY_HEADS * HEAD_SIZE
VALUE_WIDTH = KEY_VALUE_HEADS * HEAD_SIZE
SCALING = HEAD_SIZE ** (-0.5)


def swap_halves(values):
    halves, width = HEAD_SIZE // 2, values.shape[1]
    lanes = lax.broadcasted_iota(jnp.int32, values.shape, 1) % HEAD_SIZE
    return jnp.where(
        lanes < halves, pltpu.roll(values, width - halves, 1), pltpu.roll(values, halves, 1)
    )


def head_cols(idx):
    return slice(idx * HEAD_SIZE, (idx + 1) * HEAD_SIZE)


def attention_probs(query, key, allowed):
    scores = jnp.where(allowed, times_t(query, key) * SCALING, MASKED_SCORE)
    powers = jnp.exp(scores - jnp.max(scores, axis=1, keepdims=True))
    return powers / jnp.sum(powers, axis=1, keepdims=True)


def allowed_pairs(length):
    later = lax.broadcasted_iota(jnp.int32, (LEN, LEN), 0)
    sooner = lax.broadcasted_iota(jnp.int32, (LEN, LEN), 1)
    return (sooner <= later) & (sooner < length)


def forward_kernel(
    len_ref, hidden_ref, qkv_ref, out_ref, gateup_ref, down_ref, gain_ref, cos_ref, sin_ref,
    output_ref, normed_ref, turned_ref, value_ref, attended_ref, middle_ref, normed_two_ref,
    gate_up_ref, acted_ref,
):
    hidden = hidden_ref[...]
    normed_ref[...] = (hidden * rms_scale(hidden) * gain_ref[0:1, :]).astype(BF16)
    qkv = jnp.dot(normed_ref[...], qkv_ref[...], preferred_element_type=F32)
    straight = qkv[:, :ROPED]
    turned_ref[...] = (straight * cos_ref[...] + swap_halves(straight) * sin_ref[...]).astype(BF16)
    value_ref[...] = qkv[:, ROPED:].astype(BF16)
    group = QUERY_HEADS // KEY_VALUE_HEADS
    for seq in range(hidden.shape[0] // LEN):
        rows = slice(seq * LEN, (seq + 1) * LEN)
        allowed = allowed_pairs(len_ref[seq])
        for head in range(QUERY_HEADS):
            key = turned_ref[rows, head_cols(QUERY_HEADS + head // group)]
            value = value_ref[rows, head_cols(head // group)]
            probs = attention_probs(turned_ref[rows, head_cols(head)], key, allowed)
            attended_ref[rows, head_cols(head)] = jnp.dot(
                probs.astype(BF16), value, preferred_element_type=F32
            ).astype(BF16)
    middle = hidden + jnp.dot(attended_ref[...], out_ref[...], preferred_element_type=F32)
    middle_ref[...] = middle
    normed_two_ref[...] = (middle * rms_scale(middle) * gain_ref[1:2, :]).astype(BF16)
    gate_up_ref[...] = jnp.dot(normed_two_ref[...], gateup_ref[...], preferred_element_type=F32)
    gate = gate_up_ref[:, :FEED_UNITS]
    acted_ref[...] = (gate / (1.0 + jnp.exp(-gate)) * gate_up_ref[:, FEED_UNITS:]).astype(BF16)
    output_ref[...] = middle + jnp.dot(acted_ref[...], down_ref[...], preferred_element_type=F32)


def backward_kernel(
    len_ref, grad_ref, hidden_ref, qkv_ref, out_ref, gateup_ref, down_ref, gain_ref, cos_ref,
    sin_ref, turned_ref, value_ref, middle_ref, gate_up_ref,
    grad_in_ref, low_ref, grad_gu_ref, grad_mid_ref, grad_qkv_ref, gains_out_ref,
    grad_att_ref, grad_turned_ref,
):
    grad = grad_ref[...]
    low_ref[...] = grad.astype(BF16)
    grad_act = times_t(low_ref[...], down_ref[...]).astype(BF16).astype(F32)
    gate, up = gate_up_ref[:, :FEED_UNITS], gate_up_ref[:, FEED_UNITS:]
    sigma = 1.0 / (1.0 + jnp.exp(-gate))
    grad_gu_ref[:, FEED_UNITS:] = (grad_act * (gate * sigma)).astype(BF16)
    grad_gu_ref[:, :FEED_UNITS] = (
        grad_act * up * (sigma * (1.0 + gate * (1.0 - sigma)))
    ).astype(BF16)
    middle = middle_ref[...]
    grad_mid, gain_two = rms_back(
        middle, rms_scale(middle), gain_ref[1:2, :], times_t(grad_gu_ref[...], gateup_ref[...])
    )
    grad_mid = grad_mid + grad
    grad_mid_ref[...] = grad_mid.astype(BF16)
    grad_att_ref[...] = times_t(grad_mid_ref[...], out_ref[...]).astype(BF16)
    group = QUERY_HEADS // KEY_VALUE_HEADS
    for seq in range(grad.shape[0] // LEN):
        rows = slice(seq * LEN, (seq + 1) * LEN)
        allowed = allowed_pairs(len_ref[seq])
        for kv in range(KEY_VALUE_HEADS):
            key = turned_ref[rows, head_cols(QUERY_HEADS + kv)]
            value = value_ref[rows, head_cols(kv)]
            grad_key = jnp.zeros((LEN, HEAD_SIZE), F32)
            grad_value = jnp.zeros((LEN, HEAD_SIZE), F32)
            for head in range(kv * group, (kv + 1) * group):
                query = turned_ref[rows, head_cols(head)]
                grad_out = grad_att_ref[rows, head_cols(head)]
                probs = attention_probs(query, key, allowed)
                grad_probs = times_t(grad_out, value)
                grad_value = grad_value + against(probs.astype(BF16), grad_out)
                inner = jnp.sum(grad_probs * probs, axis=1, keepdims=True)
                grad_scores = (probs * (grad_probs - inner)).astype(BF16)
                grad_query = jnp.dot(grad_scores, key, preferred_element_type=F32) * SCALING
                grad_turned_ref[rows, head_cols(head)] = grad_query.astype(BF16).astype(F32)
                grad_key = grad_key + against(grad_scores, query)
            grad_turned_ref[rows, head_cols(QUERY_HEADS + kv)] = (
                (grad_key * SCALING).astype(BF16).astype(F32)
            )
            at = slice(ROPED + kv * HEAD_SIZE, ROPED + (kv + 1) * HEAD_SIZE)
            grad_qkv_ref[rows, at] = grad_value.astype(BF16)
    turned = grad_turned_ref[...]
    grad_qkv_ref[:, :ROPED] = (
        turned * cos_ref[...] - swap_halves(turned) * sin_ref[...]
    ).astype(BF16)
    hidden = hidden_ref[...]
    grad_hidden, gain_one = rms_back(
        hidden, rms_scale(hidden), gain_ref[0:1, :], times_t(grad_qkv_ref[...], qkv_ref[...])
    )
    grad_in_ref[...] = grad_hidden + grad_mid
    gains_out_ref[...] = jnp.concatenate([gain_one[None], gain_two[None]], 0)


def layer_call(kernel, name, lens, operands, outs, scratch, flops):
    in_place = pl.BlockSpec(memory_space=pltpu.VMEM)
    return pl.pallas_call(
        kernel,
        in_specs=[pl.BlockSpec(memory_space=pltpu.SMEM)] + [in_place] * len(operands),
        out_specs=[in_place] * len(outs),
        out_shape=[jax.ShapeDtypeStruct(shape, dtype) for shape, dtype in outs],
        scratch_shapes=scratch,
        compiler_params=pltpu.CompilerParams(vmem_limit_bytes=VMEM_LIMIT),
        cost_estimate=pl.CostEstimate(flops=flops, bytes_accessed=8 * PL, transcendentals=0),
        name=name,
    )(lens, *operands)


def layer_forward(hidden, pieces, lens, rope):
    rows = hidden.shape[0]
    outs = [
        ((rows, MODEL_WIDTH), F32),
        ((rows, MODEL_WIDTH), BF16),
        ((rows, ROPED), BF16),
        ((rows, VALUE_WIDTH), BF16),
        ((rows, QUERY_WIDTH), BF16),
        ((rows, MODEL_WIDTH), F32),
        ((rows, MODEL_WIDTH), BF16),
        ((rows, 2 * FEED_UNITS), F32),
        ((rows, FEED_UNITS), BF16),
    ]
    output, *kept = layer_call(
        forward_kernel, "layer_forward", lens, [hidden, *pieces, *rope], outs, [], 2 * rows * PL
    )
    return output, (hidden, *kept)


def layer_backward(kept, pieces, lens, rope, grad_output):
    hidden, normed, turned, value, attended, middle, normed_two, gate_up, acted = kept
    rows = hidden.shape[0]
    outs = [
        ((rows, MODEL_WIDTH), F32),
        ((rows, MODEL_WIDTH), BF16),
        ((rows, 2 * FEED_UNITS), BF16),
        ((rows, MODEL_WIDTH), BF16),
        ((rows, QKV), BF16),
        ((2, MODEL_WIDTH), F32),
    ]
    scratch = [pltpu.VMEM((rows, QUERY_WIDTH), BF16), pltpu.VMEM((rows, ROPED), F32)]
    operands = [grad_output, hidden, *pieces, *rope, turned, value, middle, gate_up]
    grad_input, low, grad_gu, grad_mid, grad_qkv, gains = layer_call(
        backward_kernel, "layer_backward", lens, operands, outs, scratch, 2 * rows * PL
    )
    pairs = [(normed, grad_qkv), (attended, grad_mid), (normed_two, grad_gu), (acted, low)]
    return grad_input, pairs, gains.reshape(-1, 128)


def flat_rows(first, second):
    return jnp.concatenate([first, second]).reshape(-1, 128)


def token_bits(tokens):
    return tokens.bit_length() - 1


def for_chunks(keys_ref, lines_ref, span_ref, columns, run):
    bits = token_bits(keys_ref.shape[0])
    base = span_ref[2]
    places = lax.broadcasted_iota(jnp.int32, (LANES, LANES), 1)

    def chunk_step(chunk, _):
        line = lines_ref[pl.ds(chunk, 1), :]
        ids = jnp.transpose(jnp.broadcast_to(lax.shift_right_logical(line, bits), (LANES, LANES)))
        low = lax.shift_right_logical(keys_ref[chunk * LANES], bits) - base
        high = lax.shift_right_logical(keys_ref[chunk * LANES + LANES - 1], bits) - base
        first = jnp.maximum(low, 0) // COLUMNS
        last = jnp.minimum(high, columns - 1) // COLUMNS

        def hot(block):
            parts = []
            for k in range(COLUMNS // LANES):
                match = ids - (base + block * COLUMNS + k * LANES) == places
                parts.append(jnp.where(match, 1.0, 0.0).astype(BF16))
            return jnp.concatenate(parts, 1)

        run(chunk, first, last + 1, hot)
        return 0

    lax.fori_loop(span_ref[0] // LANES, (span_ref[1] + LANES - 1) // LANES, chunk_step, 0)


def row_of(keys_ref, at):
    return keys_ref[at] & (keys_ref.shape[0] - 1)


def embed_kernel(keys_ref, span_ref, lines_ref, table_ref, out_ref, low_ref, rows_ref, found_ref):
    features, columns = table_ref.shape
    blocks, _, width = out_ref.shape
    low_ref[:features, :] = table_ref[...].astype(BF16)
    low_ref[features:, :] = jnp.zeros((LANES - features, columns), BF16)
    for k in range(blocks):
        rows_ref[k * width : (k + 1) * width, :] = jnp.zeros((width, LANES), F32)

    def run(chunk, first, last, hot):
        def block_step(block, total):
            at = pl.multiple_of(block * COLUMNS, COLUMNS)
            return total + times_t(hot(block), low_ref[:, pl.ds(at, COLUMNS)])

        found_ref[...] = lax.fori_loop(first, last, block_step, jnp.zeros((LANES, LANES), F32))

        def move(k, _):
            for j in range(8):
                row = row_of(keys_ref, chunk * LANES + k * 8 + j)
                rows_ref[pl.ds(row, 1), :] = found_ref[pl.ds(k * 8 + j, 1), :]
            return 0

        lax.fori_loop(0, LANES // 8, move, 0)

    for_chunks(keys_ref, lines_ref, span_ref, columns, run)

    def finish(k, _):
        at = pl.multiple_of(k * width, width)
        out_ref[k] = jnp.transpose(rows_ref[pl.ds(at, width), :])[:features].astype(BF16)
        return 0

    lax.fori_loop(0, blocks, finish, 0)


def embed_rows(keys, span, table, blocks):
    tokens = keys.shape[0]
    features, columns = table.shape
    scalars = pl.BlockSpec(memory_space=pltpu.SMEM)
    in_place = pl.BlockSpec(memory_space=pltpu.VMEM)
    return pl.pallas_call(
        embed_kernel,
        in_specs=[scalars, scalars, in_place, in_place],
        out_specs=in_place,
        out_shape=jax.ShapeDtypeStruct((blocks, features, tokens // blocks), BF16),
        scratch_shapes=[
            pltpu.VMEM((LANES, columns), BF16),
            pltpu.VMEM((tokens, LANES), F32),
            pltpu.VMEM((LANES, LANES), F32),
        ],
        compiler_params=pltpu.CompilerParams(vmem_limit_bytes=VMEM_LIMIT),
        cost_estimate=pl.CostEstimate(
            flops=2 * tokens * LANES * COLUMNS, bytes_accessed=4 * table.size, transcendentals=0
        ),
        name="embed_rows",
    )(keys, span, keys.reshape(-1, LANES), table)


def spread_kernel(keys_ref, span_ref, place_ref, lines_ref, *refs):
    parts, (base_ref, out_ref, rows_ref, packed_ref) = refs[:-4], refs[-4:]
    features, columns = base_ref.shape
    count, _, width = parts[0].shape
    for k, part in enumerate(parts):
        def unfold(j, _):
            at = pl.multiple_of(place_ref[k * count + j] * width, width)
            flat = part[j].astype(F32)
            flat = jnp.concatenate([flat, jnp.zeros((LANES - features, width), F32)], 0)
            rows_ref[pl.ds(at, width), :] = jnp.transpose(flat)
            return 0

        lax.fori_loop(0, count, unfold, 0)
    out_ref[...] = base_ref[...]

    def run(chunk, first, last, hot):
        def move(k, _):
            for j in range(8):
                row = row_of(keys_ref, chunk * LANES + k * 8 + j)
                packed_ref[pl.ds(k * 8 + j, 1), :] = rows_ref[pl.ds(row, 1), :]
            return 0

        lax.fori_loop(0, LANES // 8, move, 0)
        packed = packed_ref[...].astype(BF16)

        def block_step(block, _):
            at = pl.multiple_of(block * COLUMNS, COLUMNS)
            out_ref[:, pl.ds(at, COLUMNS)] += against(packed, hot(block))[:features]
            return 0

        lax.fori_loop(first, last, block_step, 0)

    for_chunks(keys_ref, lines_ref, span_ref, columns, run)


def spread_rows(keys, span, places, parts, base):
    tokens = keys.shape[0]
    scalars = pl.BlockSpec(memory_space=pltpu.SMEM)
    in_place = pl.BlockSpec(memory_space=pltpu.VMEM)
    return pl.pallas_call(
        spread_kernel,
        in_specs=[scalars] * 3 + [in_place] * (2 + len(parts)),
        out_specs=in_place,
        out_shape=jax.ShapeDtypeStruct(base.shape, F32),
        scratch_shapes=[
            pltpu.VMEM((tokens, LANES), F32),
            pltpu.VMEM((LANES, LANES), F32),
        ],
        compiler_params=pltpu.CompilerParams(vmem_limit_bytes=VMEM_LIMIT),
        cost_estimate=pl.CostEstimate(
            flops=2 * tokens * LANES * COLUMNS, bytes_accessed=8 * base.size, transcendentals=0
        ),
        name="spread_rows",
    )(keys, span, places, keys.reshape(-1, LANES), *parts, base)


def block_count(count_ref):
    per = BLOCK // GRANULE
    return (count_ref[0] + per - 1) // per


def block_at(i, count_ref, list_ref):
    return (jnp.minimum(i, jnp.maximum(block_count(count_ref) - 1, 0)), 0)


def head_kernel(
    count_ref, list_ref, rows_ref, table_ref,
    exp_ref, back_ref, sum_ref, peak_ref,
    packed, even, odd,
):
    columns = table_ref.shape[1]
    chunk = even.shape[1]
    chunks = columns // chunk
    logits = (even, odd)
    per = BLOCK // GRANULE
    block = pl.program_id(0)

    @pl.when(block == 0)
    def _():
        back_ref[...] = jnp.zeros(back_ref.shape, F32)
        sum_ref[...] = jnp.ones(sum_ref.shape, F32)
        peak_ref[...] = jnp.zeros(peak_ref.shape, F32)

    def spot(g):
        return pl.multiple_of(list_ref[block * per + g] * GRANULE, GRANULE)

    def dot_chunk(k):
        return jnp.dot(
            packed[...], table_ref[:, k * chunk : (k + 1) * chunk], preferred_element_type=F32
        )

    def put(stat_ref, line):
        for g in range(per):
            lane = g * GRANULE // 128 * 128
            part = line[:, lane : lane + 128]
            if g * GRANULE % 128:
                part = pltpu.roll(part, 128 - g * GRANULE % 128, 1)
            stat_ref[pl.ds(list_ref[block * per + g], 1), :] = part

    def run(peak):
        total = jnp.zeros((BLOCK, 128), F32)
        logits[0][...] = dot_chunk(0)
        for k in range(chunks):
            if k + 1 < chunks:
                logits[(k + 1) % 2][...] = dot_chunk(k + 1)
            here = logits[k % 2][...]
            powers = jnp.exp(here if peak is None else here - peak)
            for j in range(chunk // 128):
                total = total + powers[:, j * 128 : (j + 1) * 128]
            exp_ref[:, k * chunk : (k + 1) * chunk] = powers.astype(BF16)
        line = jnp.sum(jnp.transpose(total), axis=0, keepdims=True)
        put(sum_ref, line)
        back = times_t(exp_ref[...], table_ref[...])
        for g in range(per):
            back_ref[pl.ds(spot(g), GRANULE), :] = back[g * GRANULE : (g + 1) * GRANULE]
        return line

    @pl.when(block < block_count(count_ref))
    def _():
        for g in range(per):
            packed[g * GRANULE : (g + 1) * GRANULE, :] = rows_ref[pl.ds(spot(g), GRANULE), :]
        sums = run(None)
        fits = jnp.min(jnp.where((sums > 1e-20) & (sums < 1e30), 1.0, 0.0))

        @pl.when(fits < 0.5)
        def _():
            wide = jnp.full((BLOCK, 128), -jnp.inf, F32)
            for k in range(chunks):
                here = dot_chunk(k)
                for j in range(chunk // 128):
                    wide = jnp.maximum(wide, here[:, j * 128 : (j + 1) * 128])
            put(peak_ref, jnp.max(jnp.transpose(wide), axis=0, keepdims=True))
            run(jnp.max(wide, axis=1, keepdims=True))


def head_forward(count, order, rows, table):
    height, columns = rows.shape[0], table.shape[1]
    granules = height // GRANULE
    chunk = min(CHUNK // 2, columns // 2)
    whole = pl.Buffered(1)

    def once(i, count_ref, list_ref):
        return (0, 0)

    return pl.pallas_call(
        head_kernel,
        grid_spec=pltpu.PrefetchScalarGridSpec(
            num_scalar_prefetch=2,
            grid=(height // BLOCK,),
            in_specs=[
                pl.BlockSpec(rows.shape, once, pipeline_mode=whole),
                pl.BlockSpec(table.shape, once, pipeline_mode=whole),
            ],
            out_specs=[
                pl.BlockSpec((BLOCK, columns), block_at),
                pl.BlockSpec((height, MODEL_WIDTH), once, pipeline_mode=whole),
                pl.BlockSpec((granules, 128), once),
                pl.BlockSpec((granules, 128), once),
            ],
            scratch_shapes=[
                pltpu.VMEM((BLOCK, MODEL_WIDTH), BF16),
                pltpu.VMEM((BLOCK, chunk), F32),
                pltpu.VMEM((BLOCK, chunk), F32),
            ],
        ),
        out_shape=[
            jax.ShapeDtypeStruct((height, columns), BF16),
            jax.ShapeDtypeStruct((height, MODEL_WIDTH), F32),
            jax.ShapeDtypeStruct((granules, 128), F32),
            jax.ShapeDtypeStruct((granules, 128), F32),
        ],
        compiler_params=pltpu.CompilerParams(vmem_limit_bytes=VMEM_LIMIT),
        cost_estimate=pl.CostEstimate(
            flops=4 * height * table.size,
            bytes_accessed=2 * height * columns,
            transcendentals=height * columns,
        ),
        name="head_forward",
    )(count, order, rows, table)


def scale_kernel(
    count_ref, list_ref, rows_ref, back_ref, scale_ref, grad_ref, turned_ref, scaled, packed
):
    per = BLOCK // GRANULE
    step, blocks = pl.program_id(0), pl.num_programs(0) // 2

    @pl.when(step < blocks)
    def _():
        for k in range(BLOCK // LANES):
            at = slice(k * LANES, (k + 1) * LANES)
            line = scale_ref[pl.ds(step * (BLOCK // LANES) + k, 1), :]
            column = jnp.transpose(jnp.broadcast_to(line, (LANES, LANES)))[:, :1]
            grad_ref[at, :] = back_ref[at, :] * column
            row = pl.multiple_of(step * BLOCK + k * LANES, LANES)
            scaled[pl.ds(row, LANES), :] = (rows_ref[at, :].astype(F32) * column).astype(BF16)

    block = step - blocks

    @pl.when((block >= 0) & (block < block_count(count_ref)))
    def _():
        for g in range(per):
            at = block * per + g
            spot = pl.multiple_of(list_ref[at] * GRANULE, GRANULE)
            part = scaled[pl.ds(spot, GRANULE), :].astype(F32)
            packed[g * GRANULE : (g + 1) * GRANULE, :] = jnp.where(
                at < count_ref[0], part, jnp.zeros_like(part)
            )
        turned_ref[...] = jnp.transpose(packed[...]).astype(BF16)


def scale_rows(count, order, rows, back, scale):
    height = rows.shape[0]
    blocks = height // BLOCK

    def first(i, count_ref, list_ref):
        return (jnp.minimum(i, blocks - 1), 0)

    def second(i, count_ref, list_ref):
        return (0, block_at(jnp.maximum(i - blocks, 0), count_ref, list_ref)[0])

    return pl.pallas_call(
        scale_kernel,
        grid_spec=pltpu.PrefetchScalarGridSpec(
            num_scalar_prefetch=2,
            grid=(2 * blocks,),
            in_specs=[
                pl.BlockSpec((BLOCK, MODEL_WIDTH), first),
                pl.BlockSpec((BLOCK, MODEL_WIDTH), first),
                pl.BlockSpec(scale.shape, lambda i, count_ref, list_ref: (0, 0)),
            ],
            out_specs=[
                pl.BlockSpec((BLOCK, MODEL_WIDTH), first),
                pl.BlockSpec((MODEL_WIDTH, BLOCK), second),
            ],
            scratch_shapes=[
                pltpu.VMEM((height, MODEL_WIDTH), BF16),
                pltpu.VMEM((BLOCK, MODEL_WIDTH), F32),
            ],
        ),
        out_shape=[
            jax.ShapeDtypeStruct((height, MODEL_WIDTH), F32),
            jax.ShapeDtypeStruct((MODEL_WIDTH, height), BF16),
        ],
        compiler_params=pltpu.CompilerParams(vmem_limit_bytes=VMEM_LIMIT),
        cost_estimate=pl.CostEstimate(flops=0, bytes_accessed=12 * rows.size, transcendentals=0),
        name="scale_rows",
    )(count, order, rows, back, scale)


def table_kernel(count_ref, turned_ref, exp_ref, out_ref):
    used = block_count(count_ref)

    @pl.when(used == 0)
    def _():
        out_ref[...] = jnp.zeros(out_ref.shape, BF16)

    for blocks in range(1, exp_ref.shape[0] // BLOCK + 1):

        @pl.when(used == blocks)
        def _():
            out_ref[...] = jnp.dot(
                turned_ref[:, : blocks * BLOCK],
                exp_ref[: blocks * BLOCK, :],
                preferred_element_type=F32,
            ).astype(BF16)


def table_backward(count, turned, powers, part, parts):
    height, columns = powers.shape[0], powers.shape[1] // parts
    chunk = 512 if columns % 512 == 0 else 256
    steps = columns // chunk
    return pl.pallas_call(
        table_kernel,
        grid_spec=pltpu.PrefetchScalarGridSpec(
            num_scalar_prefetch=1,
            grid=(steps,),
            in_specs=[
                pl.BlockSpec(
                    turned.shape, lambda i, count_ref: (0, 0), pipeline_mode=pl.Buffered(1)
                ),
                pl.BlockSpec((height, chunk), lambda i, count_ref: (0, part * steps + i)),
            ],
            out_specs=pl.BlockSpec((MODEL_WIDTH, chunk), lambda i, count_ref: (0, i)),
        ),
        out_shape=jax.ShapeDtypeStruct((MODEL_WIDTH, columns), BF16),
        compiler_params=pltpu.CompilerParams(vmem_limit_bytes=VMEM_LIMIT),
        cost_estimate=pl.CostEstimate(
            flops=2 * MODEL_WIDTH * powers.size // parts,
            bytes_accessed=2 * powers.size // parts,
            transcendentals=0,
        ),
        name="table_backward",
    )(count, turned, powers)


def shards(
    token_ids,
    lengths,
    deal_order,
    embed_table,
    table_mom,
    table_avg,
    model_flat,
    model_mom,
    model_avg,
):
    dp_size, shard_size = lax.axis_size("dp"), lax.axis_size("shard")
    shard_idx, dp_idx = lax.axis_index("shard"), lax.axis_index("dp")
    device_idx = lax.axis_index(("dp", "shard"))
    core = dp_bit(1)
    seqs = token_ids.shape[0]
    own_rows = seqs * LEN
    group = 2 * shard_size
    groups = dp_size // 2
    slots = group * seqs
    seq_total = groups * slots
    target_count = jnp.float32((MEAN_LENGTH - 1) * seq_total)
    features, columns = embed_table.shape
    half = columns // 2
    vocab_start = shard_idx * columns + core * half
    length = model_flat.shape[0]

    tiny = jnp.concatenate([token_ids, jnp.broadcast_to(lengths[:, None], (seqs, LEN))], 0)
    tiny = tiny.reshape((1,) * (len(bits_below(dp_size)) + len(bits_below(shard_size))) + tiny.shape)
    for k, bit in enumerate(bits_below(dp_size)[::-1]):
        tiny = join(tiny, flip_dp(tiny, bit), bit, k)
    for k, bit in enumerate(bits_below(shard_size)[::-1]):
        other = flip_shard(tiny, bit)
        axis = len(bits_below(dp_size)) + k
        tiny = jnp.where(
            (shard_idx // bit) % 2 == 0,
            jnp.concatenate([tiny, other], axis),
            jnp.concatenate([other, tiny], axis),
        )
    tiny = tiny.reshape(dp_size * shard_size, 2 * seqs, LEN)
    all_ids = tiny[:, :seqs].reshape(seq_total, LEN)
    all_lens = tiny[:, seqs:, 0].reshape(seq_total)
    here = jnp.arange(seq_total)
    longer = all_lens[None, :] > all_lens[:, None]
    equal = (all_lens[None, :] == all_lens[:, None]) & (here[None, :] < here[:, None])
    rank = jnp.sum((longer | equal).astype(jnp.int32), axis=1)
    turn, seat = rank // groups, rank % groups
    group_of = jnp.where(turn % 2 == 0, seat, groups - 1 - seat)
    place_of = group_of * slots + turn
    hits = (place_of[None, :] == here[:, None]).astype(jnp.int32)
    seq_at = jnp.sum(hits * here[None, :], axis=1)
    dealt_ids = all_ids[seq_at]
    dealt_lens = jnp.sum(hits * all_lens[None, :], axis=1)
    my_group = dp_idx // 2
    group_ids = lax.dynamic_slice_in_dim(dealt_ids, my_group * slots, slots, 0)
    group_lens = lax.dynamic_slice_in_dim(dealt_lens, my_group * slots, slots, 0)
    own_at = core * shard_size + shard_idx
    own_lens = lax.dynamic_slice_in_dim(group_lens, own_at * seqs, seqs, 0)
    own_seqs = lax.dynamic_slice_in_dim(seq_at, (my_group * group + own_at) * seqs, seqs, 0)

    places = jnp.arange(LEN)
    weight_one = (places[None, :] + 1 < group_lens[:, None]).astype(F32)
    weight_two = SECOND_WEIGHT * (places[None, :] + 2 < group_lens[:, None]).astype(F32)
    weights = jnp.stack([weight_one, weight_two]) / target_count

    per_seq = LEN // GRANULE
    starts = jnp.arange(per_seq) * GRANULE
    useful = jnp.stack([starts[None, :] + k + 1 < group_lens[:, None] for k in range(2)])
    useful = useful.reshape(-1)
    index = jnp.arange(useful.shape[0])
    before = jnp.sum((useful[None, :] & (index[None, :] < index[:, None])).astype(jnp.int32), axis=1)
    count = jnp.sum(useful.astype(jnp.int32))
    last = jnp.max(jnp.where(useful, index, 0))
    found = useful[None, :] & (before[None, :] == index[:, None])
    order = jnp.sum(jnp.where(found, index[None, :], 0), axis=1)
    order = jnp.where(index < count, order, last).astype(jnp.int32)
    count = count.reshape(1)

    everything = lax.all_gather(own_blocks(model_flat), ("dp", "shard"))

    tokens = seq_total * LEN
    bits = token_bits(tokens)
    kept_ids = jnp.where(places[None, :] < dealt_lens[:, None], dealt_ids, columns * shard_size)
    keys = jnp.sort(kept_ids.reshape(-1) * tokens + jnp.arange(tokens, dtype=jnp.int32))
    first_id = shard_idx * columns
    span = jnp.stack(
        [
            jnp.sum((keys < first_id * tokens).astype(jnp.int32)),
            jnp.sum(((keys >> bits) < first_id + columns).astype(jnp.int32)),
            first_id,
        ]
    ).astype(jnp.int32)
    devices = dp_size * shard_size
    picked = embed_rows(keys, span, embed_table, devices)
    picked = picked.reshape(dp_size, shard_size, features, own_rows)
    mine = ring_reduce(picked.transpose(1, 0, 2, 3)).astype(BF16)
    parts = [pick(mine, dp_idx, 0)]
    parts += [flip_dp(pick(mine, dp_idx ^ k, 0), k) for k in range(1, dp_size)]
    embedded = jnp.stack(parts)[jnp.arange(dp_size) ^ dp_idx]
    embedded = embedded.reshape(MODEL_WIDTH, own_rows).T.astype(F32)

    held_table, everything = lax.optimization_barrier((embed_table, everything))
    table_gather = TableGather(held_table)
    middle_rows = PL // 128
    low_rows = middle_rows // 16 * 16
    total_devices = dp_size * shard_size
    per = GRAIN // 128
    end_row = block_starts(length, total_devices)[-1] * per
    tail = 2 * MODEL_WIDTH // 128
    square = MODEL_WIDTH * MODEL_WIDTH // 128
    *layer_zero, gains_zero = unpack_rows(
        everything, length, 0, low_rows + 16, LAYER_SHAPES, {}, 0, ((middle_rows - tail, 16),)
    )
    gain_row = middle_rows - low_rows + middle_rows - tail
    second_row = gain_row + tail + square
    base_one = gain_row // 16 * 16
    base_two = second_row // 16 * 16 - 16
    *layer_one, w_second, gains_one, gains_head = unpack_rows(
        everything, length, low_rows, end_row, LAYER_SHAPES + SQUARE, {3: tail},
        middle_rows - low_rows, ((base_one, 32), (base_two, 32)),
    )

    def gain_pair(rows, at):
        return rows[at : at + tail].reshape(2, MODEL_WIDTH)

    layer_zero.append(gain_pair(gains_zero, 0).astype(F32))
    layer_one.append(gain_pair(gains_one, gain_row - base_one).astype(F32))
    head_gains = gain_pair(gains_head, second_row - base_two).astype(F32)

    rope = rope_rows(own_rows)
    hidden, kept_zero = layer_forward(embedded, layer_zero, own_lens, rope)
    hidden = table_gather.tied(hidden)
    table_gather.step()
    hidden, kept_one = layer_forward(hidden, layer_one, own_lens, rope)
    scale_final = rms_scale(hidden)
    head_one = (hidden * scale_final * head_gains[0]).astype(BF16)
    all_one = group_gather(head_one, table_gather.tied).reshape(-1, MODEL_WIDTH)
    table_low = table_gather.finish()
    projected = jnp.dot(all_one, w_second, preferred_element_type=F32)
    scale_second = rms_scale(projected)
    all_two = (projected * scale_second * head_gains[1]).astype(BF16)
    both = jnp.concatenate([all_one, all_two], 0)
    group_rows = all_one.shape[0]

    powers, back, sums, peaks = head_forward(count, order, both, table_low)
    sums = sums[:, :GRANULE].reshape(-1, 128)
    peaks = peaks[:, :GRANULE].reshape(-1, 128)
    sum_all_rows, peak_all = sums, peaks
    for flip, bits in ((flip_shard, bits_below(shard_size)), (flip_dp, [1])):
        for bit in bits:
            stats = flip(jnp.stack([sum_all_rows, peak_all]), bit)
            top = jnp.maximum(peak_all, stats[1])
            sum_all_rows = sum_all_rows * jnp.exp(peak_all - top) + stats[0] * jnp.exp(
                stats[1] - top
            )
            peak_all = top
    log_total = (peak_all + jnp.log(sum_all_rows)).reshape(2, group, seqs, LEN)
    row_scale = weights.reshape(-1, 128) * jnp.exp(peaks - peak_all) / sum_all_rows
    grad_rows, turned_rows = scale_rows(count, order, both, back, row_scale)

    own_log = pick(log_total, own_at, 1)
    own_weights = pick(weights.reshape(2, group, seqs, LEN), own_at, 1)
    words = embedded.reshape(seqs, LEN, MODEL_WIDTH)
    next_one = jnp.roll(words, -1, 1).reshape(own_rows, MODEL_WIDTH)
    next_two = jnp.roll(words, -2, 1).reshape(own_rows, MODEL_WIDTH)
    head_two = lax.dynamic_slice_in_dim(all_two, own_at * own_rows, own_rows, 0)
    chosen_one = jnp.sum(head_one.astype(F32) * next_one, axis=-1)
    chosen_two = jnp.sum(head_two.astype(F32) * next_two, axis=-1)
    chosen = jnp.stack([chosen_one, chosen_two]).reshape(2, seqs, LEN)
    own_loss = jnp.sum(own_weights * (own_log - chosen), axis=(0, 2))

    weight_col = own_weights.reshape(2, own_rows, 1)
    part_two = grad_rows[group_rows:]
    own_two = lax.dynamic_slice_in_dim(part_two, own_at * own_rows, own_rows, 0)
    part_two = lax.dynamic_update_slice_in_dim(
        part_two, own_two - weight_col[1] * next_two, own_at * own_rows, 0
    )
    grad_proj, grad_gain_second = rms_back(projected, scale_second, head_gains[1], part_two)
    grad_proj_low = grad_proj.astype(BF16)
    part_one = grad_rows[:group_rows] + times_t(grad_proj_low, w_second)
    quarters = 4
    cubes = [None] * quarters
    running = [turned_rows]

    def quarter_hook(k):
        def hook(got):
            part = table_backward(count, running[0], powers, k, quarters)
            got, part, running[0] = lax.optimization_barrier((got, part, running[0]))
            bits = high_bits() if k < quarters // 2 else high_bits()[::-1]
            cubes[k] = Cube(part.reshape(-1, 2 * features, part.shape[1]), bits)
            return got

        return hook

    grad_final = group_reduce(
        part_one.reshape(2, shard_size, own_rows, MODEL_WIDTH),
        [quarter_hook(k) for k in (0, 2, 1, 3)],
    )
    grad_final = grad_final - weight_col[0] * next_one
    grad_hidden, grad_gain_final = rms_back(hidden, scale_final, head_gains[0], grad_final)

    sub_rows = owner_sub_rows(length)
    height_zero = length * (total_devices // 2 - 1) // GRAIN * per + 2 * sub_rows
    height_one = length * (total_devices - 1) // GRAIN * per + 2 * sub_rows - low_rows
    keep = height_zero - low_rows
    grad_hidden = tie(grad_hidden, [cubes[0], cubes[2]])
    cubes[0].step(), cubes[2].step()
    grad_hidden, pairs, gain_grads = layer_backward(
        kept_one, layer_one, own_lens, rope, grad_hidden
    )
    gain_grads = tie(gain_grads, [cubes[1], cubes[3]])
    cubes[1].step(), cubes[3].step()
    own_one, send_one, kept_rows = pack_half(
        owner_rows(length, 1, low_rows),
        pairs + [(all_one, grad_proj_low)],
        [gain_grads, flat_rows(grad_gain_final, grad_gain_second)],
        None, middle_rows - low_rows, {3: tail, 4: tail}, height_one, sub_rows, keep, 0,
    )
    got_one = flip_dp(send_one, 1)
    grad_hidden, own_one = lax.optimization_barrier((grad_hidden, own_one))
    grad_hidden, pairs, gain_grads = layer_backward(
        kept_zero, layer_zero, own_lens, rope, grad_hidden
    )
    gain_grads, got_one = lax.optimization_barrier((gain_grads, got_one))
    gain_grads = tie(gain_grads, cubes)
    joined = jnp.concatenate([cube.finish() for cube in cubes], 1)
    flipped = owner_flip(joined, features)
    cubes_one = half_cubes(own_one, got_one)
    own_zero, send_zero = pack_half(
        owner_rows(length, 0, 0), pairs, [gain_grads],
        (kept_rows, height_zero - middle_rows), 0, {3: tail}, height_zero, sub_rows, 0,
        middle_rows - low_rows,
    )
    one_terms = (weight_col[0] * head_one.astype(F32)).reshape(seqs, LEN, MODEL_WIDTH)
    two_terms = (weight_col[1] * head_two.astype(F32)).reshape(seqs, LEN, MODEL_WIDTH)
    token_grad = (
        grad_hidden.astype(BF16).astype(F32)
        - jnp.roll(one_terms, 1, 1).reshape(own_rows, MODEL_WIDTH)
        - jnp.roll(two_terms, 2, 1).reshape(own_rows, MODEL_WIDTH)
    ).astype(BF16)
    token_parts = token_grad.T.reshape(dp_size, features, own_rows)
    parts = [pick(token_parts, dp_idx, 0)]
    parts += [flip_dp(pick(token_parts, dp_idx ^ k, 0), k) for k in range(1, dp_size)]
    got_zero, parts, flipped = lax.optimization_barrier((flip_dp(send_zero, 1), parts, flipped))
    table_part = owner_join(joined, flipped, features)
    cubes_zero = half_cubes(own_zero, got_zero)
    chain = [jnp.stack(parts)]
    chain[0] = tie(chain[0], cubes_one)
    for cube in cubes_one:
        cube.step()
    chain.append(next_shard(chain[0]))
    chain[1] = tie(chain[1], cubes_one)
    sums_one = jnp.concatenate([cube.finish() for cube in cubes_one], 0).astype(BF16)
    sums_one = tie(sums_one, cubes_zero)
    for cube in cubes_zero:
        cube.step()
    done_one = ring_reduce(sums_one)
    done_one = tie(done_one, cubes_zero)
    for _ in range(shard_size - 2):
        chain.append(next_shard(chain[-1]))
    done_zero, top_zero = to_top(finish_cubes(cubes_zero), 0)
    done_one, top_one = to_top(done_one, 1)
    model_sum = own_part(((done_zero, top_zero), (done_one, top_one)), length)
    chain[-1], done_zero = lax.optimization_barrier((chain[-1], done_zero))
    from_dp = (jnp.arange(dp_size) ^ dp_idx)[None, :]
    from_shard = (shard_idx - jnp.arange(shard_size))[:, None] % shard_size
    spots = (from_dp * shard_size + from_shard).reshape(-1).astype(jnp.int32)
    table_sum = spread_rows(keys, span, spots, chain, table_part)

    square_sum = sum_all(
        (jnp.sum(table_sum * table_sum) + jnp.sum(model_sum * model_sum)).reshape(1, 1)
    )[0, 0]
    grad_norm = jnp.sqrt(square_sum)
    factor = jnp.minimum(1.0, CLIP_NORM / (grad_norm + 1e-06))

    spots = jnp.sum(
        jnp.where(own_seqs[:, None] == here[None, :], own_loss[:, None], 0.0), axis=0
    )[None]
    all_loss = sum_all(spots)[0]
    loss_total = jnp.sum(all_loss)
    seq_loss = lax.dynamic_slice_in_dim(all_loss, device_idx * seqs, seqs, 0)
    own_slots = lax.dynamic_slice_in_dim(deal_order, device_idx * seqs, seqs, 0)
    slot_loss = all_loss[own_slots]

    results = []
    for weights_in, gradient, moment, average in (
        (embed_table, table_sum, table_mom, table_avg),
        (model_flat, model_sum, model_mom, model_avg),
    ):
        clipped = gradient * factor
        new_moment = MOMENTUM * moment + clipped
        new_weight = weights_in - LEARN_RATE * (clipped + MOMENTUM * new_moment)
        new_average = AVERAGE_KEEP * average + (1.0 - AVERAGE_KEEP) * new_weight
        results.append(
            (clipped, new_weight, new_moment, new_average, new_weight.astype(BF16))
        )
    return (loss_total, seq_loss, slot_loss, grad_norm) + results[0] + results[1]


def solution(mesh):
    both = P(("dp", "shard"))
    block = P("dp", "shard")
    return jax.shard_map(
        shards,
        mesh=mesh,
        in_specs=(P(("dp", "shard"), None), both, P(), block, block, block, both, both, both),
        out_specs=(P(), both, both, P()) + (block,) * 5 + (both,) * 5,
        check_vma=False,
    )
```

```python
import jax
import jax.numpy as jnp
from jax import lax
from jax.experimental import pallas as pl
from jax.experimental.pallas import tpu as pltpu
from jax.sharding import PartitionSpec as P

MODEL_WIDTH = 576
QUERY_HEADS = 9
KEY_VALUE_HEADS = 3
HEAD_SIZE = 64
FEED_UNITS = 1536
LAYERS = 2
LEN = 128
PL = 3540096
NP = 7413120
QKV = (QUERY_HEADS + 2 * KEY_VALUE_HEADS) * HEAD_SIZE
ROPED = (QUERY_HEADS + KEY_VALUE_HEADS) * HEAD_SIZE
MEAN_LENGTH = 96

EPSILON = 1e-05
ROPE_BASE = 100000.0
CLIP_NORM = 0.01
LEARN_RATE = 6000.0
MOMENTUM = 0.9
AVERAGE_KEEP = 0.9
SECOND_WEIGHT = 0.3
MASKED_SCORE = -1e30

GRAIN = 2048
GRANULE = 16
BLOCK = 512
CHUNK = 1024
LANES = 128
COLUMNS = 256
VMEM_LIMIT = 62 * 1024 * 1024
F32 = jnp.float32
BF16 = jnp.bfloat16


def flip_dp(values, bit):
    return lax.ppermute(values, "dp", [(i, i ^ bit) for i in range(lax.axis_size("dp"))])


def flip_shard(values, bit):
    return lax.ppermute(values, "shard", [(i, i ^ bit) for i in range(lax.axis_size("shard"))])


def next_shard(values):
    size = lax.axis_size("shard")
    return lax.ppermute(values, "shard", [(i, (i + 1) % size) for i in range(size)])


def bits_below(size):
    return [1 << k for k in range(size.bit_length() - 1)]


def dp_bit(bit):
    return (lax.axis_index("dp") // bit) % 2


def join(own, other, bit, axis):
    return jnp.where(
        dp_bit(bit) == 0,
        jnp.concatenate([own, other], axis),
        jnp.concatenate([other, own], axis),
    )


def pick(values, idx, axis):
    return lax.dynamic_index_in_dim(values, idx, axis, keepdims=False)


def high_bits():
    return bits_below(lax.axis_size("dp"))[1:]


def gather_cube(values, order):
    bits = sorted(order, reverse=True)
    out = values.reshape((1,) * len(bits) + values.shape)
    for bit in order:
        out = join(out, flip_dp(out, bit), bit, bits.index(bit))
    return out.reshape((-1,) + values.shape)


class Cube:
    def __init__(self, values, order):
        self.left = sorted(order, reverse=True)
        self.order = list(order)
        self.out = values.reshape((2,) * len(order) + values.shape[1:])
        self.start()

    def start(self):
        bit = self.order[0]
        axis = self.left.index(bit)
        mine = dp_bit(bit)
        self.got = flip_dp(pick(self.out, 1 - mine, axis).astype(BF16), bit)
        self.keep = pick(self.out, mine, axis)

    def step(self):
        self.out = self.keep.astype(F32) + self.got.astype(F32)
        self.left.remove(self.order.pop(0))
        if self.order:
            self.start()
        return bool(self.order)

    def finish(self):
        while self.order:
            self.step()
        return self.out


def tie(main, cubes):
    main, gots = lax.optimization_barrier((main, [cube.got for cube in cubes]))
    for cube, got in zip(cubes, gots):
        cube.got = got
    return main


def ring_gather(values, hook=None):
    size = lax.axis_size("shard")
    me = lax.axis_index("shard")
    parts = [values]
    for k in range(size - 1):
        parts.append(next_shard(parts[-1]))
        if hook is not None and k == 1:
            parts[-1] = hook(parts[-1])
    stacked = jnp.stack(parts[::-1])
    return jnp.roll(stacked, me + 1, axis=0)


def ring_reduce(values, hooks=()):
    size = lax.axis_size("shard")
    me = lax.axis_index("shard")
    total = None
    for step in range(size - 1):
        term = pick(values, (me - 1 - step) % size, 0).astype(F32)
        if total is not None:
            term = term + total
        got = next_shard(term.astype(BF16))
        if step < len(hooks):
            got = hooks[step](got)
        total = got.astype(F32)
    return total + pick(values, me, 0).astype(F32)


def group_gather(rows, hook=None):
    parts = ring_gather(rows, hook)
    other = flip_dp(parts, 1)
    return join(parts[None], other[None], 1, 0)


def group_reduce(parts, hooks):
    mine = dp_bit(1)
    got = hooks[0](flip_dp(pick(parts, 1 - mine, 0).astype(BF16), 1))
    return ring_reduce(pick(parts, mine, 0).astype(F32) + got.astype(F32), hooks[1:])


def sum_all(value):
    total = value
    for bit in bits_below(lax.axis_size("dp")):
        total = total + flip_dp(total, bit)
    for bit in bits_below(lax.axis_size("shard")):
        total = total + flip_shard(total, bit)
    return total


def top_bit():
    return high_bits()[-1]


def block_starts(length, total):
    return [length * i // GRAIN for i in range(total)] + [-(-length * total // GRAIN)]


def own_blocks(model_flat):
    length = model_flat.shape[0]
    total = lax.axis_size("dp") * lax.axis_size("shard")
    device = lax.axis_index(("dp", "shard"))
    low = model_flat.astype(BF16)
    before = lax.ppermute(
        low[length - GRAIN :], ("dp", "shard"), [(i, i + 1) for i in range(total - 1)]
    )
    starts = block_starts(length, total)
    blocks = max(starts[i + 1] - starts[i] for i in range(total))
    extended = jnp.concatenate([before, low, jnp.zeros((3 * GRAIN,), BF16)])
    shift = (length * device) % GRAIN
    whole = lax.dynamic_slice_in_dim(extended, GRAIN - shift, blocks * GRAIN, 0)
    return whole.reshape(-1, 128)


LAYER_SHAPES = (
    (MODEL_WIDTH, QKV),
    (MODEL_WIDTH, MODEL_WIDTH),
    (MODEL_WIDTH, 2 * FEED_UNITS),
    (FEED_UNITS, MODEL_WIDTH),
)
SQUARE = ((MODEL_WIDTH, MODEL_WIDTH),)
TALL = 64


def line_up(flat_at, out, height, breadth):
    tiles, odd = breadth // 128, breadth % 128
    if not odd:
        for j in range(tiles):
            out(0, j, flat_at(j, height, tiles))
        return
    period = 2 * tiles + 1
    loads = [flat_at(j, height // 2, period) for j in range(period)]
    for j in range(tiles + 1):
        out(0, j, loads[j])
        after = loads[min(tiles + j + 1, period - 1)]
        out(1, j, jnp.concatenate([loads[tiles + j][:, 64:], after[:, :64]], 1))


def unpack_matrix(flat_ref, at, out_ref, wide_ref, tall_ref):
    height, breadth = out_ref.shape
    rows = TALL * breadth // 128
    shift = at % 16
    load = rows + (16 if shift else 0)

    @pl.loop(0, height // TALL)
    def _(k):
        first = pl.multiple_of(k * rows + (at - shift), 16)
        wide_ref[:load, :] = flat_ref[pl.ds(first, load), :].astype(F32)
        out_at = pl.multiple_of(k * TALL, TALL)

        def flat_at(j, count, stride):
            return wide_ref[pl.ds(shift + j, count, stride=stride), :]

        if breadth % 128:
            def put(parity, j, values):
                tall_ref[j, pl.ds(parity, TALL // 2, stride=2), :] = values

            line_up(flat_at, put, TALL, breadth)
            for j in range(breadth // 128 + 1):
                stop = min((j + 1) * 128, breadth)
                out_ref[pl.ds(out_at, TALL), j * 128 : stop] = tall_ref[
                    j, :, : stop - j * 128
                ].astype(BF16)
        else:
            def put(_, j, values):
                out_ref[pl.ds(out_at, TALL), j * 128 : (j + 1) * 128] = values.astype(BF16)

            line_up(flat_at, put, TALL, breadth)


def unpack_rows(everything, length, first_row, last_row, shapes, gaps, lead, tails):
    total = lax.axis_size("dp") * lax.axis_size("shard")
    starts = block_starts(length, total)
    per = GRAIN // 128
    moves = []
    for owner in range(total):
        low = max(starts[owner] * per, first_row)
        high = min(starts[owner + 1] * per, last_row)
        if low < high:
            moves.append((owner, low - starts[owner] * per, low - first_row, high - low))
    outs = [jax.ShapeDtypeStruct(shape, BF16) for shape in shapes]
    outs += [jax.ShapeDtypeStruct((rows, 128), BF16) for _, rows in tails]
    wide_rows = TALL * max(shape[1] for shape in shapes) // 128 + 16
    height = last_row - first_row

    def kernel(all_ref, *refs):
        outs, (flat_ref, wide_ref, tall_ref, sems) = refs[:-4], refs[-4:]
        copies = [
            pltpu.make_async_copy(
                all_ref.at[owner, pl.ds(source, rows)], flat_ref.at[pl.ds(at, rows)], sems.at[k]
            )
            for k, (owner, source, at, rows) in enumerate(moves)
        ]
        for copy in copies:
            copy.start()
        arrived = 0
        at = lead
        for k, (tall, wide) in enumerate(shapes):
            end = at + tall * wide // 128
            while arrived < len(moves) and moves[arrived][2] < end:
                copies[arrived].wait()
                arrived += 1
            unpack_matrix(flat_ref, at, outs[k], wide_ref, tall_ref)
            at = end + gaps.get(k, 0)
        for copy in copies[arrived:]:
            copy.wait()
        for k, (start, rows) in enumerate(tails):
            outs[len(shapes) + k][...] = flat_ref[pl.ds(start, rows), :]

    return pl.pallas_call(
        kernel,
        in_specs=[pl.BlockSpec(memory_space=pl.ANY)],
        out_specs=[pl.BlockSpec(memory_space=pltpu.VMEM)] * len(outs),
        out_shape=outs,
        scratch_shapes=[
            pltpu.VMEM((height, 128), BF16),
            pltpu.VMEM((wide_rows, 128), F32),
            pltpu.VMEM((8, TALL, 128), F32),
            pltpu.SemaphoreType.DMA((len(moves),)),
        ],
        compiler_params=pltpu.CompilerParams(vmem_limit_bytes=VMEM_LIMIT),
        cost_estimate=pl.CostEstimate(flops=0, bytes_accessed=512 * height, transcendentals=0),
        name="unpack_rows",
    )(everything)


def pack_matrix(left_ref, right_ref, flat_ref, at, tall_ref):
    height, breadth = left_ref.shape[1], right_ref.shape[1]
    part = 512 if height % 512 == 0 else height
    tiles, odd = breadth // 128, breadth % 128
    for k in range(height // part):
        first = at + k * part * breadth // 128
        product = against(left_ref[:, k * part : (k + 1) * part], right_ref[...])
        for j in range(tiles + (1 if odd else 0)):
            stop = min((j + 1) * 128, breadth)
            tall_ref[j, :part, : stop - j * 128] = product[:, j * 128 : stop]
        if not odd:
            for j in range(tiles):
                flat_ref[pl.ds(first + j, part, stride=tiles), :] = tall_ref[j, :part, :]
            continue
        period = 2 * tiles + 1
        count = part // 2

        def half(parity, j):
            return tall_ref[j, pl.ds(parity, count, stride=2), :]

        for j in range(tiles):
            flat_ref[pl.ds(first + j, count, stride=period), :] = half(0, j)
        flat_ref[pl.ds(first + tiles, count, stride=period), :] = jnp.concatenate(
            [half(0, tiles)[:, :64], half(1, 0)[:, :64]], 1
        )
        for j in range(tiles):
            flat_ref[pl.ds(first + tiles + 1 + j, count, stride=period), :] = jnp.concatenate(
                [half(1, j)[:, 64:], half(1, j + 1)[:, :64]], 1
            )


def pack_kernel(info_ref, *refs, pairs, loose, early, lead, gaps, count, sub_rows, keep, first_loose):
    lefts, rights, refs = refs[:pairs], refs[pairs : 2 * pairs], refs[2 * pairs :]
    loose_refs, refs = refs[:loose], refs[loose:]
    if early:
        early_ref, refs = refs[0], refs[1:]
    own_ref, send_ref, refs = refs[0], refs[1], refs[2:]
    if keep:
        keep_ref, refs = refs[0], refs[1:]
    flat_ref, low_ref, tall_ref, sems = refs
    height = flat_ref.shape[0]
    at = lead
    for k in range(pairs):
        pack_matrix(lefts[k], rights[k], flat_ref, at, tall_ref)
        at += lefts[k].shape[1] * rights[k].shape[1] // 128
        if k in gaps:
            flat_ref[at : at + gaps[k], :] = loose_refs[list(gaps).index(k)][...]
            at += gaps[k]
    if early:
        flat_ref[at : at + early, :] = early_ref[...].astype(F32)[first_loose : first_loose + early]
        at += early
    if at < height:
        flat_ref[at:height, :] = jnp.zeros((height - at, 128), F32)
    step = 16 * 32
    for row in range(0, height, step):
        rows = min(step, height - row)
        low_ref[row : row + rows, :] = flat_ref[row : row + rows, :].astype(BF16)
    copies = []
    for idx in range(count):
        for k, ref in enumerate((own_ref, send_ref)):
            row = pl.multiple_of(info_ref[k * count + idx], 16)
            copies.append(
                pltpu.make_async_copy(
                    low_ref.at[pl.ds(row, sub_rows)], ref.at[idx], sems.at[k * count + idx]
                )
            )
    for copy in copies:
        copy.start()
    if keep:
        keep_ref[...] = low_ref[:keep, :]
    for copy in copies:
        copy.wait()


def pack_half(info, pairs, loose, early, lead, gaps, height, sub_rows, keep, skip):
    count = info.shape[0] // 2
    lefts = [left for left, _ in pairs]
    rights = [right for _, right in pairs]
    in_place = pl.BlockSpec(memory_space=pltpu.VMEM)
    anywhere = pl.BlockSpec(memory_space=pl.ANY)
    operands = lefts + rights + loose + ([early[0]] if early is not None else [])
    outs = [jax.ShapeDtypeStruct((count, sub_rows, 128), BF16)] * 2
    specs = [anywhere] * 2
    if keep:
        outs.append(jax.ShapeDtypeStruct((keep, 128), BF16))
        specs.append(in_place)

    def kernel(info_ref, *refs):
        pack_kernel(
            info_ref, *refs, pairs=len(pairs), loose=len(loose),
            early=0 if early is None else early[1], lead=lead, gaps=gaps,
            count=count, sub_rows=sub_rows, keep=keep, first_loose=skip,
        )

    return pl.pallas_call(
        kernel,
        in_specs=[pl.BlockSpec(memory_space=pltpu.SMEM)] + [in_place] * len(operands),
        out_specs=specs,
        out_shape=outs,
        scratch_shapes=[
            pltpu.VMEM((height, 128), F32),
            pltpu.VMEM((height, 128), BF16),
            pltpu.VMEM((max(right.shape[1] for right in rights) // 128, MODEL_WIDTH, 128), F32),
            pltpu.SemaphoreType.DMA((2 * count,)),
        ],
        compiler_params=pltpu.CompilerParams(vmem_limit_bytes=VMEM_LIMIT),
        cost_estimate=pl.CostEstimate(
            flops=0, bytes_accessed=32 * height, transcendentals=0
        ),
        name="pack_half",
    )(info, *operands)


def owner_rows(length, which, first_row):
    dp_size, shard_size = lax.axis_size("dp"), lax.axis_size("shard")
    sub_rows = owner_sub_rows(length)
    per = GRAIN // 128
    j = jnp.arange(2)[:, None, None]
    x = jnp.arange(dp_size // 4)[None, :, None]
    z = jnp.arange(shard_size)[None, None, :]
    rows = []
    for core in (dp_bit(1), 1 - dp_bit(1)):
        owner = ((which * (dp_size // 4) + x) * 2 + core) * shard_size + z
        rows.append((length * owner // GRAIN * per + sub_rows * j - first_row).reshape(-1))
    return jnp.concatenate(rows).astype(jnp.int32)


def owner_sub_rows(length):
    blocks = -(-(GRAIN - 1 + length) // GRAIN)
    return (blocks + blocks % 2) * (GRAIN // 128) // 2


def half_cubes(own, got):
    shard_size = lax.axis_size("shard")
    paired = (own.astype(F32) + got.astype(F32)).astype(BF16)
    paired = paired.reshape((-1, shard_size) + own.shape[1:])
    half = shard_size // 2
    order = high_bits()
    return [Cube(paired[:, :half], order), Cube(paired[:, half:], order[::-1])]


def own_part(sums_zero, sums_one, length):
    done = ring_reduce(jnp.stack([sums_zero, sums_one], 1).astype(BF16))
    top = dp_bit(top_bit())
    got = flip_dp(pick(done, 1 - top, 0).astype(BF16), top_bit()).astype(F32)
    own = pick(done, top, 0)
    both = jnp.where(top == 0, jnp.concatenate([own, got], 0), jnp.concatenate([got, own], 0))
    shift = (length * lax.axis_index(("dp", "shard"))) % GRAIN
    return lax.dynamic_slice_in_dim(both.reshape(-1), shift, length, 0)


class TableGather:
    def __init__(self, embed_table):
        low = embed_table.astype(BF16)
        half = low.shape[1] // 2
        core = dp_bit(1)
        own = lax.dynamic_slice_in_dim(low, core * half, half, 1)
        send = lax.dynamic_slice_in_dim(low, (1 - core) * half, half, 1)
        pair = join(own, flip_dp(send, 1), 1, 0)
        self.bits = sorted(high_bits(), reverse=True)
        shape = (1,) * len(self.bits) + (pair.shape[0], half // 2)
        self.sides = [pair[:, : half // 2].reshape(shape), pair[:, half // 2 :].reshape(shape)]
        self.orders = [high_bits(), high_bits()[::-1]]
        self.start()

    def start(self):
        self.got = [flip_dp(side, order[0]) for side, order in zip(self.sides, self.orders)]

    def step(self):
        self.sides = [
            join(side, other, order[0], self.bits.index(order[0]))
            for side, other, order in zip(self.sides, self.got, self.orders)
        ]
        self.orders = [order[1:] for order in self.orders]
        if self.orders[0]:
            self.start()

    def tied(self, main):
        main, self.got = lax.optimization_barrier((main, self.got))
        return main

    def finish(self):
        while self.orders[0]:
            self.step()
        return jnp.concatenate([side.reshape(MODEL_WIDTH, -1) for side in self.sides], 1)


def owner_flip(joined, features):
    core = dp_bit(1)
    send = lax.dynamic_slice_in_dim(joined, (1 - core) * features, features, 0)
    return flip_dp(send, 1)


def owner_join(joined, got, features):
    own = lax.dynamic_slice_in_dim(joined, dp_bit(1) * features, features, 0)
    return join(own, got, 1, 1)


def rms_scale(values):
    return lax.rsqrt(jnp.mean(values * values, axis=-1, keepdims=True) + EPSILON)


def rms_back(values, scale, gain, grad):
    weighted = grad * gain
    inner = jnp.sum(weighted * values, axis=-1, keepdims=True)
    grad_values = scale * weighted - values * (scale * scale * scale * inner / MODEL_WIDTH)
    grad_gain = jnp.sum(grad * values * scale, axis=0)
    return grad_values, grad_gain


def rope_rows(rows):
    halves = HEAD_SIZE // 2
    inverse = ROPE_BASE ** (-jnp.arange(halves, dtype=F32) * 2.0 / HEAD_SIZE)
    angles = jnp.arange(LEN, dtype=F32)[:, None] * inverse[None, :]
    cosine, sine = jnp.cos(angles), jnp.sin(angles)
    heads = ROPED // HEAD_SIZE
    cos_full = jnp.tile(jnp.concatenate([cosine, cosine], 1), (rows // LEN, heads))
    sin_full = jnp.tile(jnp.concatenate([-sine, sine], 1), (rows // LEN, heads))
    return cos_full, sin_full


def against(left, right):
    return lax.dot_general(left, right, (((0,), (0,)), ((), ())), preferred_element_type=F32)


def times_t(left, right):
    return lax.dot_general(left, right, (((1,), (1,)), ((), ())), preferred_element_type=F32)


QUERY_WIDTH = QUERY_HEADS * HEAD_SIZE
VALUE_WIDTH = KEY_VALUE_HEADS * HEAD_SIZE
SCALING = HEAD_SIZE ** (-0.5)


def swap_halves(values):
    halves, width = HEAD_SIZE // 2, values.shape[1]
    lanes = lax.broadcasted_iota(jnp.int32, values.shape, 1) % HEAD_SIZE
    return jnp.where(
        lanes < halves, pltpu.roll(values, width - halves, 1), pltpu.roll(values, halves, 1)
    )


def head_cols(idx):
    return slice(idx * HEAD_SIZE, (idx + 1) * HEAD_SIZE)


def attention_probs(query, key, allowed):
    scores = jnp.where(allowed, times_t(query, key) * SCALING, MASKED_SCORE)
    powers = jnp.exp(scores - jnp.max(scores, axis=1, keepdims=True))
    return powers / jnp.sum(powers, axis=1, keepdims=True)


def allowed_pairs(length):
    later = lax.broadcasted_iota(jnp.int32, (LEN, LEN), 0)
    sooner = lax.broadcasted_iota(jnp.int32, (LEN, LEN), 1)
    return (sooner <= later) & (sooner < length)


def forward_kernel(
    len_ref, hidden_ref, qkv_ref, out_ref, gateup_ref, down_ref, gain_ref, cos_ref, sin_ref,
    output_ref, normed_ref, turned_ref, value_ref, attended_ref, middle_ref, normed_two_ref,
    gate_up_ref, acted_ref,
):
    hidden = hidden_ref[...]
    normed_ref[...] = (hidden * rms_scale(hidden) * gain_ref[0:1, :]).astype(BF16)
    qkv = jnp.dot(normed_ref[...], qkv_ref[...], preferred_element_type=F32)
    straight = qkv[:, :ROPED]
    turned_ref[...] = (straight * cos_ref[...] + swap_halves(straight) * sin_ref[...]).astype(BF16)
    value_ref[...] = qkv[:, ROPED:].astype(BF16)
    group = QUERY_HEADS // KEY_VALUE_HEADS
    for seq in range(hidden.shape[0] // LEN):
        rows = slice(seq * LEN, (seq + 1) * LEN)
        allowed = allowed_pairs(len_ref[seq])
        for head in range(QUERY_HEADS):
            key = turned_ref[rows, head_cols(QUERY_HEADS + head // group)]
            value = value_ref[rows, head_cols(head // group)]
            probs = attention_probs(turned_ref[rows, head_cols(head)], key, allowed)
            attended_ref[rows, head_cols(head)] = jnp.dot(
                probs.astype(BF16), value, preferred_element_type=F32
            ).astype(BF16)
    middle = hidden + jnp.dot(attended_ref[...], out_ref[...], preferred_element_type=F32)
    middle_ref[...] = middle
    normed_two_ref[...] = (middle * rms_scale(middle) * gain_ref[1:2, :]).astype(BF16)
    gate_up_ref[...] = jnp.dot(normed_two_ref[...], gateup_ref[...], preferred_element_type=F32)
    gate = gate_up_ref[:, :FEED_UNITS]
    acted_ref[...] = (gate / (1.0 + jnp.exp(-gate)) * gate_up_ref[:, FEED_UNITS:]).astype(BF16)
    output_ref[...] = middle + jnp.dot(acted_ref[...], down_ref[...], preferred_element_type=F32)


def backward_kernel(
    len_ref, grad_ref, hidden_ref, qkv_ref, out_ref, gateup_ref, down_ref, gain_ref, cos_ref,
    sin_ref, turned_ref, value_ref, middle_ref, gate_up_ref,
    grad_in_ref, low_ref, grad_gu_ref, grad_mid_ref, grad_qkv_ref, gains_out_ref,
    grad_att_ref, grad_turned_ref,
):
    grad = grad_ref[...]
    low_ref[...] = grad.astype(BF16)
    grad_act = times_t(low_ref[...], down_ref[...]).astype(BF16).astype(F32)
    gate, up = gate_up_ref[:, :FEED_UNITS], gate_up_ref[:, FEED_UNITS:]
    sigma = 1.0 / (1.0 + jnp.exp(-gate))
    grad_gu_ref[:, FEED_UNITS:] = (grad_act * (gate * sigma)).astype(BF16)
    grad_gu_ref[:, :FEED_UNITS] = (
        grad_act * up * (sigma * (1.0 + gate * (1.0 - sigma)))
    ).astype(BF16)
    middle = middle_ref[...]
    grad_mid, gain_two = rms_back(
        middle, rms_scale(middle), gain_ref[1:2, :], times_t(grad_gu_ref[...], gateup_ref[...])
    )
    grad_mid = grad_mid + grad
    grad_mid_ref[...] = grad_mid.astype(BF16)
    grad_att_ref[...] = times_t(grad_mid_ref[...], out_ref[...]).astype(BF16)
    group = QUERY_HEADS // KEY_VALUE_HEADS
    for seq in range(grad.shape[0] // LEN):
        rows = slice(seq * LEN, (seq + 1) * LEN)
        allowed = allowed_pairs(len_ref[seq])
        for kv in range(KEY_VALUE_HEADS):
            key = turned_ref[rows, head_cols(QUERY_HEADS + kv)]
            value = value_ref[rows, head_cols(kv)]
            grad_key = jnp.zeros((LEN, HEAD_SIZE), F32)
            grad_value = jnp.zeros((LEN, HEAD_SIZE), F32)
            for head in range(kv * group, (kv + 1) * group):
                query = turned_ref[rows, head_cols(head)]
                grad_out = grad_att_ref[rows, head_cols(head)]
                probs = attention_probs(query, key, allowed)
                grad_probs = times_t(grad_out, value)
                grad_value = grad_value + against(probs.astype(BF16), grad_out)
                inner = jnp.sum(grad_probs * probs, axis=1, keepdims=True)
                grad_scores = (probs * (grad_probs - inner)).astype(BF16)
                grad_query = jnp.dot(grad_scores, key, preferred_element_type=F32) * SCALING
                grad_turned_ref[rows, head_cols(head)] = grad_query.astype(BF16).astype(F32)
                grad_key = grad_key + against(grad_scores, query)
            grad_turned_ref[rows, head_cols(QUERY_HEADS + kv)] = (
                (grad_key * SCALING).astype(BF16).astype(F32)
            )
            at = slice(ROPED + kv * HEAD_SIZE, ROPED + (kv + 1) * HEAD_SIZE)
            grad_qkv_ref[rows, at] = grad_value.astype(BF16)
    turned = grad_turned_ref[...]
    grad_qkv_ref[:, :ROPED] = (
        turned * cos_ref[...] - swap_halves(turned) * sin_ref[...]
    ).astype(BF16)
    hidden = hidden_ref[...]
    grad_hidden, gain_one = rms_back(
        hidden, rms_scale(hidden), gain_ref[0:1, :], times_t(grad_qkv_ref[...], qkv_ref[...])
    )
    grad_in_ref[...] = grad_hidden + grad_mid
    gains_out_ref[...] = jnp.concatenate([gain_one[None], gain_two[None]], 0)


def layer_call(kernel, name, lens, operands, outs, scratch, flops):
    in_place = pl.BlockSpec(memory_space=pltpu.VMEM)
    return pl.pallas_call(
        kernel,
        in_specs=[pl.BlockSpec(memory_space=pltpu.SMEM)] + [in_place] * len(operands),
        out_specs=[in_place] * len(outs),
        out_shape=[jax.ShapeDtypeStruct(shape, dtype) for shape, dtype in outs],
        scratch_shapes=scratch,
        compiler_params=pltpu.CompilerParams(vmem_limit_bytes=VMEM_LIMIT),
        cost_estimate=pl.CostEstimate(flops=flops, bytes_accessed=8 * PL, transcendentals=0),
        name=name,
    )(lens, *operands)


def layer_forward(hidden, pieces, lens, rope):
    rows = hidden.shape[0]
    outs = [
        ((rows, MODEL_WIDTH), F32),
        ((rows, MODEL_WIDTH), BF16),
        ((rows, ROPED), BF16),
        ((rows, VALUE_WIDTH), BF16),
        ((rows, QUERY_WIDTH), BF16),
        ((rows, MODEL_WIDTH), F32),
        ((rows, MODEL_WIDTH), BF16),
        ((rows, 2 * FEED_UNITS), F32),
        ((rows, FEED_UNITS), BF16),
    ]
    output, *kept = layer_call(
        forward_kernel, "layer_forward", lens, [hidden, *pieces, *rope], outs, [], 2 * rows * PL
    )
    return output, (hidden, *kept)


def layer_backward(kept, pieces, lens, rope, grad_output):
    hidden, normed, turned, value, attended, middle, normed_two, gate_up, acted = kept
    rows = hidden.shape[0]
    outs = [
        ((rows, MODEL_WIDTH), F32),
        ((rows, MODEL_WIDTH), BF16),
        ((rows, 2 * FEED_UNITS), BF16),
        ((rows, MODEL_WIDTH), BF16),
        ((rows, QKV), BF16),
        ((2, MODEL_WIDTH), F32),
    ]
    scratch = [pltpu.VMEM((rows, QUERY_WIDTH), BF16), pltpu.VMEM((rows, ROPED), F32)]
    operands = [grad_output, hidden, *pieces, *rope, turned, value, middle, gate_up]
    grad_input, low, grad_gu, grad_mid, grad_qkv, gains = layer_call(
        backward_kernel, "layer_backward", lens, operands, outs, scratch, 2 * rows * PL
    )
    pairs = [(normed, grad_qkv), (attended, grad_mid), (normed_two, grad_gu), (acted, low)]
    return grad_input, pairs, gains.reshape(-1, 128)


def flat_rows(first, second):
    return jnp.concatenate([first, second]).reshape(-1, 128)


def token_bits(tokens):
    return tokens.bit_length() - 1


def for_chunks(keys_ref, lines_ref, span_ref, columns, run):
    bits = token_bits(keys_ref.shape[0])
    base = span_ref[2]
    places = lax.broadcasted_iota(jnp.int32, (LANES, LANES), 1)

    def chunk_step(chunk, _):
        line = lines_ref[pl.ds(chunk, 1), :]
        ids = jnp.transpose(jnp.broadcast_to(lax.shift_right_logical(line, bits), (LANES, LANES)))
        low = lax.shift_right_logical(keys_ref[chunk * LANES], bits) - base
        high = lax.shift_right_logical(keys_ref[chunk * LANES + LANES - 1], bits) - base
        first = jnp.maximum(low, 0) // COLUMNS
        last = jnp.minimum(high, columns - 1) // COLUMNS

        def hot(block):
            parts = []
            for k in range(COLUMNS // LANES):
                match = ids - (base + block * COLUMNS + k * LANES) == places
                parts.append(jnp.where(match, 1.0, 0.0).astype(BF16))
            return jnp.concatenate(parts, 1)

        run(chunk, first, last + 1, hot)
        return 0

    lax.fori_loop(span_ref[0] // LANES, (span_ref[1] + LANES - 1) // LANES, chunk_step, 0)


def row_of(keys_ref, at):
    return keys_ref[at] & (keys_ref.shape[0] - 1)


def embed_kernel(keys_ref, span_ref, lines_ref, table_ref, out_ref, low_ref, rows_ref, found_ref):
    features, columns = table_ref.shape
    blocks, _, width = out_ref.shape
    low_ref[:features, :] = table_ref[...].astype(BF16)
    low_ref[features:, :] = jnp.zeros((LANES - features, columns), BF16)
    for k in range(blocks):
        rows_ref[k * width : (k + 1) * width, :] = jnp.zeros((width, LANES), F32)

    def run(chunk, first, last, hot):
        def block_step(block, total):
            at = pl.multiple_of(block * COLUMNS, COLUMNS)
            return total + times_t(hot(block), low_ref[:, pl.ds(at, COLUMNS)])

        found_ref[...] = lax.fori_loop(first, last, block_step, jnp.zeros((LANES, LANES), F32))

        def move(k, _):
            for j in range(8):
                row = row_of(keys_ref, chunk * LANES + k * 8 + j)
                rows_ref[pl.ds(row, 1), :] = found_ref[pl.ds(k * 8 + j, 1), :]
            return 0

        lax.fori_loop(0, LANES // 8, move, 0)

    for_chunks(keys_ref, lines_ref, span_ref, columns, run)

    def finish(k, _):
        at = pl.multiple_of(k * width, width)
        out_ref[k] = jnp.transpose(rows_ref[pl.ds(at, width), :])[:features].astype(BF16)
        return 0

    lax.fori_loop(0, blocks, finish, 0)


def embed_rows(keys, span, table, blocks):
    tokens = keys.shape[0]
    features, columns = table.shape
    scalars = pl.BlockSpec(memory_space=pltpu.SMEM)
    in_place = pl.BlockSpec(memory_space=pltpu.VMEM)
    return pl.pallas_call(
        embed_kernel,
        in_specs=[scalars, scalars, in_place, in_place],
        out_specs=in_place,
        out_shape=jax.ShapeDtypeStruct((blocks, features, tokens // blocks), BF16),
        scratch_shapes=[
            pltpu.VMEM((LANES, columns), BF16),
            pltpu.VMEM((tokens, LANES), F32),
            pltpu.VMEM((LANES, LANES), F32),
        ],
        compiler_params=pltpu.CompilerParams(vmem_limit_bytes=VMEM_LIMIT),
        cost_estimate=pl.CostEstimate(
            flops=2 * tokens * LANES * COLUMNS, bytes_accessed=4 * table.size, transcendentals=0
        ),
        name="embed_rows",
    )(keys, span, keys.reshape(-1, LANES), table)


def spread_kernel(keys_ref, span_ref, place_ref, lines_ref, *refs):
    parts, (base_ref, out_ref, rows_ref, packed_ref) = refs[:-4], refs[-4:]
    features, columns = base_ref.shape
    count, _, width = parts[0].shape
    for k, part in enumerate(parts):
        def unfold(j, _):
            at = pl.multiple_of(place_ref[k * count + j] * width, width)
            flat = part[j].astype(F32)
            flat = jnp.concatenate([flat, jnp.zeros((LANES - features, width), F32)], 0)
            rows_ref[pl.ds(at, width), :] = jnp.transpose(flat)
            return 0

        lax.fori_loop(0, count, unfold, 0)
    out_ref[...] = base_ref[...]

    def run(chunk, first, last, hot):
        def move(k, _):
            for j in range(8):
                row = row_of(keys_ref, chunk * LANES + k * 8 + j)
                packed_ref[pl.ds(k * 8 + j, 1), :] = rows_ref[pl.ds(row, 1), :]
            return 0

        lax.fori_loop(0, LANES // 8, move, 0)
        packed = packed_ref[...].astype(BF16)

        def block_step(block, _):
            at = pl.multiple_of(block * COLUMNS, COLUMNS)
            out_ref[:, pl.ds(at, COLUMNS)] += against(packed, hot(block))[:features]
            return 0

        lax.fori_loop(first, last, block_step, 0)

    for_chunks(keys_ref, lines_ref, span_ref, columns, run)


def spread_rows(keys, span, places, parts, base):
    tokens = keys.shape[0]
    scalars = pl.BlockSpec(memory_space=pltpu.SMEM)
    in_place = pl.BlockSpec(memory_space=pltpu.VMEM)
    return pl.pallas_call(
        spread_kernel,
        in_specs=[scalars] * 3 + [in_place] * (2 + len(parts)),
        out_specs=in_place,
        out_shape=jax.ShapeDtypeStruct(base.shape, F32),
        scratch_shapes=[
            pltpu.VMEM((tokens, LANES), F32),
            pltpu.VMEM((LANES, LANES), F32),
        ],
        compiler_params=pltpu.CompilerParams(vmem_limit_bytes=VMEM_LIMIT),
        cost_estimate=pl.CostEstimate(
            flops=2 * tokens * LANES * COLUMNS, bytes_accessed=8 * base.size, transcendentals=0
        ),
        name="spread_rows",
    )(keys, span, places, keys.reshape(-1, LANES), *parts, base)


def second_kernel(rows_ref, weight_ref, gain_ref, both_ref, projected_ref):
    projected = jnp.dot(rows_ref[...], weight_ref[...], preferred_element_type=F32)
    projected_ref[...] = projected
    both_ref[0] = rows_ref[...]
    both_ref[1] = (projected * rms_scale(projected) * gain_ref[...]).astype(BF16)


def second_head(rows, weight, gain):
    count = rows.shape[0]
    return pl.pallas_call(
        second_kernel,
        grid=(count // BLOCK,),
        in_specs=[
            pl.BlockSpec((BLOCK, MODEL_WIDTH), lambda i: (i, 0)),
            pl.BlockSpec(weight.shape, lambda i: (0, 0)),
            pl.BlockSpec(gain.shape, lambda i: (0, 0)),
        ],
        out_specs=[
            pl.BlockSpec((2, BLOCK, MODEL_WIDTH), lambda i: (0, i, 0)),
            pl.BlockSpec((BLOCK, MODEL_WIDTH), lambda i: (i, 0)),
        ],
        out_shape=[
            jax.ShapeDtypeStruct((2, count, MODEL_WIDTH), BF16),
            jax.ShapeDtypeStruct((count, MODEL_WIDTH), F32),
        ],
        compiler_params=pltpu.CompilerParams(vmem_limit_bytes=VMEM_LIMIT),
        cost_estimate=pl.CostEstimate(
            flops=2 * count * weight.size, bytes_accessed=10 * rows.size, transcendentals=0
        ),
        name="second_head",
    )(rows, weight, gain)


def block_count(count_ref):
    per = BLOCK // GRANULE
    return (count_ref[0] + per - 1) // per


def block_at(i, count_ref, list_ref):
    return (jnp.minimum(i, jnp.maximum(block_count(count_ref) - 1, 0)), 0)


def head_kernel(
    count_ref, list_ref, rows_ref, table_ref,
    exp_ref, back_ref, sum_ref, peak_ref,
    packed, even, odd,
):
    columns = table_ref.shape[1]
    chunk = even.shape[1]
    chunks = columns // chunk
    logits = (even, odd)
    per = BLOCK // GRANULE
    block = pl.program_id(0)

    @pl.when(block == 0)
    def _():
        back_ref[...] = jnp.zeros(back_ref.shape, F32)
        sum_ref[...] = jnp.ones(sum_ref.shape, F32)
        peak_ref[...] = jnp.zeros(peak_ref.shape, F32)

    def spot(g):
        return pl.multiple_of(list_ref[block * per + g] * GRANULE, GRANULE)

    def dot_chunk(k):
        return jnp.dot(
            packed[...], table_ref[:, k * chunk : (k + 1) * chunk], preferred_element_type=F32
        )

    def put(stat_ref, line):
        for g in range(per):
            lane = g * GRANULE // 128 * 128
            part = line[:, lane : lane + 128]
            if g * GRANULE % 128:
                part = pltpu.roll(part, 128 - g * GRANULE % 128, 1)
            stat_ref[pl.ds(list_ref[block * per + g], 1), :] = part

    def run(peak):
        total = jnp.zeros((BLOCK, 128), F32)
        logits[0][...] = dot_chunk(0)
        for k in range(chunks):
            if k + 1 < chunks:
                logits[(k + 1) % 2][...] = dot_chunk(k + 1)
            here = logits[k % 2][...]
            powers = jnp.exp(here if peak is None else here - peak)
            for j in range(chunk // 128):
                total = total + powers[:, j * 128 : (j + 1) * 128]
            exp_ref[:, k * chunk : (k + 1) * chunk] = powers.astype(BF16)
        line = jnp.sum(jnp.transpose(total), axis=0, keepdims=True)
        put(sum_ref, line)
        back = times_t(exp_ref[...], table_ref[...])
        for g in range(per):
            back_ref[pl.ds(spot(g), GRANULE), :] = back[g * GRANULE : (g + 1) * GRANULE]
        return line

    @pl.when(block < block_count(count_ref))
    def _():
        for g in range(per):
            packed[g * GRANULE : (g + 1) * GRANULE, :] = rows_ref[pl.ds(spot(g), GRANULE), :]
        sums = run(None)
        fits = jnp.min(jnp.where((sums > 1e-20) & (sums < 1e30), 1.0, 0.0))

        @pl.when(fits < 0.5)
        def _():
            wide = jnp.full((BLOCK, 128), -jnp.inf, F32)
            for k in range(chunks):
                here = dot_chunk(k)
                for j in range(chunk // 128):
                    wide = jnp.maximum(wide, here[:, j * 128 : (j + 1) * 128])
            put(peak_ref, jnp.max(jnp.transpose(wide), axis=0, keepdims=True))
            run(jnp.max(wide, axis=1, keepdims=True))


def head_forward(count, order, rows, table):
    height, columns = rows.shape[0], table.shape[1]
    granules = height // GRANULE
    chunk = min(CHUNK // 2, columns // 2)
    whole = pl.Buffered(1)

    def once(i, count_ref, list_ref):
        return (0, 0)

    return pl.pallas_call(
        head_kernel,
        grid_spec=pltpu.PrefetchScalarGridSpec(
            num_scalar_prefetch=2,
            grid=(height // BLOCK,),
            in_specs=[
                pl.BlockSpec(rows.shape, once, pipeline_mode=whole),
                pl.BlockSpec(table.shape, once, pipeline_mode=whole),
            ],
            out_specs=[
                pl.BlockSpec((BLOCK, columns), block_at),
                pl.BlockSpec((height, MODEL_WIDTH), once, pipeline_mode=whole),
                pl.BlockSpec((granules, 128), once),
                pl.BlockSpec((granules, 128), once),
            ],
            scratch_shapes=[
                pltpu.VMEM((BLOCK, MODEL_WIDTH), BF16),
                pltpu.VMEM((BLOCK, chunk), F32),
                pltpu.VMEM((BLOCK, chunk), F32),
            ],
        ),
        out_shape=[
            jax.ShapeDtypeStruct((height, columns), BF16),
            jax.ShapeDtypeStruct((height, MODEL_WIDTH), F32),
            jax.ShapeDtypeStruct((granules, 128), F32),
            jax.ShapeDtypeStruct((granules, 128), F32),
        ],
        compiler_params=pltpu.CompilerParams(vmem_limit_bytes=VMEM_LIMIT),
        cost_estimate=pl.CostEstimate(
            flops=4 * height * table.size,
            bytes_accessed=2 * height * columns,
            transcendentals=height * columns,
        ),
        name="head_forward",
    )(count, order, rows, table)


def scale_kernel(
    count_ref, list_ref, rows_ref, back_ref, scale_ref, grad_ref, turned_ref, scaled, packed
):
    per = BLOCK // GRANULE
    step, blocks = pl.program_id(0), pl.num_programs(0) // 2

    @pl.when(step < blocks)
    def _():
        for k in range(BLOCK // LANES):
            at = slice(k * LANES, (k + 1) * LANES)
            line = scale_ref[pl.ds(step * (BLOCK // LANES) + k, 1), :]
            column = jnp.transpose(jnp.broadcast_to(line, (LANES, LANES)))[:, :1]
            grad_ref[at, :] = back_ref[at, :] * column
            row = pl.multiple_of(step * BLOCK + k * LANES, LANES)
            scaled[pl.ds(row, LANES), :] = (rows_ref[at, :].astype(F32) * column).astype(BF16)

    block = step - blocks

    @pl.when((block >= 0) & (block < block_count(count_ref)))
    def _():
        for g in range(per):
            at = block * per + g
            spot = pl.multiple_of(list_ref[at] * GRANULE, GRANULE)
            part = scaled[pl.ds(spot, GRANULE), :].astype(F32)
            packed[g * GRANULE : (g + 1) * GRANULE, :] = jnp.where(
                at < count_ref[0], part, jnp.zeros_like(part)
            )
        turned_ref[...] = jnp.transpose(packed[...]).astype(BF16)


def scale_rows(count, order, rows, back, scale):
    height = rows.shape[0]
    blocks = height // BLOCK

    def first(i, count_ref, list_ref):
        return (jnp.minimum(i, blocks - 1), 0)

    def second(i, count_ref, list_ref):
        return (0, block_at(jnp.maximum(i - blocks, 0), count_ref, list_ref)[0])

    return pl.pallas_call(
        scale_kernel,
        grid_spec=pltpu.PrefetchScalarGridSpec(
            num_scalar_prefetch=2,
            grid=(2 * blocks,),
            in_specs=[
                pl.BlockSpec((BLOCK, MODEL_WIDTH), first),
                pl.BlockSpec((BLOCK, MODEL_WIDTH), first),
                pl.BlockSpec(scale.shape, lambda i, count_ref, list_ref: (0, 0)),
            ],
            out_specs=[
                pl.BlockSpec((BLOCK, MODEL_WIDTH), first),
                pl.BlockSpec((MODEL_WIDTH, BLOCK), second),
            ],
            scratch_shapes=[
                pltpu.VMEM((height, MODEL_WIDTH), BF16),
                pltpu.VMEM((BLOCK, MODEL_WIDTH), F32),
            ],
        ),
        out_shape=[
            jax.ShapeDtypeStruct((height, MODEL_WIDTH), F32),
            jax.ShapeDtypeStruct((MODEL_WIDTH, height), BF16),
        ],
        compiler_params=pltpu.CompilerParams(vmem_limit_bytes=VMEM_LIMIT),
        cost_estimate=pl.CostEstimate(flops=0, bytes_accessed=12 * rows.size, transcendentals=0),
        name="scale_rows",
    )(count, order, rows, back, scale)


def table_kernel(count_ref, turned_ref, exp_ref, out_ref):
    used = block_count(count_ref)

    @pl.when(used == 0)
    def _():
        out_ref[...] = jnp.zeros(out_ref.shape, BF16)

    for blocks in range(1, exp_ref.shape[0] // BLOCK + 1):

        @pl.when(used == blocks)
        def _():
            out_ref[...] = jnp.dot(
                turned_ref[:, : blocks * BLOCK],
                exp_ref[: blocks * BLOCK, :],
                preferred_element_type=F32,
            ).astype(BF16)


def table_backward(count, turned, powers, part, parts):
    height, columns = powers.shape[0], powers.shape[1] // parts
    chunk = 512 if columns % 512 == 0 else 256
    steps = columns // chunk
    return pl.pallas_call(
        table_kernel,
        grid_spec=pltpu.PrefetchScalarGridSpec(
            num_scalar_prefetch=1,
            grid=(steps,),
            in_specs=[
                pl.BlockSpec(
                    turned.shape, lambda i, count_ref: (0, 0), pipeline_mode=pl.Buffered(1)
                ),
                pl.BlockSpec((height, chunk), lambda i, count_ref: (0, part * steps + i)),
            ],
            out_specs=pl.BlockSpec((MODEL_WIDTH, chunk), lambda i, count_ref: (0, i)),
        ),
        out_shape=jax.ShapeDtypeStruct((MODEL_WIDTH, columns), BF16),
        compiler_params=pltpu.CompilerParams(vmem_limit_bytes=VMEM_LIMIT),
        cost_estimate=pl.CostEstimate(
            flops=2 * MODEL_WIDTH * powers.size // parts,
            bytes_accessed=2 * powers.size // parts,
            transcendentals=0,
        ),
        name="table_backward",
    )(count, turned, powers)


def shards(
    token_ids,
    lengths,
    deal_order,
    embed_table,
    table_mom,
    table_avg,
    model_flat,
    model_mom,
    model_avg,
):
    dp_size, shard_size = lax.axis_size("dp"), lax.axis_size("shard")
    shard_idx, dp_idx = lax.axis_index("shard"), lax.axis_index("dp")
    device_idx = lax.axis_index(("dp", "shard"))
    core = dp_bit(1)
    seqs = token_ids.shape[0]
    own_rows = seqs * LEN
    group = 2 * shard_size
    groups = dp_size // 2
    slots = group * seqs
    seq_total = groups * slots
    target_count = jnp.float32((MEAN_LENGTH - 1) * seq_total)
    features, columns = embed_table.shape
    half = columns // 2
    vocab_start = shard_idx * columns + core * half
    length = model_flat.shape[0]

    tiny = jnp.concatenate([token_ids, jnp.broadcast_to(lengths[:, None], (seqs, LEN))], 0)
    tiny = tiny.reshape((1,) * (len(bits_below(dp_size)) + len(bits_below(shard_size))) + tiny.shape)
    for k, bit in enumerate(bits_below(dp_size)[::-1]):
        tiny = join(tiny, flip_dp(tiny, bit), bit, k)
    for k, bit in enumerate(bits_below(shard_size)[::-1]):
        other = flip_shard(tiny, bit)
        axis = len(bits_below(dp_size)) + k
        tiny = jnp.where(
            (shard_idx // bit) % 2 == 0,
            jnp.concatenate([tiny, other], axis),
            jnp.concatenate([other, tiny], axis),
        )
    tiny = tiny.reshape(dp_size * shard_size, 2 * seqs, LEN)
    all_ids = tiny[:, :seqs].reshape(seq_total, LEN)
    all_lens = tiny[:, seqs:, 0].reshape(seq_total)
    here = jnp.arange(seq_total)
    longer = all_lens[None, :] > all_lens[:, None]
    equal = (all_lens[None, :] == all_lens[:, None]) & (here[None, :] < here[:, None])
    rank = jnp.sum((longer | equal).astype(jnp.int32), axis=1)
    turn, seat = rank // groups, rank % groups
    group_of = jnp.where(turn % 2 == 0, seat, groups - 1 - seat)
    place_of = group_of * slots + turn
    hits = (place_of[None, :] == here[:, None]).astype(jnp.int32)
    seq_at = jnp.sum(hits * here[None, :], axis=1)
    dealt_ids = all_ids[seq_at]
    dealt_lens = jnp.sum(hits * all_lens[None, :], axis=1)
    my_group = dp_idx // 2
    group_ids = lax.dynamic_slice_in_dim(dealt_ids, my_group * slots, slots, 0)
    group_lens = lax.dynamic_slice_in_dim(dealt_lens, my_group * slots, slots, 0)
    own_at = core * shard_size + shard_idx
    own_lens = lax.dynamic_slice_in_dim(group_lens, own_at * seqs, seqs, 0)
    own_seqs = lax.dynamic_slice_in_dim(seq_at, (my_group * group + own_at) * seqs, seqs, 0)

    places = jnp.arange(LEN)
    weight_one = (places[None, :] + 1 < group_lens[:, None]).astype(F32)
    weight_two = SECOND_WEIGHT * (places[None, :] + 2 < group_lens[:, None]).astype(F32)
    weights = jnp.stack([weight_one, weight_two]) / target_count

    per_seq = LEN // GRANULE
    starts = jnp.arange(per_seq) * GRANULE
    useful = jnp.stack([starts[None, :] + k + 1 < group_lens[:, None] for k in range(2)])
    useful = useful.reshape(-1)
    index = jnp.arange(useful.shape[0])
    before = jnp.sum((useful[None, :] & (index[None, :] < index[:, None])).astype(jnp.int32), axis=1)
    count = jnp.sum(useful.astype(jnp.int32))
    last = jnp.max(jnp.where(useful, index, 0))
    found = useful[None, :] & (before[None, :] == index[:, None])
    order = jnp.sum(jnp.where(found, index[None, :], 0), axis=1)
    order = jnp.where(index < count, order, last).astype(jnp.int32)
    count = count.reshape(1)

    everything = lax.all_gather(own_blocks(model_flat), ("dp", "shard"))

    tokens = seq_total * LEN
    bits = token_bits(tokens)
    kept_ids = jnp.where(places[None, :] < dealt_lens[:, None], dealt_ids, columns * shard_size)
    keys = jnp.sort(kept_ids.reshape(-1) * tokens + jnp.arange(tokens, dtype=jnp.int32))
    first_id = shard_idx * columns
    span = jnp.stack(
        [
            jnp.sum((keys < first_id * tokens).astype(jnp.int32)),
            jnp.sum(((keys >> bits) < first_id + columns).astype(jnp.int32)),
            first_id,
        ]
    ).astype(jnp.int32)
    devices = dp_size * shard_size
    picked = embed_rows(keys, span, embed_table, devices)
    picked = picked.reshape(dp_size, shard_size, features, own_rows)
    mine = ring_reduce(picked.transpose(1, 0, 2, 3)).astype(BF16)
    parts = [pick(mine, dp_idx, 0)]
    parts += [flip_dp(pick(mine, dp_idx ^ k, 0), k) for k in range(1, dp_size)]
    embedded = jnp.stack(parts)[jnp.arange(dp_size) ^ dp_idx]
    embedded = embedded.reshape(MODEL_WIDTH, own_rows).T.astype(F32)

    held_table, everything = lax.optimization_barrier((embed_table, everything))
    table_gather = TableGather(held_table)
    middle_rows = PL // 128
    low_rows = middle_rows // 16 * 16
    total_devices = dp_size * shard_size
    per = GRAIN // 128
    end_row = block_starts(length, total_devices)[-1] * per
    tail = 2 * MODEL_WIDTH // 128
    square = MODEL_WIDTH * MODEL_WIDTH // 128
    *layer_zero, gains_zero = unpack_rows(
        everything, length, 0, low_rows + 16, LAYER_SHAPES, {}, 0, ((middle_rows - tail, 16),)
    )
    gain_row = middle_rows - low_rows + middle_rows - tail
    second_row = gain_row + tail + square
    base_one = gain_row // 16 * 16
    base_two = second_row // 16 * 16 - 16
    *layer_one, w_second, gains_one, gains_head = unpack_rows(
        everything, length, low_rows, end_row, LAYER_SHAPES + SQUARE, {3: tail},
        middle_rows - low_rows, ((base_one, 32), (base_two, 32)),
    )

    def gain_pair(rows, at):
        return rows[at : at + tail].reshape(2, MODEL_WIDTH)

    layer_zero.append(gain_pair(gains_zero, 0).astype(F32))
    layer_one.append(gain_pair(gains_one, gain_row - base_one).astype(F32))
    head_gains = gain_pair(gains_head, second_row - base_two).astype(F32)

    rope = rope_rows(own_rows)
    hidden, kept_zero = layer_forward(embedded, layer_zero, own_lens, rope)
    hidden = table_gather.tied(hidden)
    table_gather.step()
    hidden, kept_one = layer_forward(hidden, layer_one, own_lens, rope)
    scale_final = rms_scale(hidden)
    head_one = (hidden * scale_final * head_gains[0]).astype(BF16)
    all_one = group_gather(head_one, table_gather.tied).reshape(-1, MODEL_WIDTH)
    table_low = table_gather.finish()
    both, projected = second_head(all_one, w_second, head_gains[1:2])
    all_two = both[1]
    both = both.reshape(-1, MODEL_WIDTH)
    scale_second = rms_scale(projected)
    group_rows = all_one.shape[0]

    powers, back, sums, peaks = head_forward(count, order, both, table_low)
    sums = sums[:, :GRANULE].reshape(-1, 128)
    peaks = peaks[:, :GRANULE].reshape(-1, 128)
    sum_all_rows, peak_all = sums, peaks
    for flip, bits in ((flip_shard, bits_below(shard_size)), (flip_dp, [1])):
        for bit in bits:
            stats = flip(jnp.stack([sum_all_rows, peak_all]), bit)
            top = jnp.maximum(peak_all, stats[1])
            sum_all_rows = sum_all_rows * jnp.exp(peak_all - top) + stats[0] * jnp.exp(
                stats[1] - top
            )
            peak_all = top
    log_total = (peak_all + jnp.log(sum_all_rows)).reshape(2, group, seqs, LEN)
    row_scale = weights.reshape(-1, 128) * jnp.exp(peaks - peak_all) / sum_all_rows
    grad_rows, turned_rows = scale_rows(count, order, both, back, row_scale)

    own_log = pick(log_total, own_at, 1)
    own_weights = pick(weights.reshape(2, group, seqs, LEN), own_at, 1)
    words = embedded.reshape(seqs, LEN, MODEL_WIDTH)
    next_one = jnp.roll(words, -1, 1).reshape(own_rows, MODEL_WIDTH)
    next_two = jnp.roll(words, -2, 1).reshape(own_rows, MODEL_WIDTH)
    head_two = lax.dynamic_slice_in_dim(all_two, own_at * own_rows, own_rows, 0)
    chosen_one = jnp.sum(head_one.astype(F32) * next_one, axis=-1)
    chosen_two = jnp.sum(head_two.astype(F32) * next_two, axis=-1)
    chosen = jnp.stack([chosen_one, chosen_two]).reshape(2, seqs, LEN)
    own_loss = jnp.sum(own_weights * (own_log - chosen), axis=(0, 2))

    weight_col = own_weights.reshape(2, own_rows, 1)
    part_two = grad_rows[group_rows:]
    own_two = lax.dynamic_slice_in_dim(part_two, own_at * own_rows, own_rows, 0)
    part_two = lax.dynamic_update_slice_in_dim(
        part_two, own_two - weight_col[1] * next_two, own_at * own_rows, 0
    )
    grad_proj, grad_gain_second = rms_back(projected, scale_second, head_gains[1], part_two)
    grad_proj_low = grad_proj.astype(BF16)
    part_one = grad_rows[:group_rows] + times_t(grad_proj_low, w_second)
    quarters = 4
    cubes = [None] * quarters
    running = [turned_rows]

    def quarter_hook(k):
        def hook(got):
            part = table_backward(count, running[0], powers, k, quarters)
            got, part, running[0] = lax.optimization_barrier((got, part, running[0]))
            bits = high_bits() if k < quarters // 2 else high_bits()[::-1]
            cubes[k] = Cube(part.reshape(-1, 2 * features, part.shape[1]), bits)
            return got

        return hook

    grad_final = group_reduce(
        part_one.reshape(2, shard_size, own_rows, MODEL_WIDTH),
        [quarter_hook(k) for k in (0, 2, 1, 3)],
    )
    grad_final = grad_final - weight_col[0] * next_one
    grad_hidden, grad_gain_final = rms_back(hidden, scale_final, head_gains[0], grad_final)

    sub_rows = owner_sub_rows(length)
    height_zero = length * (total_devices // 2 - 1) // GRAIN * per + 2 * sub_rows
    height_one = length * (total_devices - 1) // GRAIN * per + 2 * sub_rows - low_rows
    keep = height_zero - low_rows
    grad_hidden = tie(grad_hidden, [cubes[0], cubes[2]])
    cubes[0].step(), cubes[2].step()
    grad_hidden, pairs, gain_grads = layer_backward(
        kept_one, layer_one, own_lens, rope, grad_hidden
    )
    gain_grads = tie(gain_grads, [cubes[1], cubes[3]])
    cubes[1].step(), cubes[3].step()
    own_one, send_one, kept_rows = pack_half(
        owner_rows(length, 1, low_rows),
        pairs + [(all_one, grad_proj_low)],
        [gain_grads, flat_rows(grad_gain_final, grad_gain_second)],
        None, middle_rows - low_rows, {3: tail, 4: tail}, height_one, sub_rows, keep, 0,
    )
    got_one = flip_dp(send_one, 1)
    grad_hidden, own_one, got_one = lax.optimization_barrier((grad_hidden, own_one, got_one))
    cubes_one = half_cubes(own_one, got_one)
    grad_hidden, pairs, gain_grads = layer_backward(
        kept_zero, layer_zero, own_lens, rope, grad_hidden
    )
    gain_grads = tie(gain_grads, cubes)
    joined = jnp.concatenate([cube.finish() for cube in cubes], 1)
    flipped = owner_flip(joined, features)
    own_zero, send_zero = pack_half(
        owner_rows(length, 0, 0), pairs, [gain_grads],
        (kept_rows, height_zero - middle_rows), 0, {3: tail}, height_zero, sub_rows, 0,
        middle_rows - low_rows,
    )
    one_terms = (weight_col[0] * head_one.astype(F32)).reshape(seqs, LEN, MODEL_WIDTH)
    two_terms = (weight_col[1] * head_two.astype(F32)).reshape(seqs, LEN, MODEL_WIDTH)
    token_grad = (
        grad_hidden.astype(BF16).astype(F32)
        - jnp.roll(one_terms, 1, 1).reshape(own_rows, MODEL_WIDTH)
        - jnp.roll(two_terms, 2, 1).reshape(own_rows, MODEL_WIDTH)
    ).astype(BF16)
    token_parts = token_grad.T.reshape(dp_size, features, own_rows)
    parts = [pick(token_parts, dp_idx, 0)]
    parts += [flip_dp(pick(token_parts, dp_idx ^ k, 0), k) for k in range(1, dp_size)]
    own_zero = tie(own_zero, cubes_one)
    for cube in cubes_one:
        cube.step()
    got_zero, parts, flipped = lax.optimization_barrier((flip_dp(send_zero, 1), parts, flipped))
    table_part = owner_join(joined, flipped, features)
    cubes_zero = half_cubes(own_zero, got_zero)
    chain = [jnp.stack(parts)]
    for k in range(shard_size - 1):
        chain.append(next_shard(chain[-1]))
        if k == 0:
            chain[-1] = tie(chain[-1], cubes_one)
            sums_one = jnp.concatenate([cube.finish() for cube in cubes_one], 0)
    chain[-1] = tie(chain[-1], cubes_zero)
    for cube in cubes_zero:
        cube.step()
    from_dp = (jnp.arange(dp_size) ^ dp_idx)[None, :]
    from_shard = (shard_idx - jnp.arange(shard_size))[:, None] % shard_size
    spots = (from_dp * shard_size + from_shard).reshape(-1).astype(jnp.int32)
    table_sum = spread_rows(keys, span, spots, chain, table_part)
    table_sum = tie(table_sum, cubes_zero)
    sums_zero = jnp.concatenate([cube.finish() for cube in cubes_zero], 0)
    model_sum = own_part(sums_zero, sums_one, length)

    square_sum = jnp.sum(table_sum * table_sum) + jnp.sum(model_sum * model_sum)
    losses = jnp.sum(
        jnp.where(own_seqs[:, None] == here[None, :], own_loss[:, None], 0.0), axis=0
    )
    totals = sum_all(jnp.concatenate([losses, square_sum.reshape(1)])[None])[0]
    grad_norm = jnp.sqrt(totals[seq_total])
    factor = jnp.minimum(1.0, CLIP_NORM / (grad_norm + 1e-06))
    all_loss = totals[:seq_total]
    loss_total = jnp.sum(all_loss)
    seq_loss = lax.dynamic_slice_in_dim(all_loss, device_idx * seqs, seqs, 0)
    own_slots = lax.dynamic_slice_in_dim(deal_order, device_idx * seqs, seqs, 0)
    slot_loss = all_loss[own_slots]

    results = []
    for weights_in, gradient, moment, average in (
        (embed_table, table_sum, table_mom, table_avg),
        (model_flat, model_sum, model_mom, model_avg),
    ):
        clipped = gradient * factor
        new_moment = MOMENTUM * moment + clipped
        new_weight = weights_in - LEARN_RATE * (clipped + MOMENTUM * new_moment)
        new_average = AVERAGE_KEEP * average + (1.0 - AVERAGE_KEEP) * new_weight
        results.append(
            (clipped, new_weight, new_moment, new_average, new_weight.astype(BF16))
        )
    return (loss_total, seq_loss, slot_loss, grad_norm) + results[0] + results[1]


def solution(mesh):
    both = P(("dp", "shard"))
    block = P("dp", "shard")
    return jax.shard_map(
        shards,
        mesh=mesh,
        in_specs=(P(("dp", "shard"), None), both, P(), block, block, block, both, both, both),
        out_specs=(P(), both, both, P()) + (block,) * 5 + (both,) * 5,
        check_vma=False,
    )
```

```python
import jax
import jax.numpy as jnp
from jax import lax
from jax.experimental import pallas as pl
from jax.experimental.pallas import tpu as pltpu
from jax.sharding import PartitionSpec as P

MODEL_WIDTH = 576
QUERY_HEADS = 9
KEY_VALUE_HEADS = 3
HEAD_SIZE = 64
FEED_UNITS = 1536
LAYERS = 2
LEN = 128
PL = 3540096
NP = 7413120
QKV = (QUERY_HEADS + 2 * KEY_VALUE_HEADS) * HEAD_SIZE
ROPED = (QUERY_HEADS + KEY_VALUE_HEADS) * HEAD_SIZE
MEAN_LENGTH = 96

EPSILON = 1e-05
ROPE_BASE = 100000.0
CLIP_NORM = 0.01
LEARN_RATE = 6000.0
MOMENTUM = 0.9
AVERAGE_KEEP = 0.9
SECOND_WEIGHT = 0.3
MASKED_SCORE = -1e30

GRAIN = 2048
GRANULE = 16
BLOCK = 256
STEP = 1024
CHUNK = 1024
LANES = 128
COLUMNS = 256
VMEM_LIMIT = 62 * 1024 * 1024
F32 = jnp.float32
BF16 = jnp.bfloat16


def flip_dp(values, bit):
    return lax.ppermute(values, "dp", [(i, i ^ bit) for i in range(lax.axis_size("dp"))])


def flip_shard(values, bit):
    return lax.ppermute(values, "shard", [(i, i ^ bit) for i in range(lax.axis_size("shard"))])


def next_shard(values):
    size = lax.axis_size("shard")
    return lax.ppermute(values, "shard", [(i, (i + 1) % size) for i in range(size)])


def bits_below(size):
    return [1 << k for k in range(size.bit_length() - 1)]


def dp_bit(bit):
    return (lax.axis_index("dp") // bit) % 2


def join(own, other, bit, axis):
    return jnp.where(
        dp_bit(bit) == 0,
        jnp.concatenate([own, other], axis),
        jnp.concatenate([other, own], axis),
    )


def pick(values, idx, axis):
    return lax.dynamic_index_in_dim(values, idx, axis, keepdims=False)


def high_bits():
    return bits_below(lax.axis_size("dp"))[1:]


def gather_cube(values, order):
    bits = sorted(order, reverse=True)
    out = values.reshape((1,) * len(bits) + values.shape)
    for bit in order:
        out = join(out, flip_dp(out, bit), bit, bits.index(bit))
    return out.reshape((-1,) + values.shape)


class Cube:
    def __init__(self, values, order):
        self.left = sorted(order, reverse=True)
        self.order = list(order)
        self.out = values.reshape((2,) * len(order) + values.shape[1:])
        self.start()

    def start(self):
        bit = self.order[0]
        axis = self.left.index(bit)
        mine = dp_bit(bit)
        self.got = flip_dp(pick(self.out, 1 - mine, axis).astype(BF16), bit)
        self.keep = pick(self.out, mine, axis)

    def step(self):
        self.out = self.keep.astype(F32) + self.got.astype(F32)
        self.left.remove(self.order.pop(0))
        if self.order:
            self.start()
        return bool(self.order)

    def finish(self):
        while self.order:
            self.step()
        return self.out


def tie(main, cubes):
    main, gots = lax.optimization_barrier((main, [cube.got for cube in cubes]))
    for cube, got in zip(cubes, gots):
        cube.got = got
    return main


def ring_reduce(values, hooks=()):
    size = lax.axis_size("shard")
    me = lax.axis_index("shard")
    total = None
    for step in range(size - 1):
        term = pick(values, (me - 1 - step) % size, 0).astype(F32)
        if total is not None:
            term = term + total
        got = next_shard(term.astype(BF16))
        if step < len(hooks):
            got = hooks[step](got)
        total = got.astype(F32)
    return total + pick(values, me, 0).astype(F32)


def ring_gather(values, hook=None):
    size = lax.axis_size("shard")
    me = lax.axis_index("shard")
    parts = [values]
    for k in range(size - 1):
        parts.append(next_shard(parts[-1]))
        if hook is not None and k == 1:
            parts[-1] = hook(parts[-1])
    stacked = jnp.stack(parts[::-1])
    return jnp.roll(stacked, me + 1, axis=0)


def group_gather(rows, hook=None):
    parts = ring_gather(rows, hook)
    other = flip_dp(parts, 1)
    return join(parts[None], other[None], 1, 0)


def group_reduce(parts, hooks):
    mine = dp_bit(1)
    got = hooks[0](flip_dp(pick(parts, 1 - mine, 0).astype(BF16), 1))
    return ring_reduce(pick(parts, mine, 0).astype(F32) + got.astype(F32), hooks[1:])


def sum_all(value):
    total = value
    for bit in bits_below(lax.axis_size("dp")):
        total = total + flip_dp(total, bit)
    for bit in bits_below(lax.axis_size("shard")):
        total = total + flip_shard(total, bit)
    return total


def top_bit():
    return high_bits()[-1]


def block_starts(length, total):
    return [length * i // GRAIN for i in range(total)] + [-(-length * total // GRAIN)]


def own_blocks(model_flat):
    length = model_flat.shape[0]
    total = lax.axis_size("dp") * lax.axis_size("shard")
    device = lax.axis_index(("dp", "shard"))
    low = model_flat.astype(BF16)
    starts = block_starts(length, total)
    blocks = max(starts[i + 1] - starts[i] for i in range(total)) + 1
    extended = jnp.pad(low, (GRAIN, 3 * GRAIN))
    shift = (length * device) % GRAIN
    whole = lax.dynamic_slice_in_dim(extended, GRAIN - shift, blocks * GRAIN, 0)
    return whole.reshape(-1, 128)


LAYER_SHAPES = (
    (MODEL_WIDTH, QKV),
    (MODEL_WIDTH, MODEL_WIDTH),
    (MODEL_WIDTH, 2 * FEED_UNITS),
    (FEED_UNITS, MODEL_WIDTH),
)
SQUARE = ((MODEL_WIDTH, MODEL_WIDTH),)
TALL = 64


def line_up(flat_at, out, height, breadth):
    tiles, odd = breadth // 128, breadth % 128
    if not odd:
        for j in range(tiles):
            out(0, j, flat_at(j, height, tiles))
        return
    period = 2 * tiles + 1
    loads = [flat_at(j, height // 2, period) for j in range(period)]
    for j in range(tiles + 1):
        out(0, j, loads[j])
        after = loads[min(tiles + j + 1, period - 1)]
        out(1, j, jnp.concatenate([loads[tiles + j][:, 64:], after[:, :64]], 1))


def unpack_matrix(flat_ref, at, out_ref, wide_ref, tall_ref):
    height, breadth = out_ref.shape
    rows = TALL * breadth // 128
    shift = at % 16
    load = rows + (16 if shift else 0)

    @pl.loop(0, height // TALL)
    def _(k):
        first = pl.multiple_of(k * rows + (at - shift), 16)
        wide_ref[:load, :] = flat_ref[pl.ds(first, load), :].astype(F32)
        out_at = pl.multiple_of(k * TALL, TALL)

        def flat_at(j, count, stride):
            return wide_ref[pl.ds(shift + j, count, stride=stride), :]

        if breadth % 128:
            def put(parity, j, values):
                tall_ref[j, pl.ds(parity, TALL // 2, stride=2), :] = values

            line_up(flat_at, put, TALL, breadth)
            for j in range(breadth // 128 + 1):
                stop = min((j + 1) * 128, breadth)
                out_ref[pl.ds(out_at, TALL), j * 128 : stop] = tall_ref[
                    j, :, : stop - j * 128
                ].astype(BF16)
        else:
            def put(_, j, values):
                out_ref[pl.ds(out_at, TALL), j * 128 : (j + 1) * 128] = values.astype(BF16)

            line_up(flat_at, put, TALL, breadth)


def unpack_rows(everything, length, first_row, last_row, shapes, gaps, lead, tails):
    total = lax.axis_size("dp") * lax.axis_size("shard")
    starts = block_starts(length, total)
    per = GRAIN // 128
    moves, seams = [], []
    for owner in range(total):
        low = max(starts[owner] * per, first_row)
        high = min(starts[owner + 1] * per, last_row)
        if low < high:
            moves.append((owner, low - starts[owner] * per, low - first_row, high - low))
            if owner and low == starts[owner] * per:
                source = (starts[owner] - starts[owner - 1]) * per
                seams.append((owner - 1, source, low - first_row))
    outs = [jax.ShapeDtypeStruct(shape, BF16) for shape in shapes]
    outs += [jax.ShapeDtypeStruct((rows, 128), BF16) for _, rows in tails]
    wide_rows = TALL * max(shape[1] for shape in shapes) // 128 + 16
    height = last_row - first_row

    def kernel(all_ref, *refs):
        outs, (flat_ref, seam_ref, wide_ref, tall_ref, sems) = refs[:-5], refs[-5:]
        copies = [
            pltpu.make_async_copy(
                all_ref.at[owner, pl.ds(source, rows)], flat_ref.at[pl.ds(at, rows)], sems.at[k]
            )
            for k, (owner, source, at, rows) in enumerate(moves)
        ]
        edges = [
            pltpu.make_async_copy(
                all_ref.at[owner, pl.ds(source, per)],
                seam_ref.at[pl.ds(k * per, per)],
                sems.at[len(moves) + k],
            )
            for k, (owner, source, _) in enumerate(seams)
        ]
        for copy in edges + copies:
            copy.start()
        for copy in edges:
            copy.wait()
        arrived = 0
        at = lead

        def arrive(k):
            copies[k].wait()
            for j, (owner, _, row) in enumerate(seams):
                if owner == moves[k][0] - 1:
                    rows = slice(row, row + per)
                    flat_ref[rows, :] = flat_ref[rows, :] + seam_ref[j * per : (j + 1) * per, :]

        for k, (tall, wide) in enumerate(shapes):
            end = at + tall * wide // 128
            while arrived < len(moves) and moves[arrived][2] < end:
                arrive(arrived)
                arrived += 1
            unpack_matrix(flat_ref, at, outs[k], wide_ref, tall_ref)
            at = end + gaps.get(k, 0)
        for k in range(arrived, len(moves)):
            arrive(k)
        for k, (start, rows) in enumerate(tails):
            outs[len(shapes) + k][...] = flat_ref[pl.ds(start, rows), :]

    return pl.pallas_call(
        kernel,
        in_specs=[pl.BlockSpec(memory_space=pl.ANY)],
        out_specs=[pl.BlockSpec(memory_space=pltpu.VMEM)] * len(outs),
        out_shape=outs,
        scratch_shapes=[
            pltpu.VMEM((height, 128), BF16),
            pltpu.VMEM((len(seams) * per, 128), BF16),
            pltpu.VMEM((wide_rows, 128), F32),
            pltpu.VMEM((8, TALL, 128), F32),
            pltpu.SemaphoreType.DMA((len(moves) + len(seams),)),
        ],
        compiler_params=pltpu.CompilerParams(vmem_limit_bytes=VMEM_LIMIT),
        cost_estimate=pl.CostEstimate(flops=0, bytes_accessed=512 * height, transcendentals=0),
        name="unpack_rows",
    )(everything)


def pack_matrix(left_ref, right_ref, flat_ref, at, tall_ref):
    height, breadth = left_ref.shape[1], right_ref.shape[1]
    part = 512 if height % 512 == 0 else height
    tiles, odd = breadth // 128, breadth % 128
    for k in range(height // part):
        first = at + k * part * breadth // 128
        product = against(left_ref[:, k * part : (k + 1) * part], right_ref[...])
        for j in range(tiles + (1 if odd else 0)):
            stop = min((j + 1) * 128, breadth)
            tall_ref[j, :part, : stop - j * 128] = product[:, j * 128 : stop]
        if not odd:
            for j in range(tiles):
                flat_ref[pl.ds(first + j, part, stride=tiles), :] = tall_ref[j, :part, :]
            continue
        period = 2 * tiles + 1
        count = part // 2

        def half(parity, j):
            return tall_ref[j, pl.ds(parity, count, stride=2), :]

        for j in range(tiles):
            flat_ref[pl.ds(first + j, count, stride=period), :] = half(0, j)
        flat_ref[pl.ds(first + tiles, count, stride=period), :] = jnp.concatenate(
            [half(0, tiles)[:, :64], half(1, 0)[:, :64]], 1
        )
        for j in range(tiles):
            flat_ref[pl.ds(first + tiles + 1 + j, count, stride=period), :] = jnp.concatenate(
                [half(1, j)[:, 64:], half(1, j + 1)[:, :64]], 1
            )


def pack_kernel(info_ref, *refs, pairs, loose, early, lead, gaps, count, sub_rows, keep, first_loose):
    lefts, rights, refs = refs[:pairs], refs[pairs : 2 * pairs], refs[2 * pairs :]
    loose_refs, refs = refs[:loose], refs[loose:]
    if early:
        early_ref, refs = refs[0], refs[1:]
    own_ref, send_ref, refs = refs[0], refs[1], refs[2:]
    if keep:
        keep_ref, refs = refs[0], refs[1:]
    flat_ref, low_ref, tall_ref, sems = refs
    height = flat_ref.shape[0]
    at = lead
    for k in range(pairs):
        pack_matrix(lefts[k], rights[k], flat_ref, at, tall_ref)
        at += lefts[k].shape[1] * rights[k].shape[1] // 128
        if k in gaps:
            flat_ref[at : at + gaps[k], :] = loose_refs[list(gaps).index(k)][...]
            at += gaps[k]
    if early:
        flat_ref[at : at + early, :] = early_ref[...].astype(F32)[first_loose : first_loose + early]
        at += early
    if at < height:
        flat_ref[at:height, :] = jnp.zeros((height - at, 128), F32)
    step = 16 * 32
    for row in range(0, height, step):
        rows = min(step, height - row)
        low_ref[row : row + rows, :] = flat_ref[row : row + rows, :].astype(BF16)
    copies = []
    for idx in range(count):
        for k, ref in enumerate((own_ref, send_ref)):
            row = pl.multiple_of(info_ref[k * count + idx], 16)
            copies.append(
                pltpu.make_async_copy(
                    low_ref.at[pl.ds(row, sub_rows)], ref.at[idx], sems.at[k * count + idx]
                )
            )
    for copy in copies:
        copy.start()
    if keep:
        keep_ref[...] = low_ref[:keep, :]
    for copy in copies:
        copy.wait()


def pack_half(info, pairs, loose, early, lead, gaps, height, sub_rows, keep, skip):
    count = info.shape[0] // 2
    lefts = [left for left, _ in pairs]
    rights = [right for _, right in pairs]
    in_place = pl.BlockSpec(memory_space=pltpu.VMEM)
    anywhere = pl.BlockSpec(memory_space=pl.ANY)
    operands = lefts + rights + loose + ([early[0]] if early is not None else [])
    outs = [jax.ShapeDtypeStruct((count, sub_rows, 128), BF16)] * 2
    specs = [anywhere] * 2
    if keep:
        outs.append(jax.ShapeDtypeStruct((keep, 128), BF16))
        specs.append(in_place)

    def kernel(info_ref, *refs):
        pack_kernel(
            info_ref, *refs, pairs=len(pairs), loose=len(loose),
            early=0 if early is None else early[1], lead=lead, gaps=gaps,
            count=count, sub_rows=sub_rows, keep=keep, first_loose=skip,
        )

    return pl.pallas_call(
        kernel,
        in_specs=[pl.BlockSpec(memory_space=pltpu.SMEM)] + [in_place] * len(operands),
        out_specs=specs,
        out_shape=outs,
        scratch_shapes=[
            pltpu.VMEM((height, 128), F32),
            pltpu.VMEM((height, 128), BF16),
            pltpu.VMEM((max(right.shape[1] for right in rights) // 128, MODEL_WIDTH, 128), F32),
            pltpu.SemaphoreType.DMA((2 * count,)),
        ],
        compiler_params=pltpu.CompilerParams(vmem_limit_bytes=VMEM_LIMIT),
        cost_estimate=pl.CostEstimate(
            flops=0, bytes_accessed=32 * height, transcendentals=0
        ),
        name="pack_half",
    )(info, *operands)


def owner_rows(length, which, first_row):
    dp_size, shard_size = lax.axis_size("dp"), lax.axis_size("shard")
    sub_rows = owner_sub_rows(length)
    per = GRAIN // 128
    j = jnp.arange(2)[:, None, None]
    x = jnp.arange(dp_size // 4)[None, :, None]
    z = jnp.arange(shard_size)[None, None, :]
    rows = []
    for core in (dp_bit(1), 1 - dp_bit(1)):
        owner = ((which * (dp_size // 4) + x) * 2 + core) * shard_size + z
        rows.append((length * owner // GRAIN * per + sub_rows * j - first_row).reshape(-1))
    return jnp.concatenate(rows).astype(jnp.int32)


def owner_sub_rows(length):
    blocks = -(-(GRAIN - 1 + length) // GRAIN)
    return (blocks + blocks % 2) * (GRAIN // 128) // 2


def half_cubes(own, got):
    shard_size = lax.axis_size("shard")
    paired = (own.astype(F32) + got.astype(F32)).astype(BF16)
    paired = paired.reshape((-1, shard_size) + own.shape[1:])
    half = shard_size // 2
    order = high_bits()
    return [Cube(paired[:, :half], order), Cube(paired[:, half:], order[::-1])]


def own_part(sums_zero, sums_one, length):
    done = ring_reduce(jnp.stack([sums_zero, sums_one], 1).astype(BF16))
    top = dp_bit(top_bit())
    got = flip_dp(pick(done, 1 - top, 0).astype(BF16), top_bit()).astype(F32)
    own = pick(done, top, 0)
    both = jnp.where(top == 0, jnp.concatenate([own, got], 0), jnp.concatenate([got, own], 0))
    shift = (length * lax.axis_index(("dp", "shard"))) % GRAIN
    return lax.dynamic_slice_in_dim(both.reshape(-1), shift, length, 0)


class TableGather:
    def __init__(self, embed_table):
        low = embed_table.astype(BF16)
        half = low.shape[1] // 2
        core = dp_bit(1)
        own = lax.dynamic_slice_in_dim(low, core * half, half, 1)
        send = lax.dynamic_slice_in_dim(low, (1 - core) * half, half, 1)
        pair = join(own, flip_dp(send, 1), 1, 0)
        self.bits = sorted(high_bits(), reverse=True)
        shape = (1,) * len(self.bits) + (pair.shape[0], half // 2)
        self.sides = [pair[:, : half // 2].reshape(shape), pair[:, half // 2 :].reshape(shape)]
        self.orders = [high_bits(), high_bits()[::-1]]
        self.start()

    def start(self):
        self.got = [flip_dp(side, order[0]) for side, order in zip(self.sides, self.orders)]

    def step(self):
        self.sides = [
            join(side, other, order[0], self.bits.index(order[0]))
            for side, other, order in zip(self.sides, self.got, self.orders)
        ]
        self.orders = [order[1:] for order in self.orders]
        if self.orders[0]:
            self.start()

    def tied(self, main):
        main, self.got = lax.optimization_barrier((main, self.got))
        return main

    def finish(self):
        while self.orders[0]:
            self.step()
        return jnp.concatenate([side.reshape(MODEL_WIDTH, -1) for side in self.sides], 1)


def owner_flip(joined, features):
    core = dp_bit(1)
    send = lax.dynamic_slice_in_dim(joined, (1 - core) * features, features, 0)
    return flip_dp(send, 1)


def owner_join(joined, got, features):
    own = lax.dynamic_slice_in_dim(joined, dp_bit(1) * features, features, 0)
    return join(own, got, 1, 1)


def rms_scale(values):
    return lax.rsqrt(jnp.mean(values * values, axis=-1, keepdims=True) + EPSILON)


def rms_back(values, scale, gain, grad):
    weighted = grad * gain
    inner = jnp.sum(weighted * values, axis=-1, keepdims=True)
    grad_values = scale * weighted - values * (scale * scale * scale * inner / MODEL_WIDTH)
    grad_gain = jnp.sum(grad * values * scale, axis=0)
    return grad_values, grad_gain


def rope_rows(rows):
    halves = HEAD_SIZE // 2
    inverse = ROPE_BASE ** (-jnp.arange(halves, dtype=F32) * 2.0 / HEAD_SIZE)
    angles = jnp.arange(LEN, dtype=F32)[:, None] * inverse[None, :]
    cosine, sine = jnp.cos(angles), jnp.sin(angles)
    heads = ROPED // HEAD_SIZE
    cos_full = jnp.tile(jnp.concatenate([cosine, cosine], 1), (rows // LEN, heads))
    sin_full = jnp.tile(jnp.concatenate([-sine, sine], 1), (rows // LEN, heads))
    return cos_full, sin_full


def against(left, right):
    return lax.dot_general(left, right, (((0,), (0,)), ((), ())), preferred_element_type=F32)


def times_t(left, right):
    return lax.dot_general(left, right, (((1,), (1,)), ((), ())), preferred_element_type=F32)


QUERY_WIDTH = QUERY_HEADS * HEAD_SIZE
VALUE_WIDTH = KEY_VALUE_HEADS * HEAD_SIZE
SCALING = HEAD_SIZE ** (-0.5)


def swap_halves(values):
    halves, width = HEAD_SIZE // 2, values.shape[1]
    lanes = lax.broadcasted_iota(jnp.int32, values.shape, 1) % HEAD_SIZE
    return jnp.where(
        lanes < halves, pltpu.roll(values, width - halves, 1), pltpu.roll(values, halves, 1)
    )


def head_cols(idx):
    return slice(idx * HEAD_SIZE, (idx + 1) * HEAD_SIZE)


def attention_probs(query, key, allowed):
    scores = jnp.where(allowed, times_t(query, key) * SCALING, MASKED_SCORE)
    powers = jnp.exp(scores - jnp.max(scores, axis=1, keepdims=True))
    return powers / jnp.sum(powers, axis=1, keepdims=True)


def allowed_pairs(length):
    later = lax.broadcasted_iota(jnp.int32, (LEN, LEN), 0)
    sooner = lax.broadcasted_iota(jnp.int32, (LEN, LEN), 1)
    return (sooner <= later) & (sooner < length)


def forward_kernel(
    len_ref, hidden_ref, qkv_ref, out_ref, gateup_ref, down_ref, gain_ref, cos_ref, sin_ref,
    output_ref, normed_ref, turned_ref, value_ref, attended_ref, middle_ref, normed_two_ref,
    gate_up_ref, acted_ref,
):
    hidden = hidden_ref[...]
    normed_ref[...] = (hidden * rms_scale(hidden) * gain_ref[0:1, :]).astype(BF16)
    qkv = jnp.dot(normed_ref[...], qkv_ref[...], preferred_element_type=F32)
    straight = qkv[:, :ROPED]
    turned_ref[...] = (straight * cos_ref[...] + swap_halves(straight) * sin_ref[...]).astype(BF16)
    value_ref[...] = qkv[:, ROPED:].astype(BF16)
    group = QUERY_HEADS // KEY_VALUE_HEADS
    for seq in range(hidden.shape[0] // LEN):
        rows = slice(seq * LEN, (seq + 1) * LEN)
        allowed = allowed_pairs(len_ref[seq])
        for head in range(QUERY_HEADS):
            key = turned_ref[rows, head_cols(QUERY_HEADS + head // group)]
            value = value_ref[rows, head_cols(head // group)]
            probs = attention_probs(turned_ref[rows, head_cols(head)], key, allowed)
            attended_ref[rows, head_cols(head)] = jnp.dot(
                probs.astype(BF16), value, preferred_element_type=F32
            ).astype(BF16)
    middle = hidden + jnp.dot(attended_ref[...], out_ref[...], preferred_element_type=F32)
    middle_ref[...] = middle
    normed_two_ref[...] = (middle * rms_scale(middle) * gain_ref[1:2, :]).astype(BF16)
    gate_up_ref[...] = jnp.dot(normed_two_ref[...], gateup_ref[...], preferred_element_type=F32)
    gate = gate_up_ref[:, :FEED_UNITS]
    acted_ref[...] = (gate / (1.0 + jnp.exp(-gate)) * gate_up_ref[:, FEED_UNITS:]).astype(BF16)
    output_ref[...] = middle + jnp.dot(acted_ref[...], down_ref[...], preferred_element_type=F32)


def backward_kernel(
    len_ref, grad_ref, hidden_ref, qkv_ref, out_ref, gateup_ref, down_ref, gain_ref, cos_ref,
    sin_ref, turned_ref, value_ref, middle_ref, gate_up_ref,
    grad_in_ref, low_ref, grad_gu_ref, grad_mid_ref, grad_qkv_ref, gains_out_ref,
    grad_att_ref, grad_turned_ref,
):
    grad = grad_ref[...]
    low_ref[...] = grad.astype(BF16)
    grad_act = times_t(low_ref[...], down_ref[...]).astype(BF16).astype(F32)
    gate, up = gate_up_ref[:, :FEED_UNITS], gate_up_ref[:, FEED_UNITS:]
    sigma = 1.0 / (1.0 + jnp.exp(-gate))
    grad_gu_ref[:, FEED_UNITS:] = (grad_act * (gate * sigma)).astype(BF16)
    grad_gu_ref[:, :FEED_UNITS] = (
        grad_act * up * (sigma * (1.0 + gate * (1.0 - sigma)))
    ).astype(BF16)
    middle = middle_ref[...]
    grad_mid, gain_two = rms_back(
        middle, rms_scale(middle), gain_ref[1:2, :], times_t(grad_gu_ref[...], gateup_ref[...])
    )
    grad_mid = grad_mid + grad
    grad_mid_ref[...] = grad_mid.astype(BF16)
    grad_att_ref[...] = times_t(grad_mid_ref[...], out_ref[...]).astype(BF16)
    group = QUERY_HEADS // KEY_VALUE_HEADS
    for seq in range(grad.shape[0] // LEN):
        rows = slice(seq * LEN, (seq + 1) * LEN)
        allowed = allowed_pairs(len_ref[seq])
        for kv in range(KEY_VALUE_HEADS):
            key = turned_ref[rows, head_cols(QUERY_HEADS + kv)]
            value = value_ref[rows, head_cols(kv)]
            grad_key = jnp.zeros((LEN, HEAD_SIZE), F32)
            grad_value = jnp.zeros((LEN, HEAD_SIZE), F32)
            for head in range(kv * group, (kv + 1) * group):
                query = turned_ref[rows, head_cols(head)]
                grad_out = grad_att_ref[rows, head_cols(head)]
                probs = attention_probs(query, key, allowed)
                grad_probs = times_t(grad_out, value)
                grad_value = grad_value + against(probs.astype(BF16), grad_out)
                inner = jnp.sum(grad_probs * probs, axis=1, keepdims=True)
                grad_scores = (probs * (grad_probs - inner)).astype(BF16)
                grad_query = jnp.dot(grad_scores, key, preferred_element_type=F32) * SCALING
                grad_turned_ref[rows, head_cols(head)] = grad_query.astype(BF16).astype(F32)
                grad_key = grad_key + against(grad_scores, query)
            grad_turned_ref[rows, head_cols(QUERY_HEADS + kv)] = (
                (grad_key * SCALING).astype(BF16).astype(F32)
            )
            at = slice(ROPED + kv * HEAD_SIZE, ROPED + (kv + 1) * HEAD_SIZE)
            grad_qkv_ref[rows, at] = grad_value.astype(BF16)
    turned = grad_turned_ref[...]
    grad_qkv_ref[:, :ROPED] = (
        turned * cos_ref[...] - swap_halves(turned) * sin_ref[...]
    ).astype(BF16)
    hidden = hidden_ref[...]
    grad_hidden, gain_one = rms_back(
        hidden, rms_scale(hidden), gain_ref[0:1, :], times_t(grad_qkv_ref[...], qkv_ref[...])
    )
    grad_in_ref[...] = grad_hidden + grad_mid
    gains_out_ref[...] = jnp.concatenate([gain_one[None], gain_two[None]], 0)


def layer_call(kernel, name, lens, operands, outs, scratch, flops):
    in_place = pl.BlockSpec(memory_space=pltpu.VMEM)
    return pl.pallas_call(
        kernel,
        in_specs=[pl.BlockSpec(memory_space=pltpu.SMEM)] + [in_place] * len(operands),
        out_specs=[in_place] * len(outs),
        out_shape=[jax.ShapeDtypeStruct(shape, dtype) for shape, dtype in outs],
        scratch_shapes=scratch,
        compiler_params=pltpu.CompilerParams(vmem_limit_bytes=VMEM_LIMIT),
        cost_estimate=pl.CostEstimate(flops=flops, bytes_accessed=8 * PL, transcendentals=0),
        name=name,
    )(lens, *operands)


def layer_forward(hidden, pieces, lens, rope):
    rows = hidden.shape[0]
    outs = [
        ((rows, MODEL_WIDTH), F32),
        ((rows, MODEL_WIDTH), BF16),
        ((rows, ROPED), BF16),
        ((rows, VALUE_WIDTH), BF16),
        ((rows, QUERY_WIDTH), BF16),
        ((rows, MODEL_WIDTH), F32),
        ((rows, MODEL_WIDTH), BF16),
        ((rows, 2 * FEED_UNITS), F32),
        ((rows, FEED_UNITS), BF16),
    ]
    output, *kept = layer_call(
        forward_kernel, "layer_forward", lens, [hidden, *pieces, *rope], outs, [], 2 * rows * PL
    )
    return output, (hidden, *kept)


def layer_backward(kept, pieces, lens, rope, grad_output):
    hidden, normed, turned, value, attended, middle, normed_two, gate_up, acted = kept
    rows = hidden.shape[0]
    outs = [
        ((rows, MODEL_WIDTH), F32),
        ((rows, MODEL_WIDTH), BF16),
        ((rows, 2 * FEED_UNITS), BF16),
        ((rows, MODEL_WIDTH), BF16),
        ((rows, QKV), BF16),
        ((2, MODEL_WIDTH), F32),
    ]
    scratch = [pltpu.VMEM((rows, QUERY_WIDTH), BF16), pltpu.VMEM((rows, ROPED), F32)]
    operands = [grad_output, hidden, *pieces, *rope, turned, value, middle, gate_up]
    grad_input, low, grad_gu, grad_mid, grad_qkv, gains = layer_call(
        backward_kernel, "layer_backward", lens, operands, outs, scratch, 2 * rows * PL
    )
    pairs = [(normed, grad_qkv), (attended, grad_mid), (normed_two, grad_gu), (acted, low)]
    return grad_input, pairs, gains.reshape(-1, 128)


def flat_rows(first, second):
    return jnp.concatenate([first, second]).reshape(-1, 128)


def token_bits(tokens):
    return tokens.bit_length() - 1


def for_chunks(keys_ref, lines_ref, span_ref, columns, run):
    bits = token_bits(keys_ref.shape[0])
    base = span_ref[2]
    places = lax.broadcasted_iota(jnp.int32, (LANES, LANES), 1)

    def chunk_step(chunk, _):
        line = lines_ref[pl.ds(chunk, 1), :]
        ids = jnp.transpose(jnp.broadcast_to(lax.shift_right_logical(line, bits), (LANES, LANES)))
        low = lax.shift_right_logical(keys_ref[chunk * LANES], bits) - base
        high = lax.shift_right_logical(keys_ref[chunk * LANES + LANES - 1], bits) - base
        first = jnp.maximum(low, 0) // COLUMNS
        last = jnp.minimum(high, columns - 1) // COLUMNS

        def hot(block):
            parts = []
            for k in range(COLUMNS // LANES):
                match = ids - (base + block * COLUMNS + k * LANES) == places
                parts.append(jnp.where(match, 1.0, 0.0).astype(BF16))
            return jnp.concatenate(parts, 1)

        run(chunk, first, last + 1, hot)
        return 0

    lax.fori_loop(span_ref[0] // LANES, (span_ref[1] + LANES - 1) // LANES, chunk_step, 0)


def row_of(keys_ref, at):
    return keys_ref[at] & (keys_ref.shape[0] - 1)


def embed_kernel(keys_ref, span_ref, lines_ref, table_ref, out_ref, low_ref, rows_ref, found_ref):
    features, columns = table_ref.shape
    blocks, _, width = out_ref.shape
    low_ref[:features, :] = table_ref[...].astype(BF16)
    low_ref[features:, :] = jnp.zeros((LANES - features, columns), BF16)
    for k in range(blocks):
        rows_ref[k * width : (k + 1) * width, :] = jnp.zeros((width, LANES), F32)

    def run(chunk, first, last, hot):
        def block_step(block, total):
            at = pl.multiple_of(block * COLUMNS, COLUMNS)
            return total + times_t(hot(block), low_ref[:, pl.ds(at, COLUMNS)])

        found_ref[...] = lax.fori_loop(first, last, block_step, jnp.zeros((LANES, LANES), F32))

        def move(k, _):
            for j in range(8):
                row = row_of(keys_ref, chunk * LANES + k * 8 + j)
                rows_ref[pl.ds(row, 1), :] = found_ref[pl.ds(k * 8 + j, 1), :]
            return 0

        lax.fori_loop(0, LANES // 8, move, 0)

    for_chunks(keys_ref, lines_ref, span_ref, columns, run)

    def finish(k, _):
        at = pl.multiple_of(k * width, width)
        out_ref[k] = jnp.transpose(rows_ref[pl.ds(at, width), :])[:features].astype(BF16)
        return 0

    lax.fori_loop(0, blocks, finish, 0)


def embed_rows(keys, span, table, blocks):
    tokens = keys.shape[0]
    features, columns = table.shape
    scalars = pl.BlockSpec(memory_space=pltpu.SMEM)
    in_place = pl.BlockSpec(memory_space=pltpu.VMEM)
    return pl.pallas_call(
        embed_kernel,
        in_specs=[scalars, scalars, in_place, in_place],
        out_specs=in_place,
        out_shape=jax.ShapeDtypeStruct((blocks, features, tokens // blocks), BF16),
        scratch_shapes=[
            pltpu.VMEM((LANES, columns), BF16),
            pltpu.VMEM((tokens, LANES), F32),
            pltpu.VMEM((LANES, LANES), F32),
        ],
        compiler_params=pltpu.CompilerParams(vmem_limit_bytes=VMEM_LIMIT),
        cost_estimate=pl.CostEstimate(
            flops=2 * tokens * LANES * COLUMNS, bytes_accessed=4 * table.size, transcendentals=0
        ),
        name="embed_rows",
    )(keys, span, keys.reshape(-1, LANES), table)


def spread_kernel(keys_ref, span_ref, place_ref, lines_ref, *refs):
    parts, (base_ref, out_ref, rows_ref, packed_ref) = refs[:-4], refs[-4:]
    features, columns = base_ref.shape
    count, _, width = parts[0].shape
    for k, part in enumerate(parts):
        def unfold(j, _):
            at = pl.multiple_of(place_ref[k * count + j] * width, width)
            flat = part[j].astype(F32)
            flat = jnp.concatenate([flat, jnp.zeros((LANES - features, width), F32)], 0)
            rows_ref[pl.ds(at, width), :] = jnp.transpose(flat)
            return 0

        lax.fori_loop(0, count, unfold, 0)
    out_ref[...] = base_ref[...]

    def run(chunk, first, last, hot):
        def move(k, _):
            for j in range(8):
                row = row_of(keys_ref, chunk * LANES + k * 8 + j)
                packed_ref[pl.ds(k * 8 + j, 1), :] = rows_ref[pl.ds(row, 1), :]
            return 0

        lax.fori_loop(0, LANES // 8, move, 0)
        packed = packed_ref[...].astype(BF16)

        def block_step(block, _):
            at = pl.multiple_of(block * COLUMNS, COLUMNS)
            out_ref[:, pl.ds(at, COLUMNS)] += against(packed, hot(block))[:features]
            return 0

        lax.fori_loop(first, last, block_step, 0)

    for_chunks(keys_ref, lines_ref, span_ref, columns, run)


def spread_rows(keys, span, places, parts, base):
    tokens = keys.shape[0]
    scalars = pl.BlockSpec(memory_space=pltpu.SMEM)
    in_place = pl.BlockSpec(memory_space=pltpu.VMEM)
    return pl.pallas_call(
        spread_kernel,
        in_specs=[scalars] * 3 + [in_place] * (2 + len(parts)),
        out_specs=in_place,
        out_shape=jax.ShapeDtypeStruct(base.shape, F32),
        scratch_shapes=[
            pltpu.VMEM((tokens, LANES), F32),
            pltpu.VMEM((LANES, LANES), F32),
        ],
        compiler_params=pltpu.CompilerParams(vmem_limit_bytes=VMEM_LIMIT),
        cost_estimate=pl.CostEstimate(
            flops=2 * tokens * LANES * COLUMNS, bytes_accessed=8 * base.size, transcendentals=0
        ),
        name="spread_rows",
    )(keys, span, places, keys.reshape(-1, LANES), *parts, base)


def second_kernel(rows_ref, weight_ref, gain_ref, both_ref, projected_ref):
    projected = jnp.dot(rows_ref[...], weight_ref[...], preferred_element_type=F32)
    projected_ref[...] = projected
    both_ref[0] = rows_ref[...]
    both_ref[1] = (projected * rms_scale(projected) * gain_ref[...]).astype(BF16)


def second_head(rows, weight, gain):
    count = rows.shape[0]
    return pl.pallas_call(
        second_kernel,
        grid=(count // BLOCK,),
        in_specs=[
            pl.BlockSpec((BLOCK, MODEL_WIDTH), lambda i: (i, 0)),
            pl.BlockSpec(weight.shape, lambda i: (0, 0)),
            pl.BlockSpec(gain.shape, lambda i: (0, 0)),
        ],
        out_specs=[
            pl.BlockSpec((2, BLOCK, MODEL_WIDTH), lambda i: (0, i, 0)),
            pl.BlockSpec((BLOCK, MODEL_WIDTH), lambda i: (i, 0)),
        ],
        out_shape=[
            jax.ShapeDtypeStruct((2, count, MODEL_WIDTH), BF16),
            jax.ShapeDtypeStruct((count, MODEL_WIDTH), F32),
        ],
        compiler_params=pltpu.CompilerParams(vmem_limit_bytes=VMEM_LIMIT),
        cost_estimate=pl.CostEstimate(
            flops=2 * count * weight.size, bytes_accessed=10 * rows.size, transcendentals=0
        ),
        name="second_head",
    )(rows, weight, gain)


def block_count(count_ref):
    per = BLOCK // GRANULE
    return (count_ref[0] + per - 1) // per


def block_at(i, count_ref, list_ref):
    return (jnp.minimum(i, jnp.maximum(block_count(count_ref) - 1, 0)), 0)


def head_kernel(
    count_ref, list_ref, rows_ref, table_ref,
    exp_ref, back_ref, sum_ref, peak_ref,
    packed, even, odd,
):
    columns = table_ref.shape[1]
    chunk = even.shape[1]
    chunks = columns // chunk
    logits = (even, odd)
    per = BLOCK // GRANULE
    block = pl.program_id(0)

    @pl.when(block == 0)
    def _():
        back_ref[...] = jnp.zeros(back_ref.shape, F32)
        sum_ref[...] = jnp.ones(sum_ref.shape, F32)
        peak_ref[...] = jnp.zeros(peak_ref.shape, F32)

    def spot(g):
        return pl.multiple_of(list_ref[block * per + g] * GRANULE, GRANULE)

    def dot_chunk(k):
        return jnp.dot(
            packed[...], table_ref[:, k * chunk : (k + 1) * chunk], preferred_element_type=F32
        )

    def put(stat_ref, line):
        for g in range(per):
            lane = g * GRANULE // 128 * 128
            part = line[:, lane : lane + 128]
            if g * GRANULE % 128:
                part = pltpu.roll(part, 128 - g * GRANULE % 128, 1)
            stat_ref[pl.ds(list_ref[block * per + g], 1), :] = part

    def run(peak):
        total = jnp.zeros((BLOCK, 128), F32)
        logits[0][...] = dot_chunk(0)
        for k in range(chunks):
            if k + 1 < chunks:
                logits[(k + 1) % 2][...] = dot_chunk(k + 1)
            here = logits[k % 2][...]
            powers = jnp.exp(here if peak is None else here - peak)
            for j in range(chunk // 128):
                total = total + powers[:, j * 128 : (j + 1) * 128]
            exp_ref[:, k * chunk : (k + 1) * chunk] = powers.astype(BF16)
        line = jnp.sum(jnp.transpose(total), axis=0, keepdims=True)
        put(sum_ref, line)
        back = times_t(exp_ref[...], table_ref[...])
        for g in range(per):
            back_ref[pl.ds(spot(g), GRANULE), :] = back[g * GRANULE : (g + 1) * GRANULE]
        return line

    @pl.when(block < block_count(count_ref))
    def _():
        for g in range(per):
            packed[g * GRANULE : (g + 1) * GRANULE, :] = rows_ref[pl.ds(spot(g), GRANULE), :]
        sums = run(None)
        fits = jnp.min(jnp.where((sums > 1e-20) & (sums < 1e30), 1.0, 0.0))

        @pl.when(fits < 0.5)
        def _():
            wide = jnp.full((BLOCK, 128), -jnp.inf, F32)
            for k in range(chunks):
                here = dot_chunk(k)
                for j in range(chunk // 128):
                    wide = jnp.maximum(wide, here[:, j * 128 : (j + 1) * 128])
            put(peak_ref, jnp.max(jnp.transpose(wide), axis=0, keepdims=True))
            run(jnp.max(wide, axis=1, keepdims=True))


def head_forward(count, order, rows, table):
    height, columns = rows.shape[0], table.shape[1]
    granules = height // GRANULE
    chunk = min(CHUNK // 2, columns // 2)
    whole = pl.Buffered(1)

    def once(i, count_ref, list_ref):
        return (0, 0)

    return pl.pallas_call(
        head_kernel,
        grid_spec=pltpu.PrefetchScalarGridSpec(
            num_scalar_prefetch=2,
            grid=(height // BLOCK,),
            in_specs=[
                pl.BlockSpec(rows.shape, once, pipeline_mode=whole),
                pl.BlockSpec(table.shape, once, pipeline_mode=whole),
            ],
            out_specs=[
                pl.BlockSpec((BLOCK, columns), block_at),
                pl.BlockSpec((height, MODEL_WIDTH), once, pipeline_mode=whole),
                pl.BlockSpec((granules, 128), once),
                pl.BlockSpec((granules, 128), once),
            ],
            scratch_shapes=[
                pltpu.VMEM((BLOCK, MODEL_WIDTH), BF16),
                pltpu.VMEM((BLOCK, chunk), F32),
                pltpu.VMEM((BLOCK, chunk), F32),
            ],
        ),
        out_shape=[
            jax.ShapeDtypeStruct((height, columns), BF16),
            jax.ShapeDtypeStruct((height, MODEL_WIDTH), F32),
            jax.ShapeDtypeStruct((granules, 128), F32),
            jax.ShapeDtypeStruct((granules, 128), F32),
        ],
        compiler_params=pltpu.CompilerParams(vmem_limit_bytes=VMEM_LIMIT),
        cost_estimate=pl.CostEstimate(
            flops=4 * height * table.size,
            bytes_accessed=2 * height * columns,
            transcendentals=height * columns,
        ),
        name="head_forward",
    )(count, order, rows, table)


def scale_kernel(
    count_ref, list_ref, rows_ref, back_ref, scale_ref, grad_ref, turned_ref, scaled, packed
):
    per = STEP // GRANULE
    step, blocks = pl.program_id(0), pl.num_programs(0) // 2

    @pl.when(step < blocks)
    def _():
        for k in range(STEP // LANES):
            at = slice(k * LANES, (k + 1) * LANES)
            line = scale_ref[pl.ds(step * (STEP // LANES) + k, 1), :]
            column = jnp.transpose(jnp.broadcast_to(line, (LANES, LANES)))[:, :1]
            grad_ref[at, :] = back_ref[at, :] * column
            row = pl.multiple_of(step * STEP + k * LANES, LANES)
            scaled[pl.ds(row, LANES), :] = (rows_ref[at, :].astype(F32) * column).astype(BF16)

    block = step - blocks

    @pl.when((block >= 0) & (block * per < count_ref[0]))
    def _():
        for g in range(per):
            at = block * per + g
            spot = pl.multiple_of(list_ref[at] * GRANULE, GRANULE)
            part = scaled[pl.ds(spot, GRANULE), :].astype(F32)
            packed[g * GRANULE : (g + 1) * GRANULE, :] = jnp.where(
                at < count_ref[0], part, jnp.zeros_like(part)
            )
        turned_ref[...] = jnp.transpose(packed[...]).astype(BF16)


def scale_rows(count, order, rows, back, scale):
    height = rows.shape[0]
    blocks = height // STEP

    def first(i, count_ref, list_ref):
        return (jnp.minimum(i, blocks - 1), 0)

    def second(i, count_ref, list_ref):
        used = (count_ref[0] + STEP // GRANULE - 1) // (STEP // GRANULE)
        return (0, jnp.minimum(jnp.maximum(i - blocks, 0), jnp.maximum(used - 1, 0)))

    return pl.pallas_call(
        scale_kernel,
        grid_spec=pltpu.PrefetchScalarGridSpec(
            num_scalar_prefetch=2,
            grid=(2 * blocks,),
            in_specs=[
                pl.BlockSpec((STEP, MODEL_WIDTH), first),
                pl.BlockSpec((STEP, MODEL_WIDTH), first),
                pl.BlockSpec(scale.shape, lambda i, count_ref, list_ref: (0, 0)),
            ],
            out_specs=[
                pl.BlockSpec((STEP, MODEL_WIDTH), first),
                pl.BlockSpec((MODEL_WIDTH, STEP), second),
            ],
            scratch_shapes=[
                pltpu.VMEM((height, MODEL_WIDTH), BF16),
                pltpu.VMEM((STEP, MODEL_WIDTH), F32),
            ],
        ),
        out_shape=[
            jax.ShapeDtypeStruct((height, MODEL_WIDTH), F32),
            jax.ShapeDtypeStruct((MODEL_WIDTH, height), BF16),
        ],
        compiler_params=pltpu.CompilerParams(vmem_limit_bytes=VMEM_LIMIT),
        cost_estimate=pl.CostEstimate(flops=0, bytes_accessed=12 * rows.size, transcendentals=0),
        name="scale_rows",
    )(count, order, rows, back, scale)


def table_kernel(count_ref, turned_ref, exp_ref, out_ref, total):
    used = block_count(count_ref)
    most = exp_ref.shape[0] // BLOCK
    straight = most * 5 // 8

    @pl.when(used < straight)
    def _():
        total[...] = jnp.zeros(total.shape, F32)

        def step(k, _):
            at = pl.multiple_of(k * BLOCK, BLOCK)
            total[...] += jnp.dot(
                turned_ref[:, pl.ds(at, BLOCK)],
                exp_ref[pl.ds(at, BLOCK), :],
                preferred_element_type=F32,
            )
            return 0

        lax.fori_loop(0, used, step, 0)
        out_ref[...] = total[...].astype(BF16)

    for blocks in range(straight, most + 1):

        @pl.when(used == blocks)
        def _():
            out_ref[...] = jnp.dot(
                turned_ref[:, : blocks * BLOCK],
                exp_ref[: blocks * BLOCK, :],
                preferred_element_type=F32,
            ).astype(BF16)


def table_backward(count, turned, powers, part, parts):
    height, columns = powers.shape[0], powers.shape[1] // parts
    chunk = 512 if columns % 512 == 0 else 256
    steps = columns // chunk
    return pl.pallas_call(
        table_kernel,
        grid_spec=pltpu.PrefetchScalarGridSpec(
            num_scalar_prefetch=1,
            grid=(steps,),
            in_specs=[
                pl.BlockSpec(
                    turned.shape, lambda i, count_ref: (0, 0), pipeline_mode=pl.Buffered(1)
                ),
                pl.BlockSpec((height, chunk), lambda i, count_ref: (0, part * steps + i)),
            ],
            out_specs=pl.BlockSpec((MODEL_WIDTH, chunk), lambda i, count_ref: (0, i)),
            scratch_shapes=[pltpu.VMEM((MODEL_WIDTH, chunk), F32)],
        ),
        out_shape=jax.ShapeDtypeStruct((MODEL_WIDTH, columns), BF16),
        compiler_params=pltpu.CompilerParams(vmem_limit_bytes=VMEM_LIMIT),
        cost_estimate=pl.CostEstimate(
            flops=2 * MODEL_WIDTH * powers.size // parts,
            bytes_accessed=2 * powers.size // parts,
            transcendentals=0,
        ),
        name="table_backward",
    )(count, turned, powers)


def shards(
    token_ids,
    lengths,
    deal_order,
    embed_table,
    table_mom,
    table_avg,
    model_flat,
    model_mom,
    model_avg,
):
    dp_size, shard_size = lax.axis_size("dp"), lax.axis_size("shard")
    shard_idx, dp_idx = lax.axis_index("shard"), lax.axis_index("dp")
    device_idx = lax.axis_index(("dp", "shard"))
    core = dp_bit(1)
    seqs = token_ids.shape[0]
    own_rows = seqs * LEN
    group = 2 * shard_size
    groups = dp_size // 2
    slots = group * seqs
    seq_total = groups * slots
    target_count = jnp.float32((MEAN_LENGTH - 1) * seq_total)
    features, columns = embed_table.shape
    half = columns // 2
    vocab_start = shard_idx * columns + core * half
    length = model_flat.shape[0]

    tiny = jnp.concatenate([token_ids, jnp.broadcast_to(lengths[:, None], (seqs, LEN))], 0)
    tiny = tiny.reshape((1,) * (len(bits_below(dp_size)) + len(bits_below(shard_size))) + tiny.shape)
    for k, bit in enumerate(bits_below(dp_size)[::-1]):
        tiny = join(tiny, flip_dp(tiny, bit), bit, k)
    for k, bit in enumerate(bits_below(shard_size)[::-1]):
        other = flip_shard(tiny, bit)
        axis = len(bits_below(dp_size)) + k
        tiny = jnp.where(
            (shard_idx // bit) % 2 == 0,
            jnp.concatenate([tiny, other], axis),
            jnp.concatenate([other, tiny], axis),
        )
    tiny = tiny.reshape(dp_size * shard_size, 2 * seqs, LEN)
    all_ids = tiny[:, :seqs].reshape(seq_total, LEN)
    all_lens = tiny[:, seqs:, 0].reshape(seq_total)
    here = jnp.arange(seq_total)
    longer = all_lens[None, :] > all_lens[:, None]
    equal = (all_lens[None, :] == all_lens[:, None]) & (here[None, :] < here[:, None])
    rank = jnp.sum((longer | equal).astype(jnp.int32), axis=1)
    turn, seat = rank // groups, rank % groups
    group_of = jnp.where(turn % 2 == 0, seat, groups - 1 - seat)
    place_of = group_of * slots + turn
    hits = (place_of[None, :] == here[:, None]).astype(jnp.int32)
    seq_at = jnp.sum(hits * here[None, :], axis=1)
    dealt_ids = all_ids[seq_at]
    dealt_lens = jnp.sum(hits * all_lens[None, :], axis=1)
    my_group = dp_idx // 2
    group_ids = lax.dynamic_slice_in_dim(dealt_ids, my_group * slots, slots, 0)
    group_lens = lax.dynamic_slice_in_dim(dealt_lens, my_group * slots, slots, 0)
    own_at = core * shard_size + shard_idx
    own_lens = lax.dynamic_slice_in_dim(group_lens, own_at * seqs, seqs, 0)
    own_seqs = lax.dynamic_slice_in_dim(seq_at, (my_group * group + own_at) * seqs, seqs, 0)

    places = jnp.arange(LEN)
    weight_one = (places[None, :] + 1 < group_lens[:, None]).astype(F32)
    weight_two = SECOND_WEIGHT * (places[None, :] + 2 < group_lens[:, None]).astype(F32)
    weights = jnp.stack([weight_one, weight_two]) / target_count

    per_seq = LEN // GRANULE
    starts = jnp.arange(per_seq) * GRANULE
    useful = jnp.stack([starts[None, :] + k + 1 < group_lens[:, None] for k in range(2)])
    useful = useful.reshape(-1)
    index = jnp.arange(useful.shape[0])
    before = jnp.sum((useful[None, :] & (index[None, :] < index[:, None])).astype(jnp.int32), axis=1)
    count = jnp.sum(useful.astype(jnp.int32))
    last = jnp.max(jnp.where(useful, index, 0))
    found = useful[None, :] & (before[None, :] == index[:, None])
    order = jnp.sum(jnp.where(found, index[None, :], 0), axis=1)
    order = jnp.where(index < count, order, last).astype(jnp.int32)
    count = count.reshape(1)

    everything = lax.all_gather(own_blocks(model_flat), ("dp", "shard"))

    tokens = seq_total * LEN
    bits = token_bits(tokens)
    kept_ids = jnp.where(places[None, :] < dealt_lens[:, None], dealt_ids, columns * shard_size)
    keys = jnp.sort(kept_ids.reshape(-1) * tokens + jnp.arange(tokens, dtype=jnp.int32))
    first_id = shard_idx * columns
    span = jnp.stack(
        [
            jnp.sum((keys < first_id * tokens).astype(jnp.int32)),
            jnp.sum(((keys >> bits) < first_id + columns).astype(jnp.int32)),
            first_id,
        ]
    ).astype(jnp.int32)
    devices = dp_size * shard_size
    picked = embed_rows(keys, span, embed_table, devices)
    picked = picked.reshape(dp_size, shard_size, features, own_rows)
    mine = ring_reduce(picked.transpose(1, 0, 2, 3)).astype(BF16)
    parts = [pick(mine, dp_idx, 0)]
    parts += [flip_dp(pick(mine, dp_idx ^ k, 0), k) for k in range(1, dp_size)]
    embedded = jnp.stack(parts)[jnp.arange(dp_size) ^ dp_idx]
    embedded = embedded.reshape(MODEL_WIDTH, own_rows).T.astype(F32)

    held_table, everything, embedded = lax.optimization_barrier(
        (embed_table, everything, embedded)
    )
    table_gather = TableGather(held_table)
    middle_rows = PL // 128
    low_rows = middle_rows // 16 * 16
    total_devices = dp_size * shard_size
    per = GRAIN // 128
    end_row = block_starts(length, total_devices)[-1] * per
    tail = 2 * MODEL_WIDTH // 128
    square = MODEL_WIDTH * MODEL_WIDTH // 128
    *layer_zero, gains_zero = unpack_rows(
        everything, length, 0, low_rows + 16, LAYER_SHAPES, {}, 0, ((middle_rows - tail, 16),)
    )
    gain_row = middle_rows - low_rows + middle_rows - tail
    second_row = gain_row + tail + square
    base_one = gain_row // 16 * 16
    base_two = second_row // 16 * 16 - 16
    *layer_one, w_second, gains_one, gains_head = unpack_rows(
        everything, length, low_rows, end_row, LAYER_SHAPES + SQUARE, {3: tail},
        middle_rows - low_rows, ((base_one, 32), (base_two, 32)),
    )

    def gain_pair(rows, at):
        return rows[at : at + tail].reshape(2, MODEL_WIDTH)

    layer_zero.append(gain_pair(gains_zero, 0).astype(F32))
    layer_one.append(gain_pair(gains_one, gain_row - base_one).astype(F32))
    head_gains = gain_pair(gains_head, second_row - base_two).astype(F32)

    rope = rope_rows(own_rows)
    first_hidden = table_gather.tied(embedded)
    table_gather.step()
    hidden, kept_zero = layer_forward(first_hidden, layer_zero, own_lens, rope)
    hidden, kept_one = layer_forward(hidden, layer_one, own_lens, rope)
    scale_final = rms_scale(hidden)
    head_one = (hidden * scale_final * head_gains[0]).astype(BF16)
    all_one = group_gather(head_one, table_gather.tied).reshape(-1, MODEL_WIDTH)
    table_low = table_gather.finish()
    both, projected = second_head(all_one, w_second, head_gains[1:2])
    all_two = both[1]
    both = both.reshape(-1, MODEL_WIDTH)
    scale_second = rms_scale(projected)
    group_rows = all_one.shape[0]

    powers, back, sums, peaks = head_forward(count, order, both, table_low)
    sums = sums[:, :GRANULE].reshape(-1, 128)
    peaks = peaks[:, :GRANULE].reshape(-1, 128)
    sum_all_rows, peak_all = sums, peaks
    for flip, bits in ((flip_shard, bits_below(shard_size)), (flip_dp, [1])):
        for bit in bits:
            stats = flip(jnp.stack([sum_all_rows, peak_all]), bit)
            top = jnp.maximum(peak_all, stats[1])
            sum_all_rows = sum_all_rows * jnp.exp(peak_all - top) + stats[0] * jnp.exp(
                stats[1] - top
            )
            peak_all = top
    log_total = (peak_all + jnp.log(sum_all_rows)).reshape(2, group, seqs, LEN)
    row_scale = weights.reshape(-1, 128) * jnp.exp(peaks - peak_all) / sum_all_rows
    grad_rows, turned_rows = scale_rows(count, order, both, back, row_scale)

    own_log = pick(log_total, own_at, 1)
    own_weights = pick(weights.reshape(2, group, seqs, LEN), own_at, 1)
    words = embedded.reshape(seqs, LEN, MODEL_WIDTH)
    next_one = jnp.roll(words, -1, 1).reshape(own_rows, MODEL_WIDTH)
    next_two = jnp.roll(words, -2, 1).reshape(own_rows, MODEL_WIDTH)
    head_two = lax.dynamic_slice_in_dim(all_two, own_at * own_rows, own_rows, 0)
    chosen_one = jnp.sum(head_one.astype(F32) * next_one, axis=-1)
    chosen_two = jnp.sum(head_two.astype(F32) * next_two, axis=-1)
    chosen = jnp.stack([chosen_one, chosen_two]).reshape(2, seqs, LEN)
    own_loss = jnp.sum(own_weights * (own_log - chosen), axis=(0, 2))

    weight_col = own_weights.reshape(2, own_rows, 1)
    part_two = grad_rows[group_rows:]
    own_two = lax.dynamic_slice_in_dim(part_two, own_at * own_rows, own_rows, 0)
    part_two = lax.dynamic_update_slice_in_dim(
        part_two, own_two - weight_col[1] * next_two, own_at * own_rows, 0
    )
    grad_proj, grad_gain_second = rms_back(projected, scale_second, head_gains[1], part_two)
    grad_proj_low = grad_proj.astype(BF16)
    part_one = grad_rows[:group_rows] + times_t(grad_proj_low, w_second)
    quarters = 4
    cubes = [None] * quarters
    running = [turned_rows]

    def quarter_hook(k):
        def hook(got):
            part = table_backward(count, running[0], powers, k, quarters)
            got, part, running[0] = lax.optimization_barrier((got, part, running[0]))
            bits = high_bits() if k < quarters // 2 else high_bits()[::-1]
            cubes[k] = Cube(part.reshape(-1, 2 * features, part.shape[1]), bits)
            return got

        return hook

    grad_final = group_reduce(
        part_one.reshape(2, shard_size, own_rows, MODEL_WIDTH),
        [quarter_hook(k) for k in (0, 2, 1, 3)],
    )
    grad_final = grad_final - weight_col[0] * next_one
    grad_hidden, grad_gain_final = rms_back(hidden, scale_final, head_gains[0], grad_final)

    sub_rows = owner_sub_rows(length)
    height_zero = length * (total_devices // 2 - 1) // GRAIN * per + 2 * sub_rows
    height_one = length * (total_devices - 1) // GRAIN * per + 2 * sub_rows - low_rows
    keep = height_zero - low_rows
    grad_hidden = tie(grad_hidden, [cubes[0], cubes[2]])
    cubes[0].step(), cubes[2].step()
    grad_hidden, pairs, gain_grads = layer_backward(
        kept_one, layer_one, own_lens, rope, grad_hidden
    )
    gain_grads = tie(gain_grads, [cubes[1], cubes[3]])
    cubes[1].step(), cubes[3].step()
    own_one, send_one, kept_rows = pack_half(
        owner_rows(length, 1, low_rows),
        pairs + [(all_one, grad_proj_low)],
        [gain_grads, flat_rows(grad_gain_final, grad_gain_second)],
        None, middle_rows - low_rows, {3: tail, 4: tail}, height_one, sub_rows, keep, 0,
    )
    got_one = flip_dp(send_one, 1)
    grad_hidden, own_one, got_one = lax.optimization_barrier((grad_hidden, own_one, got_one))
    cubes_one = half_cubes(own_one, got_one)
    grad_hidden, pairs, gain_grads = layer_backward(
        kept_zero, layer_zero, own_lens, rope, grad_hidden
    )
    gain_grads = tie(gain_grads, cubes)
    joined = jnp.concatenate([cube.finish() for cube in cubes], 1)
    flipped = owner_flip(joined, features)
    own_zero, send_zero = pack_half(
        owner_rows(length, 0, 0), pairs, [gain_grads],
        (kept_rows, height_zero - middle_rows), 0, {3: tail}, height_zero, sub_rows, 0,
        middle_rows - low_rows,
    )
    one_terms = (weight_col[0] * head_one.astype(F32)).reshape(seqs, LEN, MODEL_WIDTH)
    two_terms = (weight_col[1] * head_two.astype(F32)).reshape(seqs, LEN, MODEL_WIDTH)
    token_grad = (
        grad_hidden.astype(BF16).astype(F32)
        - jnp.roll(one_terms, 1, 1).reshape(own_rows, MODEL_WIDTH)
        - jnp.roll(two_terms, 2, 1).reshape(own_rows, MODEL_WIDTH)
    ).astype(BF16)
    token_parts = token_grad.T.reshape(dp_size, features, own_rows)
    parts = [pick(token_parts, dp_idx, 0)]
    parts += [flip_dp(pick(token_parts, dp_idx ^ k, 0), k) for k in range(1, dp_size)]
    own_zero = tie(own_zero, cubes_one)
    for cube in cubes_one:
        cube.step()
    got_zero, parts, flipped = lax.optimization_barrier((flip_dp(send_zero, 1), parts, flipped))
    table_part = owner_join(joined, flipped, features)
    cubes_zero = half_cubes(own_zero, got_zero)
    chain = [jnp.stack(parts)]
    for k in range(shard_size - 1):
        chain.append(next_shard(chain[-1]))
        if k == 0:
            chain[-1] = tie(chain[-1], cubes_one)
            sums_one = jnp.concatenate([cube.finish() for cube in cubes_one], 0)
    chain[-1] = tie(chain[-1], cubes_zero)
    for cube in cubes_zero:
        cube.step()
    from_dp = (jnp.arange(dp_size) ^ dp_idx)[None, :]
    from_shard = (shard_idx - jnp.arange(shard_size))[:, None] % shard_size
    spots = (from_dp * shard_size + from_shard).reshape(-1).astype(jnp.int32)
    table_sum = spread_rows(keys, span, spots, chain, table_part)
    table_sum = tie(table_sum, cubes_zero)
    sums_zero = jnp.concatenate([cube.finish() for cube in cubes_zero], 0)
    model_sum = own_part(sums_zero, sums_one, length)

    square_sum = jnp.sum(table_sum * table_sum) + jnp.sum(model_sum * model_sum)
    losses = jnp.sum(
        jnp.where(own_seqs[:, None] == here[None, :], own_loss[:, None], 0.0), axis=0
    )
    totals = sum_all(jnp.concatenate([losses, square_sum.reshape(1)])[None])[0]
    grad_norm = jnp.sqrt(totals[seq_total])
    factor = jnp.minimum(1.0, CLIP_NORM / (grad_norm + 1e-06))
    all_loss = totals[:seq_total]
    loss_total = jnp.sum(all_loss)
    seq_loss = lax.dynamic_slice_in_dim(all_loss, device_idx * seqs, seqs, 0)
    own_slots = lax.dynamic_slice_in_dim(deal_order, device_idx * seqs, seqs, 0)
    slot_loss = all_loss[own_slots]

    results = []
    for weights_in, gradient, moment, average in (
        (embed_table, table_sum, table_mom, table_avg),
        (model_flat, model_sum, model_mom, model_avg),
    ):
        clipped = gradient * factor
        new_moment = MOMENTUM * moment + clipped
        new_weight = weights_in - LEARN_RATE * (clipped + MOMENTUM * new_moment)
        new_average = AVERAGE_KEEP * average + (1.0 - AVERAGE_KEEP) * new_weight
        results.append(
            (clipped, new_weight, new_moment, new_average, new_weight.astype(BF16))
        )
    return (loss_total, seq_loss, slot_loss, grad_norm) + results[0] + results[1]


def solution(mesh):
    both = P(("dp", "shard"))
    block = P("dp", "shard")
    return jax.shard_map(
        shards,
        mesh=mesh,
        in_specs=(P(("dp", "shard"), None), both, P(), block, block, block, both, both, both),
        out_specs=(P(), both, both, P()) + (block,) * 5 + (both,) * 5,
        check_vma=False,
    )
```

```python
import jax
import jax.numpy as jnp
from jax import lax
from jax.experimental import pallas as pl
from jax.experimental.pallas import tpu as pltpu
from jax.sharding import PartitionSpec as P

MODEL_WIDTH = 576
QUERY_HEADS = 9
KEY_VALUE_HEADS = 3
HEAD_SIZE = 64
FEED_UNITS = 1536
LAYERS = 2
LEN = 128
PL = 3540096
NP = 7413120
QKV = (QUERY_HEADS + 2 * KEY_VALUE_HEADS) * HEAD_SIZE
ROPED = (QUERY_HEADS + KEY_VALUE_HEADS) * HEAD_SIZE
MEAN_LENGTH = 96

EPSILON = 1e-05
ROPE_BASE = 100000.0
CLIP_NORM = 0.01
LEARN_RATE = 6000.0
MOMENTUM = 0.9
AVERAGE_KEEP = 0.9
SECOND_WEIGHT = 0.3
MASKED_SCORE = -1e30

GRAIN = 2048
GRANULE = 16
BLOCK = 256
STEP = 1024
CHUNK = 1024
LANES = 128
COLUMNS = 256
VMEM_LIMIT = 62 * 1024 * 1024
F32 = jnp.float32
BF16 = jnp.bfloat16


def flip_dp(values, bit):
    return lax.ppermute(values, "dp", [(i, i ^ bit) for i in range(lax.axis_size("dp"))])


def flip_shard(values, bit):
    return lax.ppermute(values, "shard", [(i, i ^ bit) for i in range(lax.axis_size("shard"))])


def next_shard(values):
    size = lax.axis_size("shard")
    return lax.ppermute(values, "shard", [(i, (i + 1) % size) for i in range(size)])


def bits_below(size):
    return [1 << k for k in range(size.bit_length() - 1)]


def dp_bit(bit):
    return (lax.axis_index("dp") // bit) % 2


def join(own, other, bit, axis):
    return jnp.where(
        dp_bit(bit) == 0,
        jnp.concatenate([own, other], axis),
        jnp.concatenate([other, own], axis),
    )


def pick(values, idx, axis):
    return lax.dynamic_index_in_dim(values, idx, axis, keepdims=False)


def high_bits():
    return bits_below(lax.axis_size("dp"))[1:]


def gather_cube(values, order):
    bits = sorted(order, reverse=True)
    out = values.reshape((1,) * len(bits) + values.shape)
    for bit in order:
        out = join(out, flip_dp(out, bit), bit, bits.index(bit))
    return out.reshape((-1,) + values.shape)


class Cube:
    def __init__(self, values, order):
        self.left = sorted(order, reverse=True)
        self.order = list(order)
        self.out = values.reshape((2,) * len(order) + values.shape[1:])
        self.start()

    def start(self):
        bit = self.order[0]
        axis = self.left.index(bit)
        mine = dp_bit(bit)
        self.got = flip_dp(pick(self.out, 1 - mine, axis).astype(BF16), bit)
        self.keep = pick(self.out, mine, axis)

    def step(self):
        self.out = self.keep.astype(F32) + self.got.astype(F32)
        self.left.remove(self.order.pop(0))
        if self.order:
            self.start()
        return bool(self.order)

    def finish(self):
        while self.order:
            self.step()
        return self.out


def tie(main, cubes):
    main, gots = lax.optimization_barrier((main, [cube.got for cube in cubes]))
    for cube, got in zip(cubes, gots):
        cube.got = got
    return main


def ring_reduce(values, hooks=()):
    size = lax.axis_size("shard")
    me = lax.axis_index("shard")
    total = None
    for step in range(size - 1):
        term = pick(values, (me - 1 - step) % size, 0).astype(F32)
        if total is not None:
            term = term + total
        got = next_shard(term.astype(BF16))
        if step < len(hooks):
            got = hooks[step](got)
        total = got.astype(F32)
    return total + pick(values, me, 0).astype(F32)


def ring_gather(values, hook=None):
    size = lax.axis_size("shard")
    me = lax.axis_index("shard")
    parts = [values]
    for k in range(size - 1):
        parts.append(next_shard(parts[-1]))
        if hook is not None and k == 1:
            parts[-1] = hook(parts[-1])
    stacked = jnp.stack(parts[::-1])
    return jnp.roll(stacked, me + 1, axis=0)


def group_gather(rows, hook=None):
    parts = ring_gather(rows, hook)
    other = flip_dp(parts, 1)
    return join(parts[None], other[None], 1, 0)


def group_reduce(parts, hooks):
    mine = dp_bit(1)
    got = hooks[0](flip_dp(pick(parts, 1 - mine, 0).astype(BF16), 1))
    return ring_reduce(pick(parts, mine, 0).astype(F32) + got.astype(F32), hooks[1:])


def sum_all(value):
    total = value
    for bit in bits_below(lax.axis_size("dp")):
        total = total + flip_dp(total, bit)
    for bit in bits_below(lax.axis_size("shard")):
        total = total + flip_shard(total, bit)
    return total


def top_bit():
    return high_bits()[-1]


def block_starts(length, total):
    return [length * i // GRAIN for i in range(total)] + [-(-length * total // GRAIN)]


def own_blocks(model_flat):
    length = model_flat.shape[0]
    total = lax.axis_size("dp") * lax.axis_size("shard")
    device = lax.axis_index(("dp", "shard"))
    low = model_flat.astype(BF16)
    starts = block_starts(length, total)
    blocks = max(starts[i + 1] - starts[i] for i in range(total)) + 1
    extended = jnp.pad(low, (GRAIN, 3 * GRAIN))
    shift = (length * device) % GRAIN
    whole = lax.dynamic_slice_in_dim(extended, GRAIN - shift, blocks * GRAIN, 0)
    return whole.reshape(-1, 128)


LAYER_SHAPES = (
    (MODEL_WIDTH, QKV),
    (MODEL_WIDTH, MODEL_WIDTH),
    (MODEL_WIDTH, 2 * FEED_UNITS),
    (FEED_UNITS, MODEL_WIDTH),
)
SQUARE = ((MODEL_WIDTH, MODEL_WIDTH),)
TALL = 64


def line_up(flat_at, out, height, breadth):
    tiles, odd = breadth // 128, breadth % 128
    if not odd:
        for j in range(tiles):
            out(0, j, flat_at(j, height, tiles))
        return
    period = 2 * tiles + 1
    loads = [flat_at(j, height // 2, period) for j in range(period)]
    for j in range(tiles + 1):
        out(0, j, loads[j])
        after = loads[min(tiles + j + 1, period - 1)]
        out(1, j, jnp.concatenate([loads[tiles + j][:, 64:], after[:, :64]], 1))


def unpack_matrix(flat_ref, at, out_ref, wide_ref, tall_ref):
    height, breadth = out_ref.shape
    rows = TALL * breadth // 128
    shift = at % 16
    load = rows + (16 if shift else 0)

    @pl.loop(0, height // TALL)
    def _(k):
        first = pl.multiple_of(k * rows + (at - shift), 16)
        wide_ref[:load, :] = flat_ref[pl.ds(first, load), :].astype(F32)
        out_at = pl.multiple_of(k * TALL, TALL)

        def flat_at(j, count, stride):
            return wide_ref[pl.ds(shift + j, count, stride=stride), :]

        if breadth % 128:
            def put(parity, j, values):
                tall_ref[j, pl.ds(parity, TALL // 2, stride=2), :] = values

            line_up(flat_at, put, TALL, breadth)
            for j in range(breadth // 128 + 1):
                stop = min((j + 1) * 128, breadth)
                out_ref[pl.ds(out_at, TALL), j * 128 : stop] = tall_ref[
                    j, :, : stop - j * 128
                ].astype(BF16)
        else:
            def put(_, j, values):
                out_ref[pl.ds(out_at, TALL), j * 128 : (j + 1) * 128] = values.astype(BF16)

            line_up(flat_at, put, TALL, breadth)


def unpack_rows(everything, length, first_row, last_row, shapes, gaps, lead, tails):
    total = lax.axis_size("dp") * lax.axis_size("shard")
    starts = block_starts(length, total)
    per = GRAIN // 128
    moves, seams = [], []
    for owner in range(total):
        low = max(starts[owner] * per, first_row)
        high = min(starts[owner + 1] * per, last_row)
        if low < high:
            moves.append((owner, low - starts[owner] * per, low - first_row, high - low))
            if owner and low == starts[owner] * per:
                source = (starts[owner] - starts[owner - 1]) * per
                seams.append((owner - 1, source, low - first_row))
    outs = [jax.ShapeDtypeStruct(shape, BF16) for shape in shapes]
    outs += [jax.ShapeDtypeStruct((rows, 128), BF16) for _, rows in tails]
    wide_rows = TALL * max(shape[1] for shape in shapes) // 128 + 16
    height = last_row - first_row

    def kernel(all_ref, *refs):
        outs, (flat_ref, seam_ref, wide_ref, tall_ref, sems) = refs[:-5], refs[-5:]
        copies = [
            pltpu.make_async_copy(
                all_ref.at[owner, pl.ds(source, rows)], flat_ref.at[pl.ds(at, rows)], sems.at[k]
            )
            for k, (owner, source, at, rows) in enumerate(moves)
        ]
        edges = [
            pltpu.make_async_copy(
                all_ref.at[owner, pl.ds(source, per)],
                seam_ref.at[pl.ds(k * per, per)],
                sems.at[len(moves) + k],
            )
            for k, (owner, source, _) in enumerate(seams)
        ]
        for copy in edges + copies:
            copy.start()
        for copy in edges:
            copy.wait()
        arrived = 0
        at = lead

        def arrive(k):
            copies[k].wait()
            for j, (owner, _, row) in enumerate(seams):
                if owner == moves[k][0] - 1:
                    rows = slice(row, row + per)
                    flat_ref[rows, :] = flat_ref[rows, :] + seam_ref[j * per : (j + 1) * per, :]

        for k, (tall, wide) in enumerate(shapes):
            end = at + tall * wide // 128
            while arrived < len(moves) and moves[arrived][2] < end:
                arrive(arrived)
                arrived += 1
            unpack_matrix(flat_ref, at, outs[k], wide_ref, tall_ref)
            at = end + gaps.get(k, 0)
        for k in range(arrived, len(moves)):
            arrive(k)
        for k, (start, rows) in enumerate(tails):
            outs[len(shapes) + k][...] = flat_ref[pl.ds(start, rows), :]

    return pl.pallas_call(
        kernel,
        in_specs=[pl.BlockSpec(memory_space=pl.ANY)],
        out_specs=[pl.BlockSpec(memory_space=pltpu.VMEM)] * len(outs),
        out_shape=outs,
        scratch_shapes=[
            pltpu.VMEM((height, 128), BF16),
            pltpu.VMEM((len(seams) * per, 128), BF16),
            pltpu.VMEM((wide_rows, 128), F32),
            pltpu.VMEM((8, TALL, 128), F32),
            pltpu.SemaphoreType.DMA((len(moves) + len(seams),)),
        ],
        compiler_params=pltpu.CompilerParams(vmem_limit_bytes=VMEM_LIMIT),
        cost_estimate=pl.CostEstimate(flops=0, bytes_accessed=512 * height, transcendentals=0),
        name="unpack_rows",
    )(everything)


def pack_matrix(left_ref, right_ref, flat_ref, at, tall_ref):
    height, breadth = left_ref.shape[1], right_ref.shape[1]
    part = 512 if height % 512 == 0 else height
    tiles, odd = breadth // 128, breadth % 128
    for k in range(height // part):
        first = at + k * part * breadth // 128
        product = against(left_ref[:, k * part : (k + 1) * part], right_ref[...])
        for j in range(tiles + (1 if odd else 0)):
            stop = min((j + 1) * 128, breadth)
            tall_ref[j, :part, : stop - j * 128] = product[:, j * 128 : stop]
        if not odd:
            for j in range(tiles):
                flat_ref[pl.ds(first + j, part, stride=tiles), :] = tall_ref[j, :part, :]
            continue
        period = 2 * tiles + 1
        count = part // 2

        def half(parity, j):
            return tall_ref[j, pl.ds(parity, count, stride=2), :]

        for j in range(tiles):
            flat_ref[pl.ds(first + j, count, stride=period), :] = half(0, j)
        flat_ref[pl.ds(first + tiles, count, stride=period), :] = jnp.concatenate(
            [half(0, tiles)[:, :64], half(1, 0)[:, :64]], 1
        )
        for j in range(tiles):
            flat_ref[pl.ds(first + tiles + 1 + j, count, stride=period), :] = jnp.concatenate(
                [half(1, j)[:, 64:], half(1, j + 1)[:, :64]], 1
            )


def pack_kernel(info_ref, *refs, pairs, loose, early, lead, gaps, count, sub_rows, keep, first_loose):
    lefts, rights, refs = refs[:pairs], refs[pairs : 2 * pairs], refs[2 * pairs :]
    loose_refs, refs = refs[:loose], refs[loose:]
    if early:
        early_ref, refs = refs[0], refs[1:]
    own_ref, send_ref, refs = refs[0], refs[1], refs[2:]
    if keep:
        keep_ref, refs = refs[0], refs[1:]
    flat_ref, low_ref, tall_ref, sems = refs
    height = flat_ref.shape[0]
    at = lead
    for k in range(pairs):
        pack_matrix(lefts[k], rights[k], flat_ref, at, tall_ref)
        at += lefts[k].shape[1] * rights[k].shape[1] // 128
        if k in gaps:
            flat_ref[at : at + gaps[k], :] = loose_refs[list(gaps).index(k)][...]
            at += gaps[k]
    if early:
        flat_ref[at : at + early, :] = early_ref[...].astype(F32)[first_loose : first_loose + early]
        at += early
    if at < height:
        flat_ref[at:height, :] = jnp.zeros((height - at, 128), F32)
    step = 16 * 32
    for row in range(0, height, step):
        rows = min(step, height - row)
        low_ref[row : row + rows, :] = flat_ref[row : row + rows, :].astype(BF16)
    copies = []
    for idx in range(count):
        for k, ref in enumerate((own_ref, send_ref)):
            row = pl.multiple_of(info_ref[k * count + idx], 16)
            copies.append(
                pltpu.make_async_copy(
                    low_ref.at[pl.ds(row, sub_rows)], ref.at[idx], sems.at[k * count + idx]
                )
            )
    for copy in copies:
        copy.start()
    if keep:
        keep_ref[...] = low_ref[:keep, :]
    for copy in copies:
        copy.wait()


def pack_half(info, pairs, loose, early, lead, gaps, height, sub_rows, keep, skip):
    count = info.shape[0] // 2
    lefts = [left for left, _ in pairs]
    rights = [right for _, right in pairs]
    in_place = pl.BlockSpec(memory_space=pltpu.VMEM)
    anywhere = pl.BlockSpec(memory_space=pl.ANY)
    operands = lefts + rights + loose + ([early[0]] if early is not None else [])
    outs = [jax.ShapeDtypeStruct((count, sub_rows, 128), BF16)] * 2
    specs = [anywhere] * 2
    if keep:
        outs.append(jax.ShapeDtypeStruct((keep, 128), BF16))
        specs.append(in_place)

    def kernel(info_ref, *refs):
        pack_kernel(
            info_ref, *refs, pairs=len(pairs), loose=len(loose),
            early=0 if early is None else early[1], lead=lead, gaps=gaps,
            count=count, sub_rows=sub_rows, keep=keep, first_loose=skip,
        )

    return pl.pallas_call(
        kernel,
        in_specs=[pl.BlockSpec(memory_space=pltpu.SMEM)] + [in_place] * len(operands),
        out_specs=specs,
        out_shape=outs,
        scratch_shapes=[
            pltpu.VMEM((height, 128), F32),
            pltpu.VMEM((height, 128), BF16),
            pltpu.VMEM((max(right.shape[1] for right in rights) // 128, MODEL_WIDTH, 128), F32),
            pltpu.SemaphoreType.DMA((2 * count,)),
        ],
        compiler_params=pltpu.CompilerParams(vmem_limit_bytes=VMEM_LIMIT),
        cost_estimate=pl.CostEstimate(
            flops=0, bytes_accessed=32 * height, transcendentals=0
        ),
        name="pack_half",
    )(info, *operands)


def owner_rows(length, which, first_row):
    dp_size, shard_size = lax.axis_size("dp"), lax.axis_size("shard")
    sub_rows = owner_sub_rows(length)
    per = GRAIN // 128
    j = jnp.arange(2)[:, None, None]
    x = jnp.arange(dp_size // 4)[None, :, None]
    z = jnp.arange(shard_size)[None, None, :]
    rows = []
    for core in (dp_bit(1), 1 - dp_bit(1)):
        owner = ((which * (dp_size // 4) + x) * 2 + core) * shard_size + z
        rows.append((length * owner // GRAIN * per + sub_rows * j - first_row).reshape(-1))
    return jnp.concatenate(rows).astype(jnp.int32)


def owner_sub_rows(length):
    blocks = -(-(GRAIN - 1 + length) // GRAIN)
    return (blocks + blocks % 2) * (GRAIN // 128) // 2


def half_cubes(own, got):
    shard_size = lax.axis_size("shard")
    paired = (own.astype(F32) + got.astype(F32)).astype(BF16)
    paired = paired.reshape((-1, shard_size) + own.shape[1:])
    half = shard_size // 2
    order = high_bits()
    return [Cube(paired[:, :half], order), Cube(paired[:, half:], order[::-1])]


def own_part(sums_zero, sums_one, length):
    done = ring_reduce(jnp.stack([sums_zero, sums_one], 1).astype(BF16))
    top = dp_bit(top_bit())
    got = flip_dp(pick(done, 1 - top, 0).astype(BF16), top_bit()).astype(F32)
    own = pick(done, top, 0)
    both = jnp.where(top == 0, jnp.concatenate([own, got], 0), jnp.concatenate([got, own], 0))
    shift = (length * lax.axis_index(("dp", "shard"))) % GRAIN
    return lax.dynamic_slice_in_dim(both.reshape(-1), shift, length, 0)


class TableGather:
    def __init__(self, embed_table):
        low = embed_table.astype(BF16)
        half = low.shape[1] // 2
        core = dp_bit(1)
        own = lax.dynamic_slice_in_dim(low, core * half, half, 1)
        send = lax.dynamic_slice_in_dim(low, (1 - core) * half, half, 1)
        pair = join(own, flip_dp(send, 1), 1, 0)
        self.bits = sorted(high_bits(), reverse=True)
        shape = (1,) * len(self.bits) + (pair.shape[0], half // 2)
        self.sides = [pair[:, : half // 2].reshape(shape), pair[:, half // 2 :].reshape(shape)]
        self.orders = [high_bits(), high_bits()[::-1]]
        self.start()

    def start(self):
        self.got = [flip_dp(side, order[0]) for side, order in zip(self.sides, self.orders)]

    def step(self):
        self.sides = [
            join(side, other, order[0], self.bits.index(order[0]))
            for side, other, order in zip(self.sides, self.got, self.orders)
        ]
        self.orders = [order[1:] for order in self.orders]
        if self.orders[0]:
            self.start()

    def tied(self, main):
        main, self.got = lax.optimization_barrier((main, self.got))
        return main

    def finish(self):
        while self.orders[0]:
            self.step()
        return jnp.concatenate([side.reshape(MODEL_WIDTH, -1) for side in self.sides], 1)


def owner_flip(joined, features):
    core = dp_bit(1)
    send = lax.dynamic_slice_in_dim(joined, (1 - core) * features, features, 0)
    return flip_dp(send, 1)


def owner_join(joined, got, features):
    own = lax.dynamic_slice_in_dim(joined, dp_bit(1) * features, features, 0)
    return join(own, got, 1, 1)


def rms_scale(values):
    return lax.rsqrt(jnp.mean(values * values, axis=-1, keepdims=True) + EPSILON)


def rms_back(values, scale, gain, grad):
    weighted = grad * gain
    inner = jnp.sum(weighted * values, axis=-1, keepdims=True)
    grad_values = scale * weighted - values * (scale * scale * scale * inner / MODEL_WIDTH)
    grad_gain = jnp.sum(grad * values * scale, axis=0)
    return grad_values, grad_gain


def rope_rows(rows):
    halves = HEAD_SIZE // 2
    inverse = ROPE_BASE ** (-jnp.arange(halves, dtype=F32) * 2.0 / HEAD_SIZE)
    angles = jnp.arange(LEN, dtype=F32)[:, None] * inverse[None, :]
    cosine, sine = jnp.cos(angles), jnp.sin(angles)
    heads = ROPED // HEAD_SIZE
    cos_full = jnp.tile(jnp.concatenate([cosine, cosine], 1), (rows // LEN, heads))
    sin_full = jnp.tile(jnp.concatenate([-sine, sine], 1), (rows // LEN, heads))
    return cos_full, sin_full


def against(left, right):
    return lax.dot_general(left, right, (((0,), (0,)), ((), ())), preferred_element_type=F32)


def times_t(left, right):
    return lax.dot_general(left, right, (((1,), (1,)), ((), ())), preferred_element_type=F32)


QUERY_WIDTH = QUERY_HEADS * HEAD_SIZE
VALUE_WIDTH = KEY_VALUE_HEADS * HEAD_SIZE
SCALING = HEAD_SIZE ** (-0.5)


def swap_halves(values):
    halves, width = HEAD_SIZE // 2, values.shape[1]
    lanes = lax.broadcasted_iota(jnp.int32, values.shape, 1) % HEAD_SIZE
    return jnp.where(
        lanes < halves, pltpu.roll(values, width - halves, 1), pltpu.roll(values, halves, 1)
    )


def head_cols(idx):
    return slice(idx * HEAD_SIZE, (idx + 1) * HEAD_SIZE)


def attention_probs(query, key, allowed):
    scores = jnp.where(allowed, times_t(query, key) * SCALING, MASKED_SCORE)
    powers = jnp.exp(scores - jnp.max(scores, axis=1, keepdims=True))
    return powers / jnp.sum(powers, axis=1, keepdims=True)


def allowed_pairs(length):
    later = lax.broadcasted_iota(jnp.int32, (LEN, LEN), 0)
    sooner = lax.broadcasted_iota(jnp.int32, (LEN, LEN), 1)
    return (sooner <= later) & (sooner < length)


def forward_kernel(
    len_ref, hidden_ref, qkv_ref, out_ref, gateup_ref, down_ref, gain_ref, cos_ref, sin_ref,
    output_ref, normed_ref, turned_ref, value_ref, attended_ref, middle_ref, normed_two_ref,
    gate_up_ref, acted_ref,
):
    hidden = hidden_ref[...]
    normed_ref[...] = (hidden * rms_scale(hidden) * gain_ref[0:1, :]).astype(BF16)
    qkv = jnp.dot(normed_ref[...], qkv_ref[...], preferred_element_type=F32)
    straight = qkv[:, :ROPED]
    turned_ref[...] = (straight * cos_ref[...] + swap_halves(straight) * sin_ref[...]).astype(BF16)
    value_ref[...] = qkv[:, ROPED:].astype(BF16)
    group = QUERY_HEADS // KEY_VALUE_HEADS
    for seq in range(hidden.shape[0] // LEN):
        rows = slice(seq * LEN, (seq + 1) * LEN)
        allowed = allowed_pairs(len_ref[seq])
        for head in range(QUERY_HEADS):
            key = turned_ref[rows, head_cols(QUERY_HEADS + head // group)]
            value = value_ref[rows, head_cols(head // group)]
            probs = attention_probs(turned_ref[rows, head_cols(head)], key, allowed)
            attended_ref[rows, head_cols(head)] = jnp.dot(
                probs.astype(BF16), value, preferred_element_type=F32
            ).astype(BF16)
    middle = hidden + jnp.dot(attended_ref[...], out_ref[...], preferred_element_type=F32)
    middle_ref[...] = middle
    normed_two_ref[...] = (middle * rms_scale(middle) * gain_ref[1:2, :]).astype(BF16)
    gate_up_ref[...] = jnp.dot(normed_two_ref[...], gateup_ref[...], preferred_element_type=F32)
    gate = gate_up_ref[:, :FEED_UNITS]
    acted_ref[...] = (gate / (1.0 + jnp.exp(-gate)) * gate_up_ref[:, FEED_UNITS:]).astype(BF16)
    output_ref[...] = middle + jnp.dot(acted_ref[...], down_ref[...], preferred_element_type=F32)


def backward_kernel(
    len_ref, grad_ref, hidden_ref, qkv_ref, out_ref, gateup_ref, down_ref, gain_ref, cos_ref,
    sin_ref, turned_ref, value_ref, middle_ref, gate_up_ref,
    grad_in_ref, low_ref, grad_gu_ref, grad_mid_ref, grad_qkv_ref, gains_out_ref,
    grad_att_ref, grad_turned_ref,
):
    grad = grad_ref[...]
    low_ref[...] = grad.astype(BF16)
    grad_act = times_t(low_ref[...], down_ref[...]).astype(BF16).astype(F32)
    gate, up = gate_up_ref[:, :FEED_UNITS], gate_up_ref[:, FEED_UNITS:]
    sigma = 1.0 / (1.0 + jnp.exp(-gate))
    grad_gu_ref[:, FEED_UNITS:] = (grad_act * (gate * sigma)).astype(BF16)
    grad_gu_ref[:, :FEED_UNITS] = (
        grad_act * up * (sigma * (1.0 + gate * (1.0 - sigma)))
    ).astype(BF16)
    middle = middle_ref[...]
    grad_mid, gain_two = rms_back(
        middle, rms_scale(middle), gain_ref[1:2, :], times_t(grad_gu_ref[...], gateup_ref[...])
    )
    grad_mid = grad_mid + grad
    grad_mid_ref[...] = grad_mid.astype(BF16)
    grad_att_ref[...] = times_t(grad_mid_ref[...], out_ref[...]).astype(BF16)
    group = QUERY_HEADS // KEY_VALUE_HEADS
    for seq in range(grad.shape[0] // LEN):
        rows = slice(seq * LEN, (seq + 1) * LEN)
        allowed = allowed_pairs(len_ref[seq])
        for kv in range(KEY_VALUE_HEADS):
            key = turned_ref[rows, head_cols(QUERY_HEADS + kv)]
            value = value_ref[rows, head_cols(kv)]
            grad_key = jnp.zeros((LEN, HEAD_SIZE), F32)
            grad_value = jnp.zeros((LEN, HEAD_SIZE), F32)
            for head in range(kv * group, (kv + 1) * group):
                query = turned_ref[rows, head_cols(head)]
                grad_out = grad_att_ref[rows, head_cols(head)]
                probs = attention_probs(query, key, allowed)
                grad_probs = times_t(grad_out, value)
                grad_value = grad_value + against(probs.astype(BF16), grad_out)
                inner = jnp.sum(grad_probs * probs, axis=1, keepdims=True)
                grad_scores = (probs * (grad_probs - inner)).astype(BF16)
                grad_query = jnp.dot(grad_scores, key, preferred_element_type=F32) * SCALING
                grad_turned_ref[rows, head_cols(head)] = grad_query.astype(BF16).astype(F32)
                grad_key = grad_key + against(grad_scores, query)
            grad_turned_ref[rows, head_cols(QUERY_HEADS + kv)] = (
                (grad_key * SCALING).astype(BF16).astype(F32)
            )
            at = slice(ROPED + kv * HEAD_SIZE, ROPED + (kv + 1) * HEAD_SIZE)
            grad_qkv_ref[rows, at] = grad_value.astype(BF16)
    turned = grad_turned_ref[...]
    grad_qkv_ref[:, :ROPED] = (
        turned * cos_ref[...] - swap_halves(turned) * sin_ref[...]
    ).astype(BF16)
    hidden = hidden_ref[...]
    grad_hidden, gain_one = rms_back(
        hidden, rms_scale(hidden), gain_ref[0:1, :], times_t(grad_qkv_ref[...], qkv_ref[...])
    )
    grad_in_ref[...] = grad_hidden + grad_mid
    gains_out_ref[...] = jnp.concatenate([gain_one[None], gain_two[None]], 0)


def layer_call(kernel, name, lens, operands, outs, scratch, flops):
    in_place = pl.BlockSpec(memory_space=pltpu.VMEM)
    return pl.pallas_call(
        kernel,
        in_specs=[pl.BlockSpec(memory_space=pltpu.SMEM)] + [in_place] * len(operands),
        out_specs=[in_place] * len(outs),
        out_shape=[jax.ShapeDtypeStruct(shape, dtype) for shape, dtype in outs],
        scratch_shapes=scratch,
        compiler_params=pltpu.CompilerParams(vmem_limit_bytes=VMEM_LIMIT),
        cost_estimate=pl.CostEstimate(flops=flops, bytes_accessed=8 * PL, transcendentals=0),
        name=name,
    )(lens, *operands)


def layer_forward(hidden, pieces, lens, rope):
    rows = hidden.shape[0]
    outs = [
        ((rows, MODEL_WIDTH), F32),
        ((rows, MODEL_WIDTH), BF16),
        ((rows, ROPED), BF16),
        ((rows, VALUE_WIDTH), BF16),
        ((rows, QUERY_WIDTH), BF16),
        ((rows, MODEL_WIDTH), F32),
        ((rows, MODEL_WIDTH), BF16),
        ((rows, 2 * FEED_UNITS), F32),
        ((rows, FEED_UNITS), BF16),
    ]
    output, *kept = layer_call(
        forward_kernel, "layer_forward", lens, [hidden, *pieces, *rope], outs, [], 2 * rows * PL
    )
    return output, (hidden, *kept)


def layer_backward(kept, pieces, lens, rope, grad_output):
    hidden, normed, turned, value, attended, middle, normed_two, gate_up, acted = kept
    rows = hidden.shape[0]
    outs = [
        ((rows, MODEL_WIDTH), F32),
        ((rows, MODEL_WIDTH), BF16),
        ((rows, 2 * FEED_UNITS), BF16),
        ((rows, MODEL_WIDTH), BF16),
        ((rows, QKV), BF16),
        ((2, MODEL_WIDTH), F32),
    ]
    scratch = [pltpu.VMEM((rows, QUERY_WIDTH), BF16), pltpu.VMEM((rows, ROPED), F32)]
    operands = [grad_output, hidden, *pieces, *rope, turned, value, middle, gate_up]
    grad_input, low, grad_gu, grad_mid, grad_qkv, gains = layer_call(
        backward_kernel, "layer_backward", lens, operands, outs, scratch, 2 * rows * PL
    )
    pairs = [(normed, grad_qkv), (attended, grad_mid), (normed_two, grad_gu), (acted, low)]
    return grad_input, pairs, gains.reshape(-1, 128)


def flat_rows(first, second):
    return jnp.concatenate([first, second]).reshape(-1, 128)


def token_bits(tokens):
    return tokens.bit_length() - 1


def for_chunks(keys_ref, lines_ref, span_ref, columns, run):
    bits = token_bits(keys_ref.shape[0])
    base = span_ref[2]
    places = lax.broadcasted_iota(jnp.int32, (LANES, LANES), 1)

    def chunk_step(chunk, _):
        line = lines_ref[pl.ds(chunk, 1), :]
        ids = jnp.transpose(jnp.broadcast_to(lax.shift_right_logical(line, bits), (LANES, LANES)))
        low = lax.shift_right_logical(keys_ref[chunk * LANES], bits) - base
        high = lax.shift_right_logical(keys_ref[chunk * LANES + LANES - 1], bits) - base
        first = jnp.maximum(low, 0) // COLUMNS
        last = jnp.minimum(high, columns - 1) // COLUMNS

        def hot(block):
            parts = []
            for k in range(COLUMNS // LANES):
                match = ids - (base + block * COLUMNS + k * LANES) == places
                parts.append(jnp.where(match, 1.0, 0.0).astype(BF16))
            return jnp.concatenate(parts, 1)

        run(chunk, first, last + 1, hot)
        return 0

    lax.fori_loop(span_ref[0] // LANES, (span_ref[1] + LANES - 1) // LANES, chunk_step, 0)


def row_of(keys_ref, at):
    return keys_ref[at] & (keys_ref.shape[0] - 1)


def embed_kernel(keys_ref, span_ref, lines_ref, table_ref, out_ref, low_ref, rows_ref, found_ref):
    features, columns = table_ref.shape
    blocks, _, width = out_ref.shape
    low_ref[:features, :] = table_ref[...].astype(BF16)
    low_ref[features:, :] = jnp.zeros((LANES - features, columns), BF16)
    for k in range(blocks):
        rows_ref[k * width : (k + 1) * width, :] = jnp.zeros((width, LANES), F32)

    def run(chunk, first, last, hot):
        def block_step(block, total):
            at = pl.multiple_of(block * COLUMNS, COLUMNS)
            return total + times_t(hot(block), low_ref[:, pl.ds(at, COLUMNS)])

        found_ref[...] = lax.fori_loop(first, last, block_step, jnp.zeros((LANES, LANES), F32))

        def move(k, _):
            for j in range(32):
                row = row_of(keys_ref, chunk * LANES + k * 32 + j)
                rows_ref[pl.ds(row, 1), :] = found_ref[pl.ds(k * 32 + j, 1), :]
            return 0

        lax.fori_loop(0, LANES // 32, move, 0)

    for_chunks(keys_ref, lines_ref, span_ref, columns, run)

    def finish(k, _):
        at = pl.multiple_of(k * width, width)
        out_ref[k] = jnp.transpose(rows_ref[pl.ds(at, width), :])[:features].astype(BF16)
        return 0

    lax.fori_loop(0, blocks, finish, 0)


def embed_rows(keys, span, table, blocks):
    tokens = keys.shape[0]
    features, columns = table.shape
    scalars = pl.BlockSpec(memory_space=pltpu.SMEM)
    in_place = pl.BlockSpec(memory_space=pltpu.VMEM)
    return pl.pallas_call(
        embed_kernel,
        in_specs=[scalars, scalars, in_place, in_place],
        out_specs=in_place,
        out_shape=jax.ShapeDtypeStruct((blocks, features, tokens // blocks), BF16),
        scratch_shapes=[
            pltpu.VMEM((LANES, columns), BF16),
            pltpu.VMEM((tokens, LANES), F32),
            pltpu.VMEM((LANES, LANES), F32),
        ],
        compiler_params=pltpu.CompilerParams(vmem_limit_bytes=VMEM_LIMIT),
        cost_estimate=pl.CostEstimate(
            flops=2 * tokens * LANES * COLUMNS, bytes_accessed=4 * table.size, transcendentals=0
        ),
        name="embed_rows",
    )(keys, span, keys.reshape(-1, LANES), table)


def spread_kernel(keys_ref, span_ref, place_ref, lines_ref, *refs):
    parts, (base_ref, out_ref, rows_ref, packed_ref) = refs[:-4], refs[-4:]
    features, columns = base_ref.shape
    count, _, width = parts[0].shape
    for k, part in enumerate(parts):
        def unfold(j, _):
            at = pl.multiple_of(place_ref[k * count + j] * width, width)
            flat = part[j].astype(F32)
            flat = jnp.concatenate([flat, jnp.zeros((LANES - features, width), F32)], 0)
            rows_ref[pl.ds(at, width), :] = jnp.transpose(flat)
            return 0

        lax.fori_loop(0, count, unfold, 0)
    out_ref[...] = base_ref[...]

    def run(chunk, first, last, hot):
        def move(k, _):
            for j in range(32):
                row = row_of(keys_ref, chunk * LANES + k * 32 + j)
                packed_ref[pl.ds(k * 32 + j, 1), :] = rows_ref[pl.ds(row, 1), :]
            return 0

        lax.fori_loop(0, LANES // 32, move, 0)
        packed = packed_ref[...].astype(BF16)

        def block_step(block, _):
            at = pl.multiple_of(block * COLUMNS, COLUMNS)
            out_ref[:, pl.ds(at, COLUMNS)] += against(packed, hot(block))[:features]
            return 0

        lax.fori_loop(first, last, block_step, 0)

    for_chunks(keys_ref, lines_ref, span_ref, columns, run)


def spread_rows(keys, span, places, parts, base):
    tokens = keys.shape[0]
    scalars = pl.BlockSpec(memory_space=pltpu.SMEM)
    in_place = pl.BlockSpec(memory_space=pltpu.VMEM)
    return pl.pallas_call(
        spread_kernel,
        in_specs=[scalars] * 3 + [in_place] * (2 + len(parts)),
        out_specs=in_place,
        out_shape=jax.ShapeDtypeStruct(base.shape, F32),
        scratch_shapes=[
            pltpu.VMEM((tokens, LANES), F32),
            pltpu.VMEM((LANES, LANES), F32),
        ],
        compiler_params=pltpu.CompilerParams(vmem_limit_bytes=VMEM_LIMIT),
        cost_estimate=pl.CostEstimate(
            flops=2 * tokens * LANES * COLUMNS, bytes_accessed=8 * base.size, transcendentals=0
        ),
        name="spread_rows",
    )(keys, span, places, keys.reshape(-1, LANES), *parts, base)


def second_kernel(rows_ref, weight_ref, gain_ref, both_ref, projected_ref):
    projected = jnp.dot(rows_ref[...], weight_ref[...], preferred_element_type=F32)
    projected_ref[...] = projected
    both_ref[0] = rows_ref[...]
    both_ref[1] = (projected * rms_scale(projected) * gain_ref[...]).astype(BF16)


def second_head(rows, weight, gain):
    count = rows.shape[0]
    return pl.pallas_call(
        second_kernel,
        grid=(count // BLOCK,),
        in_specs=[
            pl.BlockSpec((BLOCK, MODEL_WIDTH), lambda i: (i, 0)),
            pl.BlockSpec(weight.shape, lambda i: (0, 0)),
            pl.BlockSpec(gain.shape, lambda i: (0, 0)),
        ],
        out_specs=[
            pl.BlockSpec((2, BLOCK, MODEL_WIDTH), lambda i: (0, i, 0)),
            pl.BlockSpec((BLOCK, MODEL_WIDTH), lambda i: (i, 0)),
        ],
        out_shape=[
            jax.ShapeDtypeStruct((2, count, MODEL_WIDTH), BF16),
            jax.ShapeDtypeStruct((count, MODEL_WIDTH), F32),
        ],
        compiler_params=pltpu.CompilerParams(vmem_limit_bytes=VMEM_LIMIT),
        cost_estimate=pl.CostEstimate(
            flops=2 * count * weight.size, bytes_accessed=10 * rows.size, transcendentals=0
        ),
        name="second_head",
    )(rows, weight, gain)


def block_count(count_ref):
    per = BLOCK // GRANULE
    return (count_ref[0] + per - 1) // per


def block_at(i, count_ref, list_ref):
    return (jnp.minimum(i, jnp.maximum(block_count(count_ref) - 1, 0)), 0)


def head_kernel(
    count_ref, list_ref, rows_ref, table_ref,
    exp_ref, back_ref, sum_ref, peak_ref,
    packed, even, odd,
):
    columns = table_ref.shape[1]
    chunk = even.shape[1]
    chunks = columns // chunk
    logits = (even, odd)
    per = BLOCK // GRANULE
    block = pl.program_id(0)

    @pl.when(block == 0)
    def _():
        back_ref[...] = jnp.zeros(back_ref.shape, F32)
        sum_ref[...] = jnp.ones(sum_ref.shape, F32)
        peak_ref[...] = jnp.zeros(peak_ref.shape, F32)

    def spot(g):
        return pl.multiple_of(list_ref[block * per + g] * GRANULE, GRANULE)

    def dot_chunk(k):
        return jnp.dot(
            packed[...], table_ref[:, k * chunk : (k + 1) * chunk], preferred_element_type=F32
        )

    def put(stat_ref, line):
        for g in range(per):
            lane = g * GRANULE // 128 * 128
            part = line[:, lane : lane + 128]
            if g * GRANULE % 128:
                part = pltpu.roll(part, 128 - g * GRANULE % 128, 1)
            stat_ref[pl.ds(list_ref[block * per + g], 1), :] = part

    def run(peak):
        total = jnp.zeros((BLOCK, 128), F32)
        logits[0][...] = dot_chunk(0)
        for k in range(chunks):
            if k + 1 < chunks:
                logits[(k + 1) % 2][...] = dot_chunk(k + 1)
            here = logits[k % 2][...]
            powers = jnp.exp(here if peak is None else here - peak)
            for j in range(chunk // 128):
                total = total + powers[:, j * 128 : (j + 1) * 128]
            exp_ref[:, k * chunk : (k + 1) * chunk] = powers.astype(BF16)
        line = jnp.sum(jnp.transpose(total), axis=0, keepdims=True)
        put(sum_ref, line)
        back = times_t(exp_ref[...], table_ref[...])
        for g in range(per):
            back_ref[pl.ds(spot(g), GRANULE), :] = back[g * GRANULE : (g + 1) * GRANULE]
        return line

    @pl.when(block < block_count(count_ref))
    def _():
        for g in range(per):
            packed[g * GRANULE : (g + 1) * GRANULE, :] = rows_ref[pl.ds(spot(g), GRANULE), :]
        sums = run(None)
        fits = jnp.min(jnp.where((sums > 1e-20) & (sums < 1e30), 1.0, 0.0))

        @pl.when(fits < 0.5)
        def _():
            wide = jnp.full((BLOCK, 128), -jnp.inf, F32)
            for k in range(chunks):
                here = dot_chunk(k)
                for j in range(chunk // 128):
                    wide = jnp.maximum(wide, here[:, j * 128 : (j + 1) * 128])
            put(peak_ref, jnp.max(jnp.transpose(wide), axis=0, keepdims=True))
            run(jnp.max(wide, axis=1, keepdims=True))


def head_forward(count, order, rows, table):
    height, columns = rows.shape[0], table.shape[1]
    granules = height // GRANULE
    chunk = min(CHUNK // 2, columns // 2)
    whole = pl.Buffered(1)

    def once(i, count_ref, list_ref):
        return (0, 0)

    return pl.pallas_call(
        head_kernel,
        grid_spec=pltpu.PrefetchScalarGridSpec(
            num_scalar_prefetch=2,
            grid=(height // BLOCK,),
            in_specs=[
                pl.BlockSpec(rows.shape, once, pipeline_mode=whole),
                pl.BlockSpec(table.shape, once, pipeline_mode=whole),
            ],
            out_specs=[
                pl.BlockSpec((BLOCK, columns), block_at),
                pl.BlockSpec((height, MODEL_WIDTH), once, pipeline_mode=whole),
                pl.BlockSpec((granules, 128), once),
                pl.BlockSpec((granules, 128), once),
            ],
            scratch_shapes=[
                pltpu.VMEM((BLOCK, MODEL_WIDTH), BF16),
                pltpu.VMEM((BLOCK, chunk), F32),
                pltpu.VMEM((BLOCK, chunk), F32),
            ],
        ),
        out_shape=[
            jax.ShapeDtypeStruct((height, columns), BF16),
            jax.ShapeDtypeStruct((height, MODEL_WIDTH), F32),
            jax.ShapeDtypeStruct((granules, 128), F32),
            jax.ShapeDtypeStruct((granules, 128), F32),
        ],
        compiler_params=pltpu.CompilerParams(vmem_limit_bytes=VMEM_LIMIT),
        cost_estimate=pl.CostEstimate(
            flops=4 * height * table.size,
            bytes_accessed=2 * height * columns,
            transcendentals=height * columns,
        ),
        name="head_forward",
    )(count, order, rows, table)


def scale_kernel(
    count_ref, list_ref, rows_ref, back_ref, scale_ref, grad_ref, turned_ref, scaled, packed
):
    per = STEP // GRANULE
    step, blocks = pl.program_id(0), pl.num_programs(0) // 2

    @pl.when(step < blocks)
    def _():
        for k in range(STEP // LANES):
            at = slice(k * LANES, (k + 1) * LANES)
            line = scale_ref[pl.ds(step * (STEP // LANES) + k, 1), :]
            column = jnp.transpose(jnp.broadcast_to(line, (LANES, LANES)))[:, :1]
            grad_ref[at, :] = back_ref[at, :] * column
            row = pl.multiple_of(step * STEP + k * LANES, LANES)
            scaled[pl.ds(row, LANES), :] = (rows_ref[at, :].astype(F32) * column).astype(BF16)

    block = step - blocks

    @pl.when((block >= 0) & (block * per < count_ref[0]))
    def _():
        for g in range(per):
            at = block * per + g
            spot = pl.multiple_of(list_ref[at] * GRANULE, GRANULE)
            part = scaled[pl.ds(spot, GRANULE), :].astype(F32)
            packed[g * GRANULE : (g + 1) * GRANULE, :] = jnp.where(
                at < count_ref[0], part, jnp.zeros_like(part)
            )
        turned_ref[...] = jnp.transpose(packed[...]).astype(BF16)


def scale_rows(count, order, rows, back, scale):
    height = rows.shape[0]
    blocks = height // STEP

    def first(i, count_ref, list_ref):
        return (jnp.minimum(i, blocks - 1), 0)

    def second(i, count_ref, list_ref):
        used = (count_ref[0] + STEP // GRANULE - 1) // (STEP // GRANULE)
        return (0, jnp.minimum(jnp.maximum(i - blocks, 0), jnp.maximum(used - 1, 0)))

    return pl.pallas_call(
        scale_kernel,
        grid_spec=pltpu.PrefetchScalarGridSpec(
            num_scalar_prefetch=2,
            grid=(2 * blocks,),
            in_specs=[
                pl.BlockSpec((STEP, MODEL_WIDTH), first),
                pl.BlockSpec((STEP, MODEL_WIDTH), first),
                pl.BlockSpec(scale.shape, lambda i, count_ref, list_ref: (0, 0)),
            ],
            out_specs=[
                pl.BlockSpec((STEP, MODEL_WIDTH), first),
                pl.BlockSpec((MODEL_WIDTH, STEP), second),
            ],
            scratch_shapes=[
                pltpu.VMEM((height, MODEL_WIDTH), BF16),
                pltpu.VMEM((STEP, MODEL_WIDTH), F32),
            ],
        ),
        out_shape=[
            jax.ShapeDtypeStruct((height, MODEL_WIDTH), F32),
            jax.ShapeDtypeStruct((MODEL_WIDTH, height), BF16),
        ],
        compiler_params=pltpu.CompilerParams(vmem_limit_bytes=VMEM_LIMIT),
        cost_estimate=pl.CostEstimate(flops=0, bytes_accessed=12 * rows.size, transcendentals=0),
        name="scale_rows",
    )(count, order, rows, back, scale)


def table_kernel(count_ref, turned_ref, exp_ref, out_ref, total):
    used = block_count(count_ref)
    most = exp_ref.shape[0] // BLOCK
    straight = most * 5 // 8

    @pl.when(used < straight)
    def _():
        total[...] = jnp.zeros(total.shape, F32)

        def step(k, _):
            at = pl.multiple_of(k * BLOCK, BLOCK)
            total[...] += jnp.dot(
                turned_ref[:, pl.ds(at, BLOCK)],
                exp_ref[pl.ds(at, BLOCK), :],
                preferred_element_type=F32,
            )
            return 0

        lax.fori_loop(0, used, step, 0)
        out_ref[...] = total[...].astype(BF16)

    for blocks in range(straight, most + 1):

        @pl.when(used == blocks)
        def _():
            out_ref[...] = jnp.dot(
                turned_ref[:, : blocks * BLOCK],
                exp_ref[: blocks * BLOCK, :],
                preferred_element_type=F32,
            ).astype(BF16)


def table_backward(count, turned, powers, part, parts):
    height, columns = powers.shape[0], powers.shape[1] // parts
    chunk = 512 if columns % 512 == 0 else 256
    steps = columns // chunk
    return pl.pallas_call(
        table_kernel,
        grid_spec=pltpu.PrefetchScalarGridSpec(
            num_scalar_prefetch=1,
            grid=(steps,),
            in_specs=[
                pl.BlockSpec(
                    turned.shape, lambda i, count_ref: (0, 0), pipeline_mode=pl.Buffered(1)
                ),
                pl.BlockSpec((height, chunk), lambda i, count_ref: (0, part * steps + i)),
            ],
            out_specs=pl.BlockSpec((MODEL_WIDTH, chunk), lambda i, count_ref: (0, i)),
            scratch_shapes=[pltpu.VMEM((MODEL_WIDTH, chunk), F32)],
        ),
        out_shape=jax.ShapeDtypeStruct((MODEL_WIDTH, columns), BF16),
        compiler_params=pltpu.CompilerParams(vmem_limit_bytes=VMEM_LIMIT),
        cost_estimate=pl.CostEstimate(
            flops=2 * MODEL_WIDTH * powers.size // parts,
            bytes_accessed=2 * powers.size // parts,
            transcendentals=0,
        ),
        name="table_backward",
    )(count, turned, powers)


def shards(
    token_ids,
    lengths,
    deal_order,
    embed_table,
    table_mom,
    table_avg,
    model_flat,
    model_mom,
    model_avg,
):
    dp_size, shard_size = lax.axis_size("dp"), lax.axis_size("shard")
    shard_idx, dp_idx = lax.axis_index("shard"), lax.axis_index("dp")
    device_idx = lax.axis_index(("dp", "shard"))
    core = dp_bit(1)
    seqs = token_ids.shape[0]
    own_rows = seqs * LEN
    group = 2 * shard_size
    groups = dp_size // 2
    slots = group * seqs
    seq_total = groups * slots
    target_count = jnp.float32((MEAN_LENGTH - 1) * seq_total)
    features, columns = embed_table.shape
    half = columns // 2
    vocab_start = shard_idx * columns + core * half
    length = model_flat.shape[0]

    tiny = jnp.concatenate([token_ids, jnp.broadcast_to(lengths[:, None], (seqs, LEN))], 0)
    tiny = tiny.reshape((1,) * (len(bits_below(dp_size)) + len(bits_below(shard_size))) + tiny.shape)
    for k, bit in enumerate(bits_below(dp_size)[::-1]):
        tiny = join(tiny, flip_dp(tiny, bit), bit, k)
    for k, bit in enumerate(bits_below(shard_size)[::-1]):
        other = flip_shard(tiny, bit)
        axis = len(bits_below(dp_size)) + k
        tiny = jnp.where(
            (shard_idx // bit) % 2 == 0,
            jnp.concatenate([tiny, other], axis),
            jnp.concatenate([other, tiny], axis),
        )
    tiny = tiny.reshape(dp_size * shard_size, 2 * seqs, LEN)
    all_ids = tiny[:, :seqs].reshape(seq_total, LEN)
    all_lens = tiny[:, seqs:, 0].reshape(seq_total)
    here = jnp.arange(seq_total)
    longer = all_lens[None, :] > all_lens[:, None]
    equal = (all_lens[None, :] == all_lens[:, None]) & (here[None, :] < here[:, None])
    rank = jnp.sum((longer | equal).astype(jnp.int32), axis=1)
    turn, seat = rank // groups, rank % groups
    group_of = jnp.where(turn % 2 == 0, seat, groups - 1 - seat)
    place_of = group_of * slots + turn
    hits = (place_of[None, :] == here[:, None]).astype(jnp.int32)
    seq_at = jnp.sum(hits * here[None, :], axis=1)
    dealt_ids = all_ids[seq_at]
    dealt_lens = jnp.sum(hits * all_lens[None, :], axis=1)
    my_group = dp_idx // 2
    group_ids = lax.dynamic_slice_in_dim(dealt_ids, my_group * slots, slots, 0)
    group_lens = lax.dynamic_slice_in_dim(dealt_lens, my_group * slots, slots, 0)
    own_at = core * shard_size + shard_idx
    own_lens = lax.dynamic_slice_in_dim(group_lens, own_at * seqs, seqs, 0)
    own_seqs = lax.dynamic_slice_in_dim(seq_at, (my_group * group + own_at) * seqs, seqs, 0)

    places = jnp.arange(LEN)
    weight_one = (places[None, :] + 1 < group_lens[:, None]).astype(F32)
    weight_two = SECOND_WEIGHT * (places[None, :] + 2 < group_lens[:, None]).astype(F32)
    weights = jnp.stack([weight_one, weight_two]) / target_count

    per_seq = LEN // GRANULE
    starts = jnp.arange(per_seq) * GRANULE
    useful = jnp.stack([starts[None, :] + k + 1 < group_lens[:, None] for k in range(2)])
    useful = useful.reshape(-1)
    index = jnp.arange(useful.shape[0])
    before = jnp.sum((useful[None, :] & (index[None, :] < index[:, None])).astype(jnp.int32), axis=1)
    count = jnp.sum(useful.astype(jnp.int32))
    last = jnp.max(jnp.where(useful, index, 0))
    found = useful[None, :] & (before[None, :] == index[:, None])
    order = jnp.sum(jnp.where(found, index[None, :], 0), axis=1)
    order = jnp.where(index < count, order, last).astype(jnp.int32)
    count = count.reshape(1)

    everything = lax.all_gather(own_blocks(model_flat), ("dp", "shard"))

    tokens = seq_total * LEN
    bits = token_bits(tokens)
    kept_ids = jnp.where(places[None, :] < dealt_lens[:, None], dealt_ids, columns * shard_size)
    keys = jnp.sort(kept_ids.reshape(-1) * tokens + jnp.arange(tokens, dtype=jnp.int32))
    first_id = shard_idx * columns
    span = jnp.stack(
        [
            jnp.sum((keys < first_id * tokens).astype(jnp.int32)),
            jnp.sum(((keys >> bits) < first_id + columns).astype(jnp.int32)),
            first_id,
        ]
    ).astype(jnp.int32)
    devices = dp_size * shard_size
    picked = embed_rows(keys, span, embed_table, devices)
    picked = picked.reshape(dp_size, shard_size, features, own_rows)
    mine = ring_reduce(picked.transpose(1, 0, 2, 3)).astype(BF16)
    parts = [pick(mine, dp_idx, 0)]
    parts += [flip_dp(pick(mine, dp_idx ^ k, 0), k) for k in range(1, dp_size)]
    embedded = jnp.stack(parts)[jnp.arange(dp_size) ^ dp_idx]
    embedded = embedded.reshape(MODEL_WIDTH, own_rows).T.astype(F32)

    held_table, everything, embedded = lax.optimization_barrier(
        (embed_table, everything, embedded)
    )
    table_gather = TableGather(held_table)
    middle_rows = PL // 128
    low_rows = middle_rows // 16 * 16
    total_devices = dp_size * shard_size
    per = GRAIN // 128
    end_row = block_starts(length, total_devices)[-1] * per
    tail = 2 * MODEL_WIDTH // 128
    square = MODEL_WIDTH * MODEL_WIDTH // 128
    *layer_zero, gains_zero = unpack_rows(
        everything, length, 0, low_rows + 16, LAYER_SHAPES, {}, 0, ((middle_rows - tail, 16),)
    )
    gain_row = middle_rows - low_rows + middle_rows - tail
    second_row = gain_row + tail + square
    base_one = gain_row // 16 * 16
    base_two = second_row // 16 * 16 - 16
    *layer_one, w_second, gains_one, gains_head = unpack_rows(
        everything, length, low_rows, end_row, LAYER_SHAPES + SQUARE, {3: tail},
        middle_rows - low_rows, ((base_one, 32), (base_two, 32)),
    )

    def gain_pair(rows, at):
        return rows[at : at + tail].reshape(2, MODEL_WIDTH)

    layer_zero.append(gain_pair(gains_zero, 0).astype(F32))
    layer_one.append(gain_pair(gains_one, gain_row - base_one).astype(F32))
    head_gains = gain_pair(gains_head, second_row - base_two).astype(F32)

    rope = rope_rows(own_rows)
    first_hidden = table_gather.tied(embedded)
    table_gather.step()
    hidden, kept_zero = layer_forward(first_hidden, layer_zero, own_lens, rope)
    hidden, kept_one = layer_forward(hidden, layer_one, own_lens, rope)
    scale_final = rms_scale(hidden)
    head_one = (hidden * scale_final * head_gains[0]).astype(BF16)
    all_one = group_gather(head_one, table_gather.tied).reshape(-1, MODEL_WIDTH)
    table_low = table_gather.finish()
    both, projected = second_head(all_one, w_second, head_gains[1:2])
    all_two = both[1]
    both = both.reshape(-1, MODEL_WIDTH)
    scale_second = rms_scale(projected)
    group_rows = all_one.shape[0]

    powers, back, sums, peaks = head_forward(count, order, both, table_low)
    sums = sums[:, :GRANULE].reshape(-1, 128)
    peaks = peaks[:, :GRANULE].reshape(-1, 128)
    sum_all_rows, peak_all = sums, peaks
    for flip, bits in ((flip_shard, bits_below(shard_size)), (flip_dp, [1])):
        for bit in bits:
            stats = flip(jnp.stack([sum_all_rows, peak_all]), bit)
            top = jnp.maximum(peak_all, stats[1])
            sum_all_rows = sum_all_rows * jnp.exp(peak_all - top) + stats[0] * jnp.exp(
                stats[1] - top
            )
            peak_all = top
    log_total = (peak_all + jnp.log(sum_all_rows)).reshape(2, group, seqs, LEN)
    row_scale = weights.reshape(-1, 128) * jnp.exp(peaks - peak_all) / sum_all_rows
    grad_rows, turned_rows = scale_rows(count, order, both, back, row_scale)

    own_log = pick(log_total, own_at, 1)
    own_weights = pick(weights.reshape(2, group, seqs, LEN), own_at, 1)
    words = embedded.reshape(seqs, LEN, MODEL_WIDTH)
    next_one = jnp.roll(words, -1, 1).reshape(own_rows, MODEL_WIDTH)
    next_two = jnp.roll(words, -2, 1).reshape(own_rows, MODEL_WIDTH)
    head_two = lax.dynamic_slice_in_dim(all_two, own_at * own_rows, own_rows, 0)
    chosen_one = jnp.sum(head_one.astype(F32) * next_one, axis=-1)
    chosen_two = jnp.sum(head_two.astype(F32) * next_two, axis=-1)
    chosen = jnp.stack([chosen_one, chosen_two]).reshape(2, seqs, LEN)
    own_loss = jnp.sum(own_weights * (own_log - chosen), axis=(0, 2))

    weight_col = own_weights.reshape(2, own_rows, 1)
    part_two = grad_rows[group_rows:]
    own_two = lax.dynamic_slice_in_dim(part_two, own_at * own_rows, own_rows, 0)
    part_two = lax.dynamic_update_slice_in_dim(
        part_two, own_two - weight_col[1] * next_two, own_at * own_rows, 0
    )
    grad_proj, grad_gain_second = rms_back(projected, scale_second, head_gains[1], part_two)
    grad_proj_low = grad_proj.astype(BF16)
    part_one = grad_rows[:group_rows] + times_t(grad_proj_low, w_second)
    quarters = 4
    cubes = [None] * quarters
    running = [turned_rows]

    def quarter_hook(k):
        def hook(got):
            part = table_backward(count, running[0], powers, k, quarters)
            got, part, running[0] = lax.optimization_barrier((got, part, running[0]))
            bits = high_bits() if k < quarters // 2 else high_bits()[::-1]
            cubes[k] = Cube(part.reshape(-1, 2 * features, part.shape[1]), bits)
            return got

        return hook

    grad_final = group_reduce(
        part_one.reshape(2, shard_size, own_rows, MODEL_WIDTH),
        [quarter_hook(k) for k in (0, 2, 1, 3)],
    )
    grad_final = grad_final - weight_col[0] * next_one
    grad_hidden, grad_gain_final = rms_back(hidden, scale_final, head_gains[0], grad_final)

    sub_rows = owner_sub_rows(length)
    height_zero = length * (total_devices // 2 - 1) // GRAIN * per + 2 * sub_rows
    height_one = length * (total_devices - 1) // GRAIN * per + 2 * sub_rows - low_rows
    keep = height_zero - low_rows
    grad_hidden = tie(grad_hidden, [cubes[0], cubes[2]])
    cubes[0].step(), cubes[2].step()
    grad_hidden, pairs, gain_grads = layer_backward(
        kept_one, layer_one, own_lens, rope, grad_hidden
    )
    gain_grads = tie(gain_grads, [cubes[1], cubes[3]])
    cubes[1].step(), cubes[3].step()
    own_one, send_one, kept_rows = pack_half(
        owner_rows(length, 1, low_rows),
        pairs + [(all_one, grad_proj_low)],
        [gain_grads, flat_rows(grad_gain_final, grad_gain_second)],
        None, middle_rows - low_rows, {3: tail, 4: tail}, height_one, sub_rows, keep, 0,
    )
    got_one = flip_dp(send_one, 1)
    grad_hidden, own_one, got_one = lax.optimization_barrier((grad_hidden, own_one, got_one))
    cubes_one = half_cubes(own_one, got_one)
    grad_hidden, pairs, gain_grads = layer_backward(
        kept_zero, layer_zero, own_lens, rope, grad_hidden
    )
    gain_grads = tie(gain_grads, cubes)
    joined = jnp.concatenate([cube.finish() for cube in cubes], 1)
    flipped = owner_flip(joined, features)
    own_zero, send_zero = pack_half(
        owner_rows(length, 0, 0), pairs, [gain_grads],
        (kept_rows, height_zero - middle_rows), 0, {3: tail}, height_zero, sub_rows, 0,
        middle_rows - low_rows,
    )
    one_terms = (weight_col[0] * head_one.astype(F32)).reshape(seqs, LEN, MODEL_WIDTH)
    two_terms = (weight_col[1] * head_two.astype(F32)).reshape(seqs, LEN, MODEL_WIDTH)
    token_grad = (
        grad_hidden.astype(BF16).astype(F32)
        - jnp.roll(one_terms, 1, 1).reshape(own_rows, MODEL_WIDTH)
        - jnp.roll(two_terms, 2, 1).reshape(own_rows, MODEL_WIDTH)
    ).astype(BF16)
    token_parts = token_grad.T.reshape(dp_size, features, own_rows)
    parts = [pick(token_parts, dp_idx, 0)]
    parts += [flip_dp(pick(token_parts, dp_idx ^ k, 0), k) for k in range(1, dp_size)]
    own_zero = tie(own_zero, cubes_one)
    for cube in cubes_one:
        cube.step()
    got_zero, parts, flipped = lax.optimization_barrier((flip_dp(send_zero, 1), parts, flipped))
    table_part = owner_join(joined, flipped, features)
    cubes_zero = half_cubes(own_zero, got_zero)
    chain = [jnp.stack(parts)]
    for k in range(shard_size - 1):
        chain.append(next_shard(chain[-1]))
        if k == 0:
            chain[-1] = tie(chain[-1], cubes_one)
            sums_one = jnp.concatenate([cube.finish() for cube in cubes_one], 0)
    chain[-1] = tie(chain[-1], cubes_zero)
    for cube in cubes_zero:
        cube.step()
    from_dp = (jnp.arange(dp_size) ^ dp_idx)[None, :]
    from_shard = (shard_idx - jnp.arange(shard_size))[:, None] % shard_size
    spots = (from_dp * shard_size + from_shard).reshape(-1).astype(jnp.int32)
    table_sum = spread_rows(keys, span, spots, chain, table_part)
    table_sum = tie(table_sum, cubes_zero)
    sums_zero = jnp.concatenate([cube.finish() for cube in cubes_zero], 0)
    model_sum = own_part(sums_zero, sums_one, length)

    square_sum = jnp.sum(table_sum * table_sum) + jnp.sum(model_sum * model_sum)
    losses = jnp.sum(
        jnp.where(own_seqs[:, None] == here[None, :], own_loss[:, None], 0.0), axis=0
    )
    totals = sum_all(jnp.concatenate([losses, square_sum.reshape(1)])[None])[0]
    grad_norm = jnp.sqrt(totals[seq_total])
    factor = jnp.minimum(1.0, CLIP_NORM / (grad_norm + 1e-06))
    all_loss = totals[:seq_total]
    loss_total = jnp.sum(all_loss)
    seq_loss = lax.dynamic_slice_in_dim(all_loss, device_idx * seqs, seqs, 0)
    own_slots = lax.dynamic_slice_in_dim(deal_order, device_idx * seqs, seqs, 0)
    slot_loss = all_loss[own_slots]

    results = []
    for weights_in, gradient, moment, average in (
        (embed_table, table_sum, table_mom, table_avg),
        (model_flat, model_sum, model_mom, model_avg),
    ):
        clipped = gradient * factor
        new_moment = MOMENTUM * moment + clipped
        new_weight = weights_in - LEARN_RATE * (clipped + MOMENTUM * new_moment)
        new_average = AVERAGE_KEEP * average + (1.0 - AVERAGE_KEEP) * new_weight
        results.append(
            (clipped, new_weight, new_moment, new_average, new_weight.astype(BF16))
        )
    return (loss_total, seq_loss, slot_loss, grad_norm) + results[0] + results[1]


def solution(mesh):
    both = P(("dp", "shard"))
    block = P("dp", "shard")
    return jax.shard_map(
        shards,
        mesh=mesh,
        in_specs=(P(("dp", "shard"), None), both, P(), block, block, block, both, both, both),
        out_specs=(P(), both, both, P()) + (block,) * 5 + (both,) * 5,
        check_vma=False,
    )
```
